32 devices in a mesh: gz: 8 (over z, y), gy: 4 (over x, core).
Axes of the slice: x: 2, y: 2, z: 4, core: 2. Of those that a mesh axis runs over, the one named last changes fastest.
Arguments:
- fraction: float32 [64, 128, 512], P('gz', 'gy'), may hold values from 0 to 1
- source: float32 [64, 128, 512], P('gz', 'gy'), may hold values from -40 to 40, as said below
- bubble_label: int32 [64, 128, 512], P('gz', 'gy'), may hold values from -1 to 511, as said below
- subdomain: int32 [64, 128, 512], P('gz', 'gy'), may hold values from 0 to 127, as said below
- coarse_inverse: float32 [640, 640], P(('gz', 'gy')), may hold values from -0.2 to 0.2, as said below
Outputs:
- iterate: float32 [64, 128, 512], P('gz', 'gy')
- residual: float32 [64, 128, 512], P('gz', 'gy')
The draws below stay inside these ranges and needn't reach their ends.
Inputs may be any that keep to these rules, and one draw needn't show every extreme that they name: `source`: vertical factor 1 + 2 z / 64, so magnitudes grow with depth. `bubble_label`: A cell at plane z and row y carries -1 or the number of a bubble of slab block a and row block y // 32 with |a - z // 8| <= 1; the bubbles of slab block a and row block b are numbered (a 4 + b) * 16 + i with i < 16. Rows y with y % 32 == 0 carry -1. `subdomain`: cells of slab block a and row block b carry (a 4 + b) * 4 + i with i < 4; the number does not change along z and y inside a block and never falls along x. `coarse_inverse`: symmetric positive definite.
All inputs are finite; a program needn't handle non-finite values.
Results may differ from the reference program's by a relative error of at most 0.0003.
Values sent between devices are 32-bit elements; how exact they have to be, the bound alone decides.
No kernel may reach another device: no remote copies, remote signals or barrier semaphores. Data moves between devices by JAX's collectives and lax.ppermute only.
A program may use at most 64 MiB of HBM per device.

```python
from functools import reduce
import jax
import jax.numpy as jnp
from jax import lax

NX = 512
CZ = 8
CY = 32
S_DEV = 4
B_DEV = 16
ITERS = 3
NZ = 64
NY = 128
COARSE = 640


def draw_source(key, part):
    noise = jnp.clip(jax.random.normal(key, (NZ, NY, NX), jnp.float32), -4.0, 4.0)
    depth = 1.0 + 2.0 * jnp.arange(NZ, dtype=jnp.float32)[:, None, None] / NZ
    return jnp.clip(3.0 * depth * noise, -40.0, 40.0)


def draw_bubble_label(key, part):
    slabs = NZ // CZ
    columns = NY // CY
    keys = jax.random.split(jax.random.fold_in(key, 11), 6)
    shape = (slabs, columns, B_DEV)
    radius_z = jax.random.randint(keys[0], shape, 1, CZ // 2 + 1)
    radius_y = jax.random.randint(keys[1], shape, 1, CY // 4 + 1)
    radius_x = jax.random.randint(keys[2], shape, 1, NX // 8 + 1)
    centre_z = jax.random.randint(keys[3], shape, 0, CZ)
    centre_y = radius_y + 1 + jax.random.randint(keys[4], shape, 0, CY - 2 * radius_y - 1)
    centre_x = jax.random.randint(keys[5], shape, 0, NX)
    local_z = jnp.arange(CZ, dtype=jnp.int32)[None, :, None, None]
    local_y = jnp.arange(CY, dtype=jnp.int32)[None, None, :, None]
    local_x = jnp.arange(NX, dtype=jnp.int32)[None, None, None, :]
    numbers = jnp.arange(B_DEV, dtype=jnp.int32)

    def block(index):
        slab = index // columns
        column = index % columns
        best = jnp.full((CZ, CY, NX), -1, jnp.int32)
        for offset in (-1, 0, 1):
            source_slab = jnp.clip(slab + offset, 0, slabs - 1)
            live = (slab + offset >= 0) & (slab + offset < slabs)
            middle_z = (source_slab * CZ + centre_z[source_slab, column] - slab * CZ)[:, None, None, None]
            inside = jnp.abs(local_z - middle_z) <= radius_z[source_slab, column][:, None, None, None]
            inside = inside & (jnp.abs(local_y - centre_y[source_slab, column][:, None, None, None]) <= radius_y[source_slab, column][:, None, None, None])
            inside = inside & (jnp.abs(local_x - centre_x[source_slab, column][:, None, None, None]) <= radius_x[source_slab, column][:, None, None, None])
            inside = inside & live
            ident = ((source_slab * columns + column) * B_DEV + numbers)[:, None, None, None]
            best = jnp.maximum(best, jnp.max(jnp.where(inside, ident, -1), axis=0))
        return best
    blocks = lax.map(block, jnp.arange(slabs * columns, dtype=jnp.int32))
    return blocks.reshape(slabs, columns, CZ, CY, NX).transpose(0, 2, 1, 3, 4).reshape(NZ, NY, NX).astype(jnp.int32)


def draw_subdomain(key, part):
    slabs = NZ // CZ
    columns = NY // CY
    cuts = jax.random.randint(jax.random.fold_in(key, 13), (slabs, columns, S_DEV - 1), 1, NX)
    across = jnp.arange(NX, dtype=jnp.int32)
    local = jnp.sum((across[None, None, :, None] >= cuts[:, :, None, :]).astype(jnp.int32), axis=-1)
    owner = jnp.arange(slabs, dtype=jnp.int32)[:, None, None] * columns + jnp.arange(columns, dtype=jnp.int32)[None, :, None]
    ident = owner * S_DEV + local
    full = jnp.broadcast_to(ident[:, None, :, None, :], (slabs, CZ, columns, CY, NX))
    return full.reshape(NZ, NY, NX).astype(jnp.int32)


def draw_coarse_inverse(key, part):
    first, second = jax.random.split(jax.random.fold_in(key, 17))
    span = S_DEV + B_DEV
    slot = jnp.arange(COARSE, dtype=jnp.int32) % span
    base = jnp.where(slot < S_DEV, 0.3 / jnp.sqrt(jnp.float32(CZ * CY * NX / S_DEV)), 0.3 / 8.0)
    spread = jnp.exp(jax.random.uniform(first, (COARSE,), jnp.float32, jnp.log(0.5), jnp.log(2.0)))
    scale = jnp.sqrt(base * spread)
    noise = jax.random.normal(second, (COARSE, COARSE), jnp.float32) * (0.35 / jnp.sqrt(2.0 * COARSE))
    rows = jnp.arange(COARSE, dtype=jnp.int32)
    same = rows[:, None] == rows[None, :]
    middle = jnp.where(same, 1.0, noise + noise.T)
    return (scale[:, None] * middle * scale[None, :]).astype(jnp.float32)


def block_scale(key, extent, pieces, smallest, largest):
    gain = 1.0
    for dim, shards_of in pieces:
        draws = jax.random.uniform(jax.random.fold_in(jax.random.fold_in(key, 6), dim), (shards_of,), jnp.float32, smallest / len(pieces), largest / len(pieces))
        gain = gain * jnp.repeat(jnp.exp(draws), extent[dim] // shards_of).reshape((-1,) + (1,) * (len(extent) - 1 - dim))
    return gain


def setup_inputs(seed: int = 0) -> dict:
    key_of = jax.random.split(jax.random.key(seed), 6)
    return {
        "fraction": jnp.clip(1.0 * jax.random.uniform(key_of[0], (NZ, NY, NX), jnp.float32) ** block_scale(key_of[0], (NZ, NY, NX), ((0, 8), (1, 4)), -0.2, 0.2), 0.0, 1.0),
        "source": draw_source(jax.random.fold_in(key_of[5], 71), 0),
        "bubble_label": draw_bubble_label(jax.random.fold_in(key_of[5], 71), 0),
        "subdomain": draw_subdomain(jax.random.fold_in(key_of[5], 71), 0),
        "coarse_inverse": draw_coarse_inverse(jax.random.fold_in(key_of[5], 71), 0),
    }


surface_tension = 0.5
shift_term = 0.05
gas_drop = 0.75
norm_floor = 0.25

def add_all(items):
    return reduce(lambda first, second: first + second, items)

def six_neighbours(padded):
    return [padded[2:, 1:-1, 1:-1], padded[:-2, 1:-1, 1:-1], padded[1:-1, 2:, 1:-1], padded[1:-1, :-2, 1:-1], padded[1:-1, 1:-1, 2:], padded[1:-1, 1:-1, :-2]]

def normals(padded):
    along = [0.5 * (padded[2:, 1:-1, 1:-1] - padded[:-2, 1:-1, 1:-1]), 0.5 * (padded[1:-1, 2:, 1:-1] - padded[1:-1, :-2, 1:-1]), 0.5 * (padded[1:-1, 1:-1, 2:] - padded[1:-1, 1:-1, :-2])]
    length = jnp.maximum(jnp.sqrt(along[0] * along[0] + along[1] * along[1] + along[2] * along[2]), norm_floor)
    return jnp.stack([member / length for member in along])

def curvature(padded):
    return -(0.5 * (padded[0, 2:, 1:-1, 1:-1] - padded[0, :-2, 1:-1, 1:-1]) + 0.5 * (padded[1, 1:-1, 2:, 1:-1] - padded[1, 1:-1, :-2, 1:-1]) + 0.5 * (padded[2, 1:-1, 1:-1, 2:] - padded[2, 1:-1, 1:-1, :-2]))

def assemble(frac_padded, kappa_padded, source):
    density = 1.0 - gas_drop * frac_padded
    centre = density[1:-1, 1:-1, 1:-1]
    coefs = [2.0 / (centre + other) for other in six_neighbours(density)]
    fraction = frac_padded[1:-1, 1:-1, 1:-1]
    kappa = kappa_padded[1:-1, 1:-1, 1:-1]
    terms = [coef * (0.5 * (kappa + kappa_other)) * (frac_other - fraction) for coef, frac_other, kappa_other in zip(coefs, six_neighbours(frac_padded), six_neighbours(kappa_padded))]
    rhs = source - surface_tension * add_all(terms)
    diagonal = shift_term + add_all(coefs)
    return (coefs, diagonal, rhs)

def operate_padded(padded, coefs, diagonal):
    return diagonal * padded[1:-1, 1:-1, 1:-1] - add_all([coef * other for coef, other in zip(coefs, six_neighbours(padded))])

def factor_planes(diagonal_planes, down_planes):
    inverse = [1.0 / diagonal_planes[0]]
    mults = [None]
    for level in range(1, len(diagonal_planes)):
        mult = down_planes[level] * inverse[level - 1]
        inverse.append(1.0 / (diagonal_planes[level] - mult * down_planes[level]))
        mults.append(mult)
    return (inverse, mults)

def solve_planes(values, inverse, mults, up_planes):
    count = len(values)
    forward = [values[0]]
    for level in range(1, count):
        forward.append(values[level] + mults[level] * forward[level - 1])
    result = [forward[count - 1] * inverse[count - 1]]
    for level in range(count - 2, -1, -1):
        result.insert(0, (forward[level] + up_planes[level] * result[0]) * inverse[level])
    return result

def reference(fraction, source, bubble_label, subdomain, coarse_inverse):
    frac_padded = jnp.pad(fraction, 1)
    normal = normals(frac_padded)
    kappa = curvature(jnp.pad(normal, ((0, 0), (1, 1), (1, 1), (1, 1))))
    kappa_padded = jnp.pad(kappa, 1)
    coefs, diagonal, rhs = assemble(frac_padded, kappa_padded, source)
    blocks = NZ // CZ

    def planes_of(field):
        shaped = field.reshape(blocks, CZ, NY, NX)
        return [shaped[:, level] for level in range(CZ)]

    def join(planes):
        return jnp.stack(planes, axis=1).reshape(NZ, NY, NX)
    inverse, mults = factor_planes(planes_of(diagonal), planes_of(coefs[1]))
    up_planes = planes_of(coefs[0])
    span = S_DEV + B_DEV
    column = jnp.where(bubble_label >= 0, bubble_label // B_DEV * span + S_DEV + bubble_label % B_DEV, subdomain // S_DEV * span + subdomain % S_DEV).astype(jnp.int32)
    flat_column = column.reshape(-1)

    def precondition(residual):
        block = join(solve_planes(planes_of(residual), inverse, mults, up_planes))
        totals = jax.ops.segment_sum(residual.reshape(-1), flat_column, num_segments=COARSE)
        coarse = jnp.dot(coarse_inverse, totals, precision=lax.Precision.HIGHEST)
        correction = jnp.take(coarse, flat_column).reshape(residual.shape)
        direction = block + correction
        return (direction, jnp.sum(residual * direction))

    def operate(field):
        return operate_padded(jnp.pad(field, 1), coefs, diagonal)
    iterate = jnp.zeros_like(rhs)
    residual = rhs
    direction, product = precondition(residual)
    search = direction
    for sweep in range(ITERS):
        image = operate(search)
        alpha = product / jnp.sum(search * image)
        iterate = iterate + alpha * search
        residual = residual - alpha * image
        if sweep + 1 < ITERS:
            direction, fresh = precondition(residual)
            search = direction + fresh / product * search
            product = fresh
    return (iterate, residual)
```

```python
from functools import partial

import jax
import jax.numpy as jnp
from jax import lax
from jax.experimental import pallas as pl
from jax.experimental.pallas import tpu as pltpu
from jax.sharding import PartitionSpec as P

S_DEV = 4
B_DEV = 16
SPAN = S_DEV + B_DEV
LANES = 128
GROUPS = 4
CODES = GROUPS * B_DEV
REGIONS = S_DEV + 3 * B_DEV
SCALARS = 96
DEPTH = 3

surface_tension = 0.5
shift_term = 0.05
gas_drop = 0.75
norm_floor = 0.25
highest = lax.Precision.HIGHEST
f32 = jnp.float32
i32 = jnp.int32
bf16 = jnp.bfloat16


def iota(shape, dim):
    return lax.broadcasted_iota(i32, shape, dim)


def up_rows(field):
    return pltpu.roll(field, field.shape[0] - 1, 0)


def down_rows(field):
    return pltpu.roll(field, 1, 0)


def next_x(field):
    return pltpu.roll(field, field.shape[1] - 1, 1)


def prev_x(field):
    return pltpu.roll(field, 1, 1)


def total(field):
    rows, width = field.shape
    folded = field[:, :LANES]
    for start in range(LANES, width, LANES):
        folded = folded + field[:, start : start + LANES]
    return jnp.sum(folded.reshape(rows // 8, 8, LANES), axis=0)


def octet_sums(values, code):
    group = code // B_DEV
    inner = code % B_DEV
    spread = jnp.concatenate([jnp.where(group == g, values, 0.0) for g in range(GROUPS)], axis=0)
    high = spread.astype(bf16)
    low = (spread - high.astype(f32)).astype(bf16)
    left = jnp.concatenate([high, low], axis=0)
    right = jnp.concatenate(
        [jnp.where(inner == i, 1.0, 0.0) for i in range(B_DEV)], axis=0
    ).astype(bf16)
    return lax.dot_general(left, right, (((1,), (1,)), ((), ())), preferred_element_type=f32)


def region_row(value_ref, code_ref):
    planes, rows, _ = value_ref.shape
    octets = rows // 8

    def step(index, acc):
        plane = index // octets
        start = pl.multiple_of((index % octets) * 8, 8)
        return acc + octet_sums(value_ref[plane, pl.ds(start, 8), :], code_ref[plane, pl.ds(start, 8), :])

    acc = lax.fori_loop(
        0, planes * octets, step, jnp.zeros((2 * GROUPS * 8, B_DEV * 8), f32), unroll=4
    )
    shape = acc.shape
    kept = jnp.where(iota(shape, 0) % 8 == iota(shape, 1) % 8, acc, 0.0)
    folded = jnp.sum(kept.reshape(2 * GROUPS, 8, LANES), axis=1)
    pick = jnp.where(iota((LANES, LANES), 0) // 8 == iota((LANES, LANES), 1) % B_DEV, 1.0, 0.0)
    spread = jnp.dot(folded, pick, precision=highest, preferred_element_type=f32)
    shape = spread.shape
    lane = iota(shape, 1)
    mine = (iota(shape, 0) % GROUPS == lane // B_DEV) & (lane < CODES)
    return jnp.sum(jnp.where(mine, spread, 0.0), axis=0, keepdims=True)


def scalar_row(scalars):
    lane = iota((1, LANES), 1)
    row = jnp.zeros((1, LANES), f32)
    for index, value in enumerate(scalars):
        row = jnp.where(lane == SCALARS + index, value, row)
    return row


def lane_of(row, index):
    return jnp.sum(jnp.where(iota(row.shape, 1) == SCALARS + index, row, 0.0))


def lookup(table, index):
    rows, width = index.shape
    wide = jnp.broadcast_to(table, (rows, LANES))
    return jnp.concatenate(
        [
            jnp.take_along_axis(wide, index[:, start : start + LANES], axis=1)
            for start in range(0, width, LANES)
        ],
        axis=1,
    )


def start_all(copies):
    for copy in copies:
        copy.start()


def wait_all(copies):
    for copy in copies:
        copy.wait()


def send_coarse(row, dest_ref, send_ref):
    wide = jnp.broadcast_to(row, (8, LANES))

    def step(region, acc):
        lane = jnp.where(region < S_DEV, region, region + B_DEV - S_DEV)
        factor = jnp.take_along_axis(wide, jnp.full((8, LANES), lane, i32), axis=1)[0:1, :]
        factor = jnp.concatenate([factor, factor], axis=1)
        return acc + factor * dest_ref[region]

    send_ref[...] = lax.fori_loop(0, REGIONS, step, jnp.zeros(send_ref.shape, f32), unroll=4)


def destinations_kernel(columns, pair_ref, own_ref, near_ref, far_ref, dest_ref, wide_ref):
    devices = own_ref.shape[1]
    even_z = pair_ref[0] == 0
    wide_ref[...] = jnp.zeros(wide_ref.shape, f32)
    low_start = pl.multiple_of(jnp.where(even_z, 2 * B_DEV, 0), B_DEV) + S_DEV
    high_start = pl.multiple_of(jnp.where(even_z, 0, 2 * B_DEV), B_DEV) + S_DEV
    wide_ref[0:S_DEV, :, 0:SPAN] = own_ref[0:S_DEV]
    wide_ref[S_DEV + B_DEV : S_DEV + 2 * B_DEV, :, 0:SPAN] = own_ref[S_DEV:SPAN]
    wide_ref[pl.ds(low_start, B_DEV), :, 0:SPAN] = near_ref[...]
    wide_ref[pl.ds(high_start, B_DEV), :, 0:SPAN] = far_ref[...]
    lane = iota((devices, LANES), 1)

    def place(base, shift, first, count):
        moved = pltpu.roll(base, shift, 1) if shift else base
        return jnp.where((lane >= first) & (lane < first + count), moved, 0.0)

    def from_device(field, step):
        return pltpu.roll(field, (-step) % devices, 0) if step % devices else field

    def one(region, carry):
        base = wide_ref[region]
        bubbles = B_DEV - S_DEV
        table = place(base, 0, 0, S_DEV) + place(base, B_DEV + bubbles, 2 * B_DEV, B_DEV)
        table = table + from_device(
            place(base, S_DEV, S_DEV, S_DEV) + place(base, 2 * B_DEV + bubbles, 3 * B_DEV, B_DEV), columns
        )
        table = table + from_device(
            place(base, 2 * S_DEV, 2 * S_DEV, S_DEV) + place(base, bubbles, B_DEV, B_DEV), -columns
        )
        table = table + from_device(place(base, 3 * S_DEV, 3 * S_DEV, S_DEV), 1)
        table = table + from_device(place(base, 3 * B_DEV + bubbles, 4 * B_DEV, B_DEV), 2 * columns)
        table = table + from_device(place(base, 4 * B_DEV + bubbles, 5 * B_DEV, B_DEV), -2 * columns)
        own_codes = jnp.where((lane < S_DEV) | ((lane >= B_DEV) & (lane < CODES)), table, 0.0)
        dest_ref[region] = jnp.concatenate([table, from_device(own_codes, -1)], axis=1)
        return carry

    lax.fori_loop(0, REGIONS, one, 0)


def write_edges(even_z, even_y, value_ref, z_refs, y_refs, convert=lambda value: value):
    planes, rows, _ = value_ref.shape
    z_refs[0][...] = convert(value_ref[jnp.where(even_z, planes - 1, 0)])
    z_refs[1][...] = convert(value_ref[jnp.where(even_z, 0, planes - 1)])
    for plane in range(planes):
        first = convert(value_ref[plane, 0:1, :])
        last = convert(value_ref[plane, rows - 1 : rows, :])
        y_refs[0][plane : plane + 1, :] = jnp.where(even_y, last, first)
        y_refs[1][plane : plane + 1, :] = jnp.where(even_y, first, last)


def setup_kernel(
    edge_ref, z0_in, z1_in, y0_in, y1_in, k0_in, k1_in, frac_hbm, source_hbm, label_hbm, sub_hbm, dest_hbm,
    ez0_ref, ez1_ref, ey0_ref, ey1_ref, send_ref,
    code_hbm, r_hbm, b_hbm, cz_hbm, cyp_hbm, cym_hbm, cxp_hbm, cxm_hbm, diag_hbm, inv_hbm, mult_hbm,
    frac_ref, source_ref, label_ref, sub_ref, dest_ref,
    code_ref, r_ref, b_ref, cz_ref, cyp_ref, cym_ref, cxp_ref, cxm_ref, diag_ref, inv_ref, mult_ref,
    deep_ref, nz_ref, flat_ref, kap_ref, fz_ref, work_ref, in_sems, out_sems,
):
    planes, rows, width = frac_ref.shape
    tall = rows + 8
    first_z, last_z, first_y, last_y = (edge_ref[i] == 1 for i in range(4))
    base, stride, sub_base = edge_ref[4], edge_ref[5], edge_ref[6]
    even_z, even_y = edge_ref[7] == 0, edge_ref[8] == 0
    pairs = [(frac_hbm, frac_ref), (label_hbm, label_ref), (sub_hbm, sub_ref), (source_hbm, source_ref), (dest_hbm, dest_ref)]
    reads = [pltpu.make_async_copy(a, b, in_sems.at[i]) for i, (a, b) in enumerate(pairs)]
    start_all(reads)
    row = iota((tall, width), 0)
    lane = iota((tall, width), 1)
    inside_y = ((row < rows) | ((row < rows + 4) & jnp.logical_not(last_y))) | (
        (row >= rows + 4) & jnp.logical_not(first_y)
    )
    first_plane = jnp.where(first_z, 0, -planes)
    last_plane = jnp.where(last_z, planes, 2 * planes)

    def right_of(field):
        return jnp.where(lane[: field.shape[0]] == width - 1, 0.0, next_x(field))

    def left_of(field):
        return jnp.where(lane[: field.shape[0]] == 0, 0.0, prev_x(field))

    deep_ref[:, rows:tall, :] = jnp.zeros((planes + 2 * DEPTH, 8, width), f32)
    near_z = jnp.where(even_z, planes + DEPTH, 0)
    far_z = jnp.where(even_z, 0, planes + DEPTH)
    deep_ref[pl.ds(near_z, DEPTH), 0:rows, :] = z0_in[...]
    deep_ref[pl.ds(far_z, DEPTH), 0:rows, :] = z1_in[...]
    high, low = slice(rows, rows + DEPTH), slice(tall - DEPTH, tall)

    def fill_rows(first, second):
        deep_ref[DEPTH : planes + DEPTH, first, :] = y0_in[...]
        deep_ref[DEPTH : planes + DEPTH, second, :] = y1_in[...]
        deep_ref[pl.ds(near_z, DEPTH), first, :] = k0_in[0]
        deep_ref[pl.ds(near_z, DEPTH), second, :] = k0_in[1]
        deep_ref[pl.ds(far_z, DEPTH), first, :] = k1_in[0]
        deep_ref[pl.ds(far_z, DEPTH), second, :] = k1_in[1]

    @pl.when(even_y)
    def _():
        fill_rows(high, low)

    @pl.when(jnp.logical_not(even_y))
    def _():
        fill_rows(low, high)

    reads[0].wait()
    deep_ref[DEPTH : planes + DEPTH, 0:rows, :] = frac_ref[...]

    def mask_plane(index, carry):
        keep = (index - DEPTH >= first_plane) & (index - DEPTH < last_plane)
        deep_ref[index] = jnp.where(inside_y & keep, deep_ref[index], 0.0)
        return carry

    lax.fori_loop(0, planes + 2 * DEPTH, mask_plane, 0)

    def normal_plane(index, carry):
        keep = (index - 2 >= first_plane) & (index - 2 < last_plane)
        here = deep_ref[index + 1]
        gz = 0.5 * (deep_ref[index + 2] - deep_ref[index])
        gy = 0.5 * (up_rows(here) - down_rows(here))
        gx = 0.5 * (right_of(here) - left_of(here))
        length = jnp.maximum(jnp.sqrt(gz * gz + gy * gy + gx * gx), norm_floor)
        scale = jnp.where(inside_y & keep, 1.0 / length, 0.0)
        ny = gy * scale
        nx = gx * scale
        nz_ref[index] = gz * scale
        flat_ref[index] = 0.5 * (up_rows(ny) - down_rows(ny)) + 0.5 * (right_of(nx) - left_of(nx))
        return carry

    lax.fori_loop(0, planes + 4, normal_plane, 0)

    def kappa_plane(index, carry):
        keep = (index - 1 >= first_plane) & (index - 1 < last_plane)
        value = -(0.5 * (nz_ref[index + 2] - nz_ref[index]) + flat_ref[index + 1])
        kap_ref[index] = jnp.where(inside_y & keep, value, 0.0)
        return carry

    lax.fori_loop(0, planes + 2, kappa_plane, 0)
    mid = pl.ds(0, rows)

    def z_face(index, carry):
        f_low = deep_ref[index + 2, mid, :]
        f_high = deep_ref[index + 3, mid, :]
        coef = 2.0 / ((1.0 - gas_drop * f_low) + (1.0 - gas_drop * f_high))
        cz_ref[index] = coef
        mean = 0.5 * (kap_ref[index, mid, :] + kap_ref[index + 1, mid, :])
        fz_ref[index] = coef * mean * (f_high - f_low)
        return carry

    lax.fori_loop(0, planes + 1, z_face, 0)
    row_mid = row[:rows]
    lane_mid = lane[:rows]
    wait_all(reads[1:])

    def assemble_plane(plane, carry):
        inv_before, g_before = carry
        f = deep_ref[plane + 3]
        k = kap_ref[plane + 1]
        d = 1.0 - gas_drop * f
        f_up = up_rows(f)
        cy = 2.0 / (d + (1.0 - gas_drop * f_up))
        fy = cy * (0.5 * (k + up_rows(k))) * (f_up - f)
        cyp, cym = cy[:rows], down_rows(cy)[:rows]
        sum_y = fy[:rows] - down_rows(fy)[:rows]
        f, k, d = f[:rows], k[:rows], d[:rows]
        f_right = right_of(f)
        cxp = 2.0 / (d + (1.0 - gas_drop * f_right))
        fx = cxp * (0.5 * (k + right_of(k))) * (f_right - f)
        outer = 2.0 / (d + 1.0)
        cxm = jnp.where(lane_mid == 0, outer, prev_x(cxp))
        fx_before = jnp.where(lane_mid == 0, outer * (0.5 * k) * f, prev_x(fx))
        terms = fz_ref[plane + 1] - fz_ref[plane] + sum_y + (fx - fx_before)
        rhs = source_ref[plane] - surface_tension * terms
        down = cz_ref[plane]
        diagonal = shift_term + (cz_ref[plane + 1] + down + cyp + cym + cxp + cxm)
        mult = down * inv_before
        inv = 1.0 / (diagonal - mult * down)
        g = rhs + mult * g_before
        r_ref[plane] = rhs
        diag_ref[plane] = diagonal
        mult_ref[plane] = mult
        inv_ref[plane] = inv
        work_ref[plane] = g
        cyp_ref[plane] = jnp.where((row_mid == rows - 1) & last_y, 0.0, cyp)
        cym_ref[plane] = jnp.where((row_mid == 0) & first_y, 0.0, cym)
        cxp_ref[plane] = jnp.where(lane_mid == width - 1, 0.0, cxp)
        cxm_ref[plane] = jnp.where(lane_mid == 0, 0.0, cxm)
        label = label_ref[plane]
        offset = label - base
        below = offset < 0
        above = offset >= stride
        group = jnp.where(below, 1, jnp.where(above, 3, 2))
        inner = jnp.where(below, offset + stride, jnp.where(above, offset - stride, offset))
        code = jnp.where(label >= 0, group * B_DEV + inner, sub_ref[plane] - sub_base)
        code_ref[plane] = code & (CODES - 1)
        return (inv, g)

    blank = jnp.zeros((rows, width), f32)
    lax.fori_loop(0, planes, assemble_plane, (blank, blank))

    def backward(step, after):
        plane = planes - 1 - step
        value = (work_ref[plane] + cz_ref[plane + 1] * after) * inv_ref[plane]
        b_ref[plane] = value
        return value

    lax.fori_loop(0, planes, backward, blank)
    cz_ref[0] = jnp.where(first_z, 0.0, cz_ref[0])
    cz_ref[planes] = jnp.where(last_z, 0.0, cz_ref[planes])
    pairs = [
        (code_ref, code_hbm), (r_ref, r_hbm), (b_ref, b_hbm), (cz_ref, cz_hbm), (cyp_ref, cyp_hbm), (cym_ref, cym_hbm),
        (cxp_ref, cxp_hbm), (cxm_ref, cxm_hbm), (diag_ref, diag_hbm), (inv_ref, inv_hbm), (mult_ref, mult_hbm),
    ]
    writes = [pltpu.make_async_copy(a, b, out_sems.at[i]) for i, (a, b) in enumerate(pairs)]
    start_all(writes)
    write_edges(even_z, even_y, b_ref, [ez0_ref.at[0], ez1_ref.at[0]], [ey0_ref.at[0], ey1_ref.at[0]])
    write_edges(
        even_z, even_y, code_ref, [ez0_ref.at[1], ez1_ref.at[1]], [ey0_ref.at[1], ey1_ref.at[1]],
        convert=lambda value: value.astype(f32),
    )
    send_coarse(region_row(r_ref, code_ref), dest_ref, send_ref)
    wait_all(writes)


def scalars_of(sums):
    alphas, betas, curves = [], [None], []
    for step, row in enumerate(sums):
        gamma = lane_of(row, 0)
        if step == 0:
            curve = lane_of(row, 1)
        else:
            beta = gamma / lane_of(sums[step - 1], 0)
            betas.append(beta)
            curve = lane_of(row, 1) + beta * (lane_of(row, 2) + beta * curves[-1])
        curves.append(curve)
        alphas.append(gamma / curve)
    return alphas, betas


def step_kernel(stage, *refs):
    refs = list(refs)

    def take(count):
        out = refs[:count]
        del refs[:count]
        return out

    (edge_ref,) = take(1)
    parts = take(stage + 1)
    halos = [take(4) for _ in range(stage + 1)]
    last = stage == 2
    states = (("b", "r"), ("b", "u0", "r", "w0", "z0"), ("b", "u0", "u1", "r", "w0", "w1", "z0", "z1"))[stage]
    first_names = ("code", "b") + tuple(name for name in states if name[0] == "u")
    later_names = tuple(name for name in states if name not in first_names)
    matrix_names = ("cz", "cyp", "cym", "cxp", "cxm", "diag") + (() if last else ("inv", "mult", "dest"))
    names = first_names + matrix_names[:6] + later_names + matrix_names[6:]
    sources = dict(zip(names, take(len(names))))
    out_names = (("z", "w", "u"), ("z", "w", "u", "bn", "rn"), ("z", "w", "p", "s", "rn"))[stage]
    if not last:
        edges_z, edges_y = take(2), take(2)
    (send_ref,) = take(1)
    sinks = dict(zip(out_names, take(len(out_names))))
    held = dict(zip(names, take(len(names))))
    pad_ref, side_ref = take(2)
    made = {"z": pad_ref.at[pl.ds(1, pad_ref.shape[0] - 2)]}
    for name in out_names[1:]:
        (made[name],) = take(1)
    if not last:
        (work_ref,) = take(1)
    in_sems, out_sems = take(2)

    reads = {name: pltpu.make_async_copy(sources[name], held[name], in_sems.at[i]) for i, name in enumerate(names)}
    start_all(reads.values())
    writes = {name: pltpu.make_async_copy(made[name], sinks[name], out_sems.at[i]) for i, name in enumerate(out_names)}
    code_ref = held["code"]
    planes, rows, width = code_ref.shape
    even_z, even_y = edge_ref[7] == 0, edge_ref[8] == 0

    sums = [jnp.sum(part[...], axis=0, keepdims=True) for part in parts]
    alphas, betas = scalars_of([row[:, :LANES] for row in sums[1:]])
    table = sums[0]
    if stage >= 1:
        table = table - alphas[0] * sums[1]
    if stage == 2:
        table = table - alphas[1] * (sums[2] + betas[1] * sums[1])
    near, side = table[:, :LANES], table[:, LANES:]

    def combine(values):
        out = values[0]
        if stage >= 1:
            out = out - alphas[0] * values[1]
        if stage == 2:
            out = out - alphas[1] * (values[2] + betas[1] * values[1])
        return out

    for slot in range(2):
        upper = even_z if slot == 0 else jnp.logical_not(even_z)
        index = halos[0][slot][1].astype(i32)
        high = jnp.where(index < B_DEV, index + S_DEV, index + B_DEV)
        low = jnp.where(
            index < B_DEV, index + 2 * S_DEV, jnp.where(index < 2 * B_DEV, index + 4 * B_DEV, index - B_DEV)
        )
        block = combine([halos[0][slot][0]] + [halo[slot][...] for halo in halos[1:]])
        pad_ref[jnp.where(upper, planes + 1, 0)] = block + lookup(near, jnp.where(upper, high, low))
        upper = even_y if slot == 0 else jnp.logical_not(even_y)
        index = halos[0][2 + slot][1].astype(i32)
        block = combine([halos[0][2 + slot][0]] + [halo[2 + slot][...] for halo in halos[1:]])
        found = jnp.where(
            upper, lookup(near, (index & (B_DEV - 1)) + 3 * S_DEV), lookup(side, index)
        )
        side_ref[jnp.where(upper, 1, 0)] = block + found

    for name in first_names:
        reads[name].wait()

    def direction(plane, carry):
        block = held["b"][plane]
        if stage == 1:
            block = block - alphas[0] * held["u0"][plane]
            made["bn"][plane] = block
        if stage == 2:
            block = block - alphas[1] * (held["u1"][plane] + betas[1] * held["u0"][plane])
        pad_ref[plane + 1] = block + lookup(near, code_ref[plane])
        return carry

    lax.fori_loop(0, planes, direction, 0)
    writes["z"].start()
    for name in names:
        if name not in first_names and name != "dest":
            reads[name].wait()
    row = iota((rows, width), 0)

    def image_plane(plane, carry):
        sums, before = carry
        here = pad_ref[plane + 1]
        north = jnp.where(row == rows - 1, side_ref[1, pl.ds(plane, 1), :], up_rows(here))
        south = jnp.where(row == 0, side_ref[0, pl.ds(plane, 1), :], down_rows(here))
        image = held["diag"][plane] * here - (
            held["cz"][plane + 1] * pad_ref[plane + 2]
            + held["cz"][plane] * pad_ref[plane]
            + held["cyp"][plane] * north
            + held["cym"][plane] * south
            + held["cxp"][plane] * next_x(here)
            + held["cxm"][plane] * prev_x(here)
        )
        made["w"][plane] = image
        residual = held["r"][plane]
        if stage == 1:
            old_z, old_w = held["z0"][plane], held["w0"][plane]
            residual = residual - alphas[0] * old_w
            made["rn"][plane] = residual
        if stage == 2:
            old_z = held["z1"][plane] + betas[1] * held["z0"][plane]
            old_w = held["w1"][plane] + betas[1] * held["w0"][plane]
            made["p"][plane] = old_z
            made["s"][plane] = old_w
            residual = residual - alphas[1] * old_w
            made["rn"][plane] = residual
        found = [total(residual * here), total(here * image)]
        if stage >= 1:
            found.append(total(here * old_w + old_z * image))
        if not last:
            before = image + held["mult"][plane] * before
            work_ref[plane] = before
        return tuple(old + new for old, new in zip(sums, found)), before

    blank = jnp.zeros((8, LANES), f32)
    empty = jnp.zeros((rows, width), f32)
    dots, _ = lax.fori_loop(
        0, planes, image_plane, ((blank,) * (3 if stage else 2), blank if last else empty)
    )
    for name in out_names[1:]:
        if name != "u":
            writes[name].start()
    row = scalar_row([jnp.sum(value) for value in dots])
    if last:
        send_ref[...] = jnp.broadcast_to(row, send_ref.shape)
    else:

        def backward(step, after):
            plane = planes - 1 - step
            value = (work_ref[plane] + held["cz"][plane + 1] * after) * held["inv"][plane]
            made["u"][plane] = value
            return value

        lax.fori_loop(0, planes, backward, empty)
        writes["u"].start()
        write_edges(even_z, even_y, made["u"], edges_z, edges_y)
        reads["dest"].wait()
        send_coarse(region_row(made["w"], code_ref), held["dest"], send_ref)
        send_ref[:, :LANES] = send_ref[:, :LANES] + row
    wait_all(writes.values())


def final_kernel(
    d0_ref, d1_ref, d2_ref, r_hbm, w_hbm, s_hbm, z0_hbm, p_hbm, z_hbm, x_out, r_out,
    r_ref, w_ref, s_ref, z0_ref, p_ref, z_ref, x_ref, in_sems, out_sems,
):
    pairs = [(z0_hbm, z0_ref), (p_hbm, p_ref), (z_hbm, z_ref), (r_hbm, r_ref), (w_hbm, w_ref), (s_hbm, s_ref)]
    reads = [pltpu.make_async_copy(a, b, in_sems.at[i]) for i, (a, b) in enumerate(pairs)]
    start_all(reads)
    sums = [jnp.sum(ref[:, :LANES], axis=0, keepdims=True) for ref in (d0_ref, d1_ref, d2_ref)]
    alphas, betas = scalars_of(sums)
    mixed = alphas[2] * betas[2]
    along = alphas[1] + mixed
    wait_all(reads[:3])
    x_ref[...] = alphas[0] * z0_ref[...] + along * p_ref[...] + alphas[2] * z_ref[...]
    x_write = pltpu.make_async_copy(x_ref, x_out, out_sems.at[0])
    x_write.start()
    wait_all(reads[3:])
    r_ref[...] = r_ref[...] - (alphas[2] * w_ref[...] + mixed * s_ref[...])
    r_write = pltpu.make_async_copy(r_ref, r_out, out_sems.at[1])
    r_write.start()
    x_write.wait()
    r_write.wait()


def in_hbm(shape):
    return ("hbm", shape)


def call(kernel, outs, scratch, args, name):
    spaces = {"smem": pltpu.SMEM, "vmem": pltpu.VMEM, "hbm": pltpu.HBM}

    def specs(items):
        return [pl.BlockSpec(memory_space=spaces[space]) for space, _ in items]

    return pl.pallas_call(
        kernel,
        out_shape=[shape for _, shape in outs],
        in_specs=specs(args),
        out_specs=specs(outs),
        scratch_shapes=scratch,
        compiler_params=pltpu.CompilerParams(vmem_limit_bytes=48 * 1024 * 1024),
        name=name,
    )(*(value for _, value in args))


def swaps(axis, first):
    count = lax.axis_size(axis)
    pairs = []
    for i in range(first, count + first, 2):
        low, high = i % count, (i + 1) % count
        pairs += [(low, high), (high, low)]
    return pairs


def swap(block, axis, first):
    return lax.ppermute(block, axis, swaps(axis, first))


def on_device(fraction, source, bubble_label, subdomain, coarse_inverse):
    planes, rows, width = fraction.shape
    slabs = lax.axis_size("gz")
    columns = lax.axis_size("gy")
    devices = slabs * columns
    slab = lax.axis_index("gz")
    column = lax.axis_index("gy")
    here = slab * columns + column
    even_z = slab % 2 == 0
    even_y = column % 2 == 0
    field = jax.ShapeDtypeStruct((planes, rows, width), f32)

    def shape(*dims, dtype=f32):
        return jax.ShapeDtypeStruct(dims, dtype)

    def vmem(*dims, dtype=f32):
        return pltpu.VMEM(dims, dtype)

    def like(items):
        return [vmem(*value.shape, dtype=value.dtype) for value in items]

    def semaphores(count):
        return pltpu.SemaphoreType.DMA((count,))

    def tag(space, items):
        return [(space, item) for item in items]

    top = lax.dynamic_slice_in_dim(fraction, jnp.where(even_z, planes - DEPTH, 0), DEPTH, 0)
    bottom = lax.dynamic_slice_in_dim(fraction, jnp.where(even_z, 0, planes - DEPTH), DEPTH, 0)
    left, right = fraction[:, :DEPTH], fraction[:, rows - DEPTH :]
    y_in = [
        swap(jnp.where(even_y, right, left), "gy", 0),
        swap(jnp.where(even_y, left, right), "gy", 1),
    ]
    z_in = [swap(top, "gz", 0), swap(bottom, "gz", 1)]
    corner = jnp.stack(y_in)
    corner_top = jnp.where(even_z, corner[:, planes - DEPTH :], corner[:, :DEPTH])
    corner_bottom = jnp.where(even_z, corner[:, :DEPTH], corner[:, planes - DEPTH :])
    corner_in = [swap(corner_top, "gz", 0), swap(corner_bottom, "gz", 1)]
    bubbles = coarse_inverse[S_DEV:]
    coarse_in = [swap(bubbles, "gz", 0), swap(bubbles, "gz", 1)]
    edge = jnp.stack(
        [
            (slab == 0).astype(i32),
            (slab == slabs - 1).astype(i32),
            (column == 0).astype(i32),
            (column == columns - 1).astype(i32),
            here * B_DEV,
            jnp.int32(columns * B_DEV),
            here * S_DEV,
            slab % 2,
            column % 2,
        ]
    )

    def spread(matrix):
        return matrix.reshape(matrix.shape[0], devices, SPAN)

    dest_shape = shape(REGIONS, devices, 2 * LANES)
    (dest,) = call(
        partial(destinations_kernel, columns),
        tag("vmem", [dest_shape]),
        [vmem(REGIONS, devices, LANES)],
        tag("smem", [(slab % 2).reshape(1)]) + tag("vmem", [spread(coarse_inverse)] + [spread(m) for m in coarse_in]),
        "destinations",
    )
    codes = shape(planes, rows, width, dtype=i32)
    faces = shape(planes + 1, rows, width)
    inputs = [fraction, source, bubble_label, subdomain, dest]
    made = [codes, field, field, faces] + [field] * 7
    tall = rows + 8
    wide = shape(devices, 2 * LANES)
    first_edges = [shape(2, rows, width)] * 2 + [shape(2, planes, width)] * 2
    later_edges = [shape(rows, width)] * 2 + [shape(planes, width)] * 2
    *sent, send, code, r0, b0, cz, cyp, cym, cxp, cxm, diag, inv, mult = call(
        setup_kernel,
        tag("vmem", first_edges + [wide]) + tag("hbm", made),
        like(inputs)
        + like(made)
        + [
            vmem(planes + 2 * DEPTH, tall, width),
            vmem(planes + 4, tall, width),
            vmem(planes + 4, tall, width),
            vmem(planes + 2, tall, width),
            vmem(planes + 1, rows, width),
            vmem(planes, rows, width),
            semaphores(len(inputs)),
            semaphores(len(made)),
        ],
        tag("smem", [edge]) + tag("vmem", z_in + y_in + corner_in) + tag("hbm", inputs),
        "setup",
    )

    def exchange(parts):
        return lax.all_to_all(parts, ("gz", "gy"), 0, 0)

    def halos(sent):
        return [swap(sent[0], "gz", 0), swap(sent[1], "gz", 1), swap(sent[2], "gy", 0), swap(sent[3], "gy", 1)]

    def step(stage, parts, edges, first, later):
        last = stage == 2
        matrix = [cz, cyp, cym, cxp, cxm, diag]
        operands = [code] + first + matrix + later + ([] if last else [inv, mult, dest])
        outs = [field] * (3, 5, 5)[stage]
        ends = [] if last else later_edges
        scratch = like(operands) + [vmem(planes + 2, rows, width), vmem(2, planes, width)] + like(outs[1:])
        if not last:
            scratch.append(vmem(planes, rows, width))
        scratch += [semaphores(len(operands)), semaphores(len(outs))]
        results = call(
            partial(step_kernel, stage),
            tag("vmem", ends + [shape(devices, LANES) if last else wide]) + tag("hbm", outs),
            scratch,
            tag("smem", [edge]) + tag("vmem", parts + edges) + tag("hbm", operands),
            f"step{stage}",
        )
        return results[: len(ends)], results[len(ends)], results[len(ends) + 1 :]

    edges = halos(sent)
    parts = [exchange(send)]
    sent, send, (z0, w0, u0) = step(0, parts, edges, [b0], [r0])
    edges = edges + halos(sent)
    parts = parts + [exchange(send)]
    sent, send, (z1, w1, u1, b1, r1) = step(1, parts, edges, [b0, u0], [r0, w0, z0])
    edges = edges + halos(sent)
    parts = parts + [exchange(send)]
    _, send, (z2, w2, p1, s1, r2) = step(2, parts, edges, [b1, u0, u1], [r1, w0, w1, z0, z1])
    parts = parts + [exchange(send)]
    return tuple(
        call(
            final_kernel,
            tag("hbm", [field, field]),
            like([field] * 7) + [semaphores(6), semaphores(2)],
            tag("vmem", parts[1:]) + tag("hbm", [r2, w2, s1, z0, p1, z2]),
            "finish",
        )
    )


def solution(mesh):
    placed = (
        P("gz", "gy", None),
        P("gz", "gy", None),
        P("gz", "gy", None),
        P("gz", "gy", None),
        P(("gz", "gy"), None),
    )
    return jax.shard_map(
        on_device,
        mesh=mesh,
        in_specs=placed,
        out_specs=(P("gz", "gy", None), P("gz", "gy", None)),
        check_vma=False,
    )
```

```python
import math
from functools import partial

import jax
import jax.numpy as jnp
from jax import lax
from jax.experimental import pallas as pl
from jax.experimental.pallas import tpu as pltpu
from jax.sharding import PartitionSpec as P

S_DEV = 4
B_DEV = 16
SPAN = S_DEV + B_DEV
LANES = 128
GROUPS = 4
CODES = GROUPS * B_DEV
REGIONS = S_DEV + 3 * B_DEV
SCALARS = 96
DEPTH = 3
PIECE = 16

surface_tension = 0.5
shift_term = 0.05
gas_drop = 0.75
norm_floor = 0.25
highest = lax.Precision.HIGHEST
f32 = jnp.float32
i32 = jnp.int32
bf16 = jnp.bfloat16


def iota(shape, dim):
    return lax.broadcasted_iota(i32, shape, dim)


def up_rows(field):
    return pltpu.roll(field, field.shape[0] - 1, 0)


def down_rows(field):
    return pltpu.roll(field, 1, 0)


def next_x(field):
    return pltpu.roll(field, field.shape[1] - 1, 1)


def prev_x(field):
    return pltpu.roll(field, 1, 1)


def total(field):
    rows, width = field.shape
    folded = field[:, :LANES]
    for start in range(LANES, width, LANES):
        folded = folded + field[:, start : start + LANES]
    return jnp.sum(folded.reshape(rows // 8, 8, LANES), axis=0)


def piece_sums(values, code):
    group = (code // B_DEV).astype(f32).astype(bf16)
    inner = (code % B_DEV).astype(f32).astype(bf16)
    high = values.astype(bf16)
    low = (values - high.astype(f32)).astype(bf16)
    zero, one = jnp.zeros_like(high), jnp.ones_like(high)
    left = [jnp.where(group == g, part, zero) for part in (high, low) for g in range(GROUPS)]
    right = [jnp.where(inner == i, one, zero) for i in range(B_DEV)]
    return lax.dot_general(
        jnp.concatenate(left, axis=0),
        jnp.concatenate(right, axis=0),
        (((1,), (1,)), ((), ())),
        preferred_element_type=f32,
    )


def region_row(value_ref, code_ref):
    planes, rows, _ = value_ref.shape
    pieces = rows // PIECE

    def step(index, acc):
        plane = index // pieces
        piece = pl.ds(pl.multiple_of((index % pieces) * PIECE, PIECE), PIECE)
        return acc + piece_sums(value_ref[plane, piece, :], code_ref[plane, piece, :])

    acc = lax.fori_loop(
        0, planes * pieces, step, jnp.zeros((2 * GROUPS * PIECE, B_DEV * PIECE), f32), unroll=planes * pieces
    )
    shape = acc.shape
    kept = jnp.where(iota(shape, 0) % PIECE == iota(shape, 1) % PIECE, acc, 0.0)
    folded = jnp.sum(kept.reshape(2 * GROUPS, PIECE, shape[1]), axis=1)
    shape = (shape[1], LANES)
    pick = jnp.where(iota(shape, 0) // PIECE == iota(shape, 1) % B_DEV, 1.0, 0.0)
    spread = jnp.dot(folded, pick, precision=highest, preferred_element_type=f32)
    shape = spread.shape
    lane = iota(shape, 1)
    mine = (iota(shape, 0) % GROUPS == lane // B_DEV) & (lane < CODES)
    return jnp.sum(jnp.where(mine, spread, 0.0), axis=0, keepdims=True)


def scalar_row(scalars):
    lane = iota((1, LANES), 1)
    row = jnp.zeros((1, LANES), f32)
    for index, value in enumerate(scalars):
        row = jnp.where(lane == SCALARS + index, value, row)
    return row


def lane_of(row, index):
    return jnp.sum(jnp.where(iota(row.shape, 1) == SCALARS + index, row, 0.0))


def lookup(table, index):
    rows, width = index.shape
    wide = jnp.broadcast_to(table, (rows, LANES))
    return jnp.concatenate(
        [
            jnp.take_along_axis(wide, index[:, start : start + LANES], axis=1)
            for start in range(0, width, LANES)
        ],
        axis=1,
    )


def start_all(copies):
    for copy in copies:
        copy.start()


def wait_all(copies):
    for copy in copies:
        copy.wait()


def coarse_parts(row, dest_ref):
    wide = jnp.broadcast_to(row, (8, LANES))

    def step(region, acc):
        lane = jnp.where(region < S_DEV, region, region + B_DEV - S_DEV)
        factor = jnp.take_along_axis(wide, jnp.full((8, LANES), lane, i32), axis=1)[0:1, :]
        return acc + factor * dest_ref[region]

    return lax.fori_loop(0, REGIONS, step, jnp.zeros(dest_ref.shape[1:], f32), unroll=4)


def destinations_kernel(columns, pair_ref, own_ref, near_ref, far_ref, dest_hbm, wide_ref, dest_ref, sems):
    devices = own_ref.shape[1]
    even_z = pair_ref[0] == 0
    wide_ref[...] = jnp.zeros(wide_ref.shape, f32)
    low_start = pl.multiple_of(jnp.where(even_z, 2 * B_DEV, 0), B_DEV) + S_DEV
    high_start = pl.multiple_of(jnp.where(even_z, 0, 2 * B_DEV), B_DEV) + S_DEV
    wide_ref[0:S_DEV, :, 0:SPAN] = own_ref[0:S_DEV]
    wide_ref[S_DEV + B_DEV : S_DEV + 2 * B_DEV, :, 0:SPAN] = own_ref[S_DEV:SPAN]
    wide_ref[pl.ds(low_start, B_DEV), :, 0:SPAN] = near_ref[...]
    wide_ref[pl.ds(high_start, B_DEV), :, 0:SPAN] = far_ref[...]
    lane = iota((devices, LANES), 1)

    def place(base, shift, first, count):
        moved = pltpu.roll(base, shift, 1) if shift else base
        return jnp.where((lane >= first) & (lane < first + count), moved, 0.0)

    def from_device(field, step):
        return pltpu.roll(field, (-step) % devices, 0) if step % devices else field

    def one(region, carry):
        base = wide_ref[region]
        bubbles = B_DEV - S_DEV
        table = place(base, 0, 0, S_DEV) + place(base, B_DEV + bubbles, 2 * B_DEV, B_DEV)
        table = table + from_device(
            place(base, S_DEV, S_DEV, S_DEV) + place(base, 2 * B_DEV + bubbles, 3 * B_DEV, B_DEV), columns
        )
        table = table + from_device(
            place(base, 2 * S_DEV, 2 * S_DEV, S_DEV) + place(base, bubbles, B_DEV, B_DEV), -columns
        )
        table = table + from_device(place(base, 3 * S_DEV, 3 * S_DEV, S_DEV), 1)
        table = table + from_device(place(base, 3 * B_DEV + bubbles, 4 * B_DEV, B_DEV), 2 * columns)
        table = table + from_device(place(base, 4 * B_DEV + bubbles, 5 * B_DEV, B_DEV), -2 * columns)
        own_codes = jnp.where((lane < S_DEV) | ((lane >= B_DEV) & (lane < CODES)), table, 0.0)
        dest_ref[region, pl.ds(0, devices, stride=2), :] = table
        dest_ref[region, pl.ds(1, devices, stride=2), :] = from_device(own_codes, -1)
        return carry

    lax.fori_loop(0, REGIONS, one, 0, unroll=4)
    write = pltpu.make_async_copy(dest_ref, dest_hbm, sems.at[0])
    write.start()
    write.wait()


def write_edges(even_z, even_y, value_ref, z_refs, y_refs, convert=lambda value: value):
    planes, rows, _ = value_ref.shape
    z_refs[0][...] = convert(value_ref[jnp.where(even_z, planes - 1, 0)])
    z_refs[1][...] = convert(value_ref[jnp.where(even_z, 0, planes - 1)])
    for plane in range(planes):
        first = convert(value_ref[plane, 0:1, :])
        last = convert(value_ref[plane, rows - 1 : rows, :])
        y_refs[0][plane : plane + 1, :] = jnp.where(even_y, last, first)
        y_refs[1][plane : plane + 1, :] = jnp.where(even_y, first, last)


def slices_kernel(edge_ref, frac_hbm, coarse_hbm, z0_ref, z1_ref, y0_ref, y1_ref, bubble_ref, frac_ref, coarse_ref, sems):
    planes, rows, _ = frac_ref.shape
    copies = [
        pltpu.make_async_copy(frac_hbm, frac_ref, sems.at[0]),
        pltpu.make_async_copy(coarse_hbm, coarse_ref, sems.at[1]),
    ]
    start_all(copies)
    even_z, even_y = edge_ref[7] == 0, edge_ref[8] == 0
    wait_all(copies)
    bubble_ref[...] = coarse_ref[S_DEV:SPAN, :]
    z0_ref[...] = frac_ref[pl.ds(jnp.where(even_z, planes - DEPTH, 0), DEPTH)]
    z1_ref[...] = frac_ref[pl.ds(jnp.where(even_z, 0, planes - DEPTH), DEPTH)]
    first, last = frac_ref[:, 0:DEPTH, :], frac_ref[:, rows - DEPTH : rows, :]
    y0_ref[...] = jnp.where(even_y, last, first)
    y1_ref[...] = jnp.where(even_y, first, last)


def setup_kernel(
    edge_ref, z0_in, z1_in, y0_in, y1_in, k0_in, k1_in, frac_hbm, source_hbm, label_hbm, sub_hbm, dest_hbm,
    ez0_ref, ez1_ref, ey0_ref, ey1_ref, send_ref,
    code_hbm, r_hbm, b_hbm, cz_hbm, cyp_hbm, cym_hbm, cxp_hbm, cxm_hbm, diag_hbm, inv_hbm, mult_hbm,
    frac_ref, source_ref, label_ref, sub_ref, dest_ref,
    code_ref, r_ref, b_ref, cz_ref, cyp_ref, cym_ref, cxp_ref, cxm_ref, diag_ref, inv_ref, mult_ref,
    deep_ref, nz_ref, flat_ref, kap_ref, fz_ref, work_ref, in_sems, out_sems,
):
    planes, rows, width = frac_ref.shape
    tall = rows + 8
    first_z, last_z, first_y, last_y = (edge_ref[i] == 1 for i in range(4))
    base, stride, sub_base = edge_ref[4], edge_ref[5], edge_ref[6]
    even_z, even_y = edge_ref[7] == 0, edge_ref[8] == 0
    pairs = [(frac_hbm, frac_ref), (label_hbm, label_ref), (sub_hbm, sub_ref), (source_hbm, source_ref), (dest_hbm, dest_ref)]
    reads = [pltpu.make_async_copy(a, b, in_sems.at[i]) for i, (a, b) in enumerate(pairs)]
    start_all(reads)
    row = iota((tall, width), 0)
    lane = iota((tall, width), 1)
    inside_y = ((row < rows) | ((row < rows + 4) & jnp.logical_not(last_y))) | (
        (row >= rows + 4) & jnp.logical_not(first_y)
    )
    first_plane = jnp.where(first_z, 0, -planes)
    last_plane = jnp.where(last_z, planes, 2 * planes)

    def right_of(field):
        return jnp.where(lane[: field.shape[0]] == width - 1, 0.0, next_x(field))

    def left_of(field):
        return jnp.where(lane[: field.shape[0]] == 0, 0.0, prev_x(field))

    deep_ref[:, rows:tall, :] = jnp.zeros((planes + 2 * DEPTH, 8, width), f32)
    near_z = jnp.where(even_z, planes + DEPTH, 0)
    far_z = jnp.where(even_z, 0, planes + DEPTH)
    deep_ref[pl.ds(near_z, DEPTH), 0:rows, :] = z0_in[...]
    deep_ref[pl.ds(far_z, DEPTH), 0:rows, :] = z1_in[...]
    high, low = slice(rows, rows + DEPTH), slice(tall - DEPTH, tall)

    def fill_rows(first, second):
        deep_ref[DEPTH : planes + DEPTH, first, :] = y0_in[...]
        deep_ref[DEPTH : planes + DEPTH, second, :] = y1_in[...]
        deep_ref[pl.ds(near_z, DEPTH), first, :] = k0_in[0]
        deep_ref[pl.ds(near_z, DEPTH), second, :] = k0_in[1]
        deep_ref[pl.ds(far_z, DEPTH), first, :] = k1_in[0]
        deep_ref[pl.ds(far_z, DEPTH), second, :] = k1_in[1]

    @pl.when(even_y)
    def _():
        fill_rows(high, low)

    @pl.when(jnp.logical_not(even_y))
    def _():
        fill_rows(low, high)

    reads[0].wait()
    deep_ref[DEPTH : planes + DEPTH, 0:rows, :] = frac_ref[...]

    def mask_plane(index, carry):
        keep = (index - DEPTH >= first_plane) & (index - DEPTH < last_plane)
        deep_ref[index] = jnp.where(inside_y & keep, deep_ref[index], 0.0)
        return carry

    lax.fori_loop(0, planes + 2 * DEPTH, mask_plane, 0)

    def normal_plane(index, carry):
        keep = (index - 2 >= first_plane) & (index - 2 < last_plane)
        here = deep_ref[index + 1]
        gz = 0.5 * (deep_ref[index + 2] - deep_ref[index])
        gy = 0.5 * (up_rows(here) - down_rows(here))
        gx = 0.5 * (right_of(here) - left_of(here))
        scale = jnp.minimum(lax.rsqrt(gz * gz + gy * gy + gx * gx), 1.0 / norm_floor)
        scale = jnp.where(inside_y & keep, scale, 0.0)
        ny = gy * scale
        nx = gx * scale
        nz_ref[index] = gz * scale
        flat_ref[index] = 0.5 * (up_rows(ny) - down_rows(ny)) + 0.5 * (right_of(nx) - left_of(nx))
        return carry

    lax.fori_loop(0, planes + 4, normal_plane, 0)

    def kappa_plane(index, carry):
        keep = (index - 1 >= first_plane) & (index - 1 < last_plane)
        value = -(0.5 * (nz_ref[index + 2] - nz_ref[index]) + flat_ref[index + 1])
        kap_ref[index] = jnp.where(inside_y & keep, value, 0.0)
        return carry

    lax.fori_loop(0, planes + 2, kappa_plane, 0)
    mid = pl.ds(0, rows)

    def z_face(index, carry):
        f_low = deep_ref[index + 2, mid, :]
        f_high = deep_ref[index + 3, mid, :]
        coef = 2.0 / ((1.0 - gas_drop * f_low) + (1.0 - gas_drop * f_high))
        cz_ref[index] = coef
        mean = 0.5 * (kap_ref[index, mid, :] + kap_ref[index + 1, mid, :])
        fz_ref[index] = coef * mean * (f_high - f_low)
        return carry

    lax.fori_loop(0, planes + 1, z_face, 0)
    row_mid = row[:rows]
    lane_mid = lane[:rows]
    wait_all(reads[1:])

    def assemble_plane(plane, carry):
        inv_before, g_before = carry
        f = deep_ref[plane + 3]
        k = kap_ref[plane + 1]
        d = 1.0 - gas_drop * f
        f_up = up_rows(f)
        cy = 2.0 / (d + (1.0 - gas_drop * f_up))
        fy = cy * (0.5 * (k + up_rows(k))) * (f_up - f)
        cyp, cym = cy[:rows], down_rows(cy)[:rows]
        sum_y = fy[:rows] - down_rows(fy)[:rows]
        f, k, d = f[:rows], k[:rows], d[:rows]
        f_right = right_of(f)
        cxp = 2.0 / (d + (1.0 - gas_drop * f_right))
        fx = cxp * (0.5 * (k + right_of(k))) * (f_right - f)
        outer = jnp.concatenate([2.0 / (d[:, :LANES] + 1.0), jnp.zeros((rows, width - LANES), f32)], axis=1)
        cxm = jnp.where(lane_mid == 0, outer, prev_x(cxp))
        fx_before = jnp.where(lane_mid == 0, outer * (0.5 * k) * f, prev_x(fx))
        terms = fz_ref[plane + 1] - fz_ref[plane] + sum_y + (fx - fx_before)
        rhs = source_ref[plane] - surface_tension * terms
        down = cz_ref[plane]
        diagonal = shift_term + (cz_ref[plane + 1] + down + cyp + cym + cxp + cxm)
        mult = down * inv_before
        inv = 1.0 / (diagonal - mult * down)
        g = rhs + mult * g_before
        r_ref[plane] = rhs
        diag_ref[plane] = diagonal
        mult_ref[plane] = mult
        inv_ref[plane] = inv
        work_ref[plane] = g
        cyp_ref[plane] = jnp.where((row_mid == rows - 1) & last_y, 0.0, cyp)
        cym_ref[plane] = jnp.where((row_mid == 0) & first_y, 0.0, cym)
        cxp_ref[plane] = jnp.where(lane_mid == width - 1, 0.0, cxp)
        cxm_ref[plane] = jnp.where(lane_mid == 0, 0.0, cxm)
        label = label_ref[plane]
        offset = label - base
        below = offset < 0
        above = offset >= stride
        group = jnp.where(below, 1, jnp.where(above, 3, 2))
        inner = jnp.where(below, offset + stride, jnp.where(above, offset - stride, offset))
        code = jnp.where(label >= 0, group * B_DEV + inner, sub_ref[plane] - sub_base)
        code_ref[plane] = code & (CODES - 1)
        return (inv, g)

    blank = jnp.zeros((rows, width), f32)
    lax.fori_loop(0, planes, assemble_plane, (blank, blank))

    def backward(step, after):
        plane = planes - 1 - step
        value = (work_ref[plane] + cz_ref[plane + 1] * after) * inv_ref[plane]
        b_ref[plane] = value
        return value

    lax.fori_loop(0, planes, backward, blank)
    cz_ref[0] = jnp.where(first_z, 0.0, cz_ref[0])
    cz_ref[planes] = jnp.where(last_z, 0.0, cz_ref[planes])
    pairs = [
        (code_ref, code_hbm), (r_ref, r_hbm), (b_ref, b_hbm), (cz_ref, cz_hbm), (cyp_ref, cyp_hbm), (cym_ref, cym_hbm),
        (cxp_ref, cxp_hbm), (cxm_ref, cxm_hbm), (diag_ref, diag_hbm), (inv_ref, inv_hbm), (mult_ref, mult_hbm),
    ]
    writes = [pltpu.make_async_copy(a, b, out_sems.at[i]) for i, (a, b) in enumerate(pairs)]
    start_all(writes)
    write_edges(even_z, even_y, b_ref, [ez0_ref.at[0], ez1_ref.at[0]], [ey0_ref.at[0], ey1_ref.at[0]])
    write_edges(
        even_z, even_y, code_ref, [ez0_ref.at[1], ez1_ref.at[1]], [ey0_ref.at[1], ey1_ref.at[1]],
        convert=lambda value: value.astype(f32),
    )
    send_ref[...] = coarse_parts(region_row(r_ref, code_ref), dest_ref)
    wait_all(writes)


def table_rows(parts):
    folded = jnp.sum(parts.reshape(parts.shape[0] // 8, 8, LANES), axis=0)
    even = iota(folded.shape, 0) % 2 == 0
    return jnp.concatenate(
        [
            jnp.sum(jnp.where(even, folded, 0.0), axis=0, keepdims=True),
            jnp.sum(jnp.where(even, 0.0, folded), axis=0, keepdims=True),
        ],
        axis=0,
    )


def scalars_of(sums):
    alphas, betas, curves = [], [None], []
    for step, row in enumerate(sums):
        gamma = lane_of(row, 0)
        if step == 0:
            curve = lane_of(row, 1)
        else:
            beta = gamma / lane_of(sums[step - 1], 0)
            betas.append(beta)
            curve = lane_of(row, 1) + beta * (lane_of(row, 2) + beta * curves[-1])
        curves.append(curve)
        alphas.append(gamma / curve)
    return alphas, betas


def step_kernel(stage, *refs):
    refs = list(refs)

    def take(count):
        out = refs[:count]
        del refs[:count]
        return out

    (edge_ref,) = take(1)
    parts = take(stage + 1)
    halos = [take(4) for _ in range(stage + 1)]
    last = stage == 2
    states = (("b", "r"), ("b", "u0", "r", "w0", "z0"), ("b", "u0", "u1", "r", "w0", "w1", "z0", "z1"))[stage]
    first_names = ("code", "b") + tuple(name for name in states if name[0] == "u")
    later_names = tuple(name for name in states if name not in first_names)
    matrix_names = ("cz", "cyp", "cym", "cxp", "cxm", "diag") + (() if last else ("inv", "mult", "dest"))
    names = first_names + matrix_names[:6] + later_names + matrix_names[6:]
    sources = dict(zip(names, take(len(names))))
    out_names = (("z", "w", "u"), ("z", "w", "u", "bn", "rn"), ("z", "w", "p", "s", "rn"))[stage]
    if not last:
        edges_z, edges_y = take(2), take(2)
    (send_ref,) = take(1)
    sinks = dict(zip(out_names, take(len(out_names))))
    held = dict(zip(names, take(len(names))))
    pad_ref, side_ref = take(2)
    made = {"z": pad_ref.at[pl.ds(1, pad_ref.shape[0] - 2)]}
    for name in out_names[1:]:
        (made[name],) = take(1)
    if not last:
        (work_ref,) = take(1)
    in_sems, out_sems = take(2)

    reads = {name: pltpu.make_async_copy(sources[name], held[name], in_sems.at[i]) for i, name in enumerate(names)}
    start_all(reads.values())
    writes = {name: pltpu.make_async_copy(made[name], sinks[name], out_sems.at[i]) for i, name in enumerate(out_names)}
    code_ref = held["code"]
    planes, rows, width = code_ref.shape
    even_z, even_y = edge_ref[7] == 0, edge_ref[8] == 0

    sums = [table_rows(part[...]) for part in parts]
    alphas, betas = scalars_of([row[0:1] for row in sums[1:]])
    table = sums[0]
    if stage >= 1:
        table = table - alphas[0] * sums[1]
    if stage == 2:
        table = table - alphas[1] * (sums[2] + betas[1] * sums[1])
    near, side = table[0:1], table[1:2]

    def combine(values):
        out = values[0]
        if stage >= 1:
            out = out - alphas[0] * values[1]
        if stage == 2:
            out = out - alphas[1] * (values[2] + betas[1] * values[1])
        return out

    for slot in range(2):
        upper = even_z if slot == 0 else jnp.logical_not(even_z)
        index = halos[0][slot][1].astype(i32)
        high = jnp.where(index < B_DEV, index + S_DEV, index + B_DEV)
        low = jnp.where(
            index < B_DEV, index + 2 * S_DEV, jnp.where(index < 2 * B_DEV, index + 4 * B_DEV, index - B_DEV)
        )
        block = combine([halos[0][slot][0]] + [halo[slot][...] for halo in halos[1:]])
        pad_ref[jnp.where(upper, planes + 1, 0)] = block + lookup(near, jnp.where(upper, high, low))
        upper = even_y if slot == 0 else jnp.logical_not(even_y)
        index = halos[0][2 + slot][1].astype(i32)
        block = combine([halos[0][2 + slot][0]] + [halo[2 + slot][...] for halo in halos[1:]])
        found = jnp.where(
            upper, lookup(near, (index & (B_DEV - 1)) + 3 * S_DEV), lookup(side, index)
        )
        side_ref[jnp.where(upper, 1, 0)] = block + found

    for name in first_names:
        reads[name].wait()

    def direction(plane, carry):
        block = held["b"][plane]
        if stage == 1:
            block = block - alphas[0] * held["u0"][plane]
            made["bn"][plane] = block
        if stage == 2:
            block = block - alphas[1] * (held["u1"][plane] + betas[1] * held["u0"][plane])
        pad_ref[plane + 1] = block + lookup(near, code_ref[plane])
        return carry

    lax.fori_loop(0, planes, direction, 0)
    writes["z"].start()
    for name in names:
        if name not in first_names and name != "dest":
            reads[name].wait()
    row = iota((rows, width), 0)

    def image_plane(plane, carry):
        sums, before = carry
        here = pad_ref[plane + 1]
        north = jnp.where(row == rows - 1, side_ref[1, pl.ds(plane, 1), :], up_rows(here))
        south = jnp.where(row == 0, side_ref[0, pl.ds(plane, 1), :], down_rows(here))
        image = held["diag"][plane] * here - (
            held["cz"][plane + 1] * pad_ref[plane + 2]
            + held["cz"][plane] * pad_ref[plane]
            + held["cyp"][plane] * north
            + held["cym"][plane] * south
            + held["cxp"][plane] * next_x(here)
            + held["cxm"][plane] * prev_x(here)
        )
        made["w"][plane] = image
        residual = held["r"][plane]
        if stage == 1:
            old_z, old_w = held["z0"][plane], held["w0"][plane]
            residual = residual - alphas[0] * old_w
            made["rn"][plane] = residual
        if stage == 2:
            old_z = held["z1"][plane] + betas[1] * held["z0"][plane]
            old_w = held["w1"][plane] + betas[1] * held["w0"][plane]
            made["p"][plane] = old_z
            made["s"][plane] = old_w
            residual = residual - alphas[1] * old_w
            made["rn"][plane] = residual
        found = [total(residual * here), total(here * image)]
        if stage >= 1:
            found.append(total(here * old_w + old_z * image))
        if not last:
            before = image + held["mult"][plane] * before
            work_ref[plane] = before
        return tuple(old + new for old, new in zip(sums, found)), before

    blank = jnp.zeros((8, LANES), f32)
    empty = jnp.zeros((rows, width), f32)
    dots, _ = lax.fori_loop(
        0, planes, image_plane, ((blank,) * (3 if stage else 2), blank if last else empty)
    )
    for name in out_names[1:]:
        if name != "u":
            writes[name].start()
    row = scalar_row([jnp.sum(value) for value in dots])
    if last:
        send_ref[...] = jnp.broadcast_to(row, send_ref.shape)
    else:

        def backward(step, after):
            plane = planes - 1 - step
            value = (work_ref[plane] + held["cz"][plane + 1] * after) * held["inv"][plane]
            made["u"][plane] = value
            return value

        lax.fori_loop(0, planes, backward, empty)
        writes["u"].start()
        write_edges(even_z, even_y, made["u"], edges_z, edges_y)
        reads["dest"].wait()
        parts = coarse_parts(region_row(made["w"], code_ref), held["dest"])
        send_ref[...] = parts + jnp.where(iota(parts.shape, 0) % 2 == 0, row, 0.0)
    wait_all(writes.values())


def final_kernel(
    d0_ref, d1_ref, d2_ref, r_hbm, w_hbm, s_hbm, z0_hbm, p_hbm, z_hbm, x_out, r_out,
    r_ref, w_ref, s_ref, z0_ref, p_ref, z_ref, x_ref, in_sems, out_sems,
):
    pairs = [(z0_hbm, z0_ref), (p_hbm, p_ref), (z_hbm, z_ref), (r_hbm, r_ref), (w_hbm, w_ref), (s_hbm, s_ref)]
    reads = [pltpu.make_async_copy(a, b, in_sems.at[i]) for i, (a, b) in enumerate(pairs)]
    start_all(reads)
    sums = [table_rows(d0_ref[...])[0:1], table_rows(d1_ref[...])[0:1], jnp.sum(d2_ref[...], axis=0, keepdims=True)]
    alphas, betas = scalars_of(sums)
    mixed = alphas[2] * betas[2]
    along = alphas[1] + mixed
    wait_all(reads[:3])
    x_ref[...] = alphas[0] * z0_ref[...] + along * p_ref[...] + alphas[2] * z_ref[...]
    x_write = pltpu.make_async_copy(x_ref, x_out, out_sems.at[0])
    x_write.start()
    wait_all(reads[3:])
    r_ref[...] = r_ref[...] - (alphas[2] * w_ref[...] + mixed * s_ref[...])
    r_write = pltpu.make_async_copy(r_ref, r_out, out_sems.at[1])
    r_write.start()
    x_write.wait()
    r_write.wait()


def call(kernel, outs, scratch, args, name):
    spaces = {"smem": pltpu.SMEM, "vmem": pltpu.VMEM, "hbm": pltpu.HBM}

    def specs(items):
        return [pl.BlockSpec(memory_space=spaces[space]) for space, _ in items]

    held = sum(4 * math.prod(ref.shape) for ref in scratch)
    made = [pltpu.HBM(out.shape, out.dtype) if space == "hbm" else out for space, out in outs]
    operands = [
        pltpu.with_memory_space_constraint(value, pltpu.HBM) if space == "hbm" else value for space, value in args
    ]
    return pl.pallas_call(
        kernel,
        out_shape=made,
        in_specs=specs(args),
        out_specs=specs(outs),
        scratch_shapes=scratch,
        compiler_params=pltpu.CompilerParams(vmem_limit_bytes=held + 12 * 1024 * 1024),
        name=name,
    )(*operands)


def swaps(axis, first):
    count = lax.axis_size(axis)
    pairs = []
    for i in range(first, count + first, 2):
        low, high = i % count, (i + 1) % count
        pairs += [(low, high), (high, low)]
    return pairs


def swap(block, axis, first):
    return lax.ppermute(block, axis, swaps(axis, first))


def on_device(fraction, source, bubble_label, subdomain, coarse_inverse):
    planes, rows, width = fraction.shape
    slabs = lax.axis_size("gz")
    columns = lax.axis_size("gy")
    devices = slabs * columns
    slab = lax.axis_index("gz")
    column = lax.axis_index("gy")
    here = slab * columns + column
    even_z = slab % 2 == 0
    even_y = column % 2 == 0
    field = jax.ShapeDtypeStruct((planes, rows, width), f32)

    def shape(*dims, dtype=f32):
        return jax.ShapeDtypeStruct(dims, dtype)

    def vmem(*dims, dtype=f32):
        return pltpu.VMEM(dims, dtype)

    def like(items):
        return [vmem(*value.shape, dtype=value.dtype) for value in items]

    def semaphores(count):
        return pltpu.SemaphoreType.DMA((count,))

    def tag(space, items):
        return [(space, item) for item in items]

    edge = jnp.stack(
        [
            (slab == 0).astype(i32),
            (slab == slabs - 1).astype(i32),
            (column == 0).astype(i32),
            (column == columns - 1).astype(i32),
            here * B_DEV,
            jnp.int32(columns * B_DEV),
            here * S_DEV,
            slab % 2,
            column % 2,
        ]
    )

    top, bottom, *sides, bubbles = call(
        slices_kernel,
        tag("vmem", [shape(DEPTH, rows, width)] * 2 + [shape(planes, DEPTH, width)] * 2 + [shape(B_DEV, devices * SPAN)]),
        [vmem(planes, rows, width), vmem(SPAN, devices * SPAN), semaphores(2)],
        tag("smem", [edge]) + tag("hbm", [fraction, coarse_inverse]),
        "slices",
    )
    coarse_in = [swap(bubbles, "gz", 0), swap(bubbles, "gz", 1)]
    y_in = [swap(sides[0], "gy", 0), swap(sides[1], "gy", 1)]
    z_in = [swap(top, "gz", 0), swap(bottom, "gz", 1)]
    corner = jnp.stack(y_in)
    corner_top = jnp.where(even_z, corner[:, planes - DEPTH :], corner[:, :DEPTH])
    corner_bottom = jnp.where(even_z, corner[:, :DEPTH], corner[:, planes - DEPTH :])
    corner_in = [swap(corner_top, "gz", 0), swap(corner_bottom, "gz", 1)]

    def spread(matrix):
        return matrix.reshape(matrix.shape[0], devices, SPAN)

    dest_shape = shape(REGIONS, 2 * devices, LANES)
    (dest,) = call(
        partial(destinations_kernel, columns),
        tag("hbm", [dest_shape]),
        [vmem(REGIONS, devices, LANES)] + like([dest_shape]) + [semaphores(1)],
        tag("smem", [(slab % 2).reshape(1)]) + tag("vmem", [spread(coarse_inverse)] + [spread(m) for m in coarse_in]),
        "destinations",
    )
    codes = shape(planes, rows, width, dtype=i32)
    faces = shape(planes + 1, rows, width)
    inputs = [fraction, source, bubble_label, subdomain, dest]
    made = [codes, field, field, faces] + [field] * 7
    tall = rows + 8
    wide = shape(2 * devices, LANES)
    first_edges = [shape(2, rows, width)] * 2 + [shape(2, planes, width)] * 2
    later_edges = [shape(rows, width)] * 2 + [shape(planes, width)] * 2
    *sent, send, code, r0, b0, cz, cyp, cym, cxp, cxm, diag, inv, mult = call(
        setup_kernel,
        tag("vmem", first_edges + [wide]) + tag("hbm", made),
        like(inputs)
        + like(made)
        + [
            vmem(planes + 2 * DEPTH, tall, width),
            vmem(planes + 4, tall, width),
            vmem(planes + 4, tall, width),
            vmem(planes + 2, tall, width),
            vmem(planes + 1, rows, width),
            vmem(planes, rows, width),
            semaphores(len(inputs)),
            semaphores(len(made)),
        ],
        tag("smem", [edge]) + tag("vmem", z_in + y_in + corner_in) + tag("hbm", inputs),
        "setup",
    )

    def exchange(parts):
        blocks = parts.reshape(devices, -1, LANES)
        return lax.all_to_all(blocks, ("gz", "gy"), 0, 0).reshape(parts.shape)

    def halos(sent):
        return [swap(sent[0], "gz", 0), swap(sent[1], "gz", 1), swap(sent[2], "gy", 0), swap(sent[3], "gy", 1)]

    def step(stage, parts, edges, first, later):
        last = stage == 2
        matrix = [cz, cyp, cym, cxp, cxm, diag]
        operands = [code] + first + matrix + later + ([] if last else [inv, mult, dest])
        outs = [field] * (3, 5, 5)[stage]
        ends = [] if last else later_edges
        scratch = like(operands) + [vmem(planes + 2, rows, width), vmem(2, planes, width)] + like(outs[1:])
        if not last:
            scratch.append(vmem(planes, rows, width))
        scratch += [semaphores(len(operands)), semaphores(len(outs))]
        results = call(
            partial(step_kernel, stage),
            tag("vmem", ends + [shape(devices, LANES) if last else wide]) + tag("hbm", outs),
            scratch,
            tag("smem", [edge]) + tag("vmem", parts + edges) + tag("hbm", operands),
            f"step{stage}",
        )
        return results[: len(ends)], results[len(ends)], results[len(ends) + 1 :]

    edges = halos(sent)
    parts = [exchange(send)]
    sent, send, (z0, w0, u0) = step(0, parts, edges, [b0], [r0])
    edges = edges + halos(sent)
    parts = parts + [exchange(send)]
    sent, send, (z1, w1, u1, b1, r1) = step(1, parts, edges, [b0, u0], [r0, w0, z0])
    edges = edges + halos(sent)
    parts = parts + [exchange(send)]
    _, send, (z2, w2, p1, s1, r2) = step(2, parts, edges, [b1, u0, u1], [r1, w0, w1, z0, z1])
    parts = parts + [exchange(send)]
    return tuple(
        call(
            final_kernel,
            tag("hbm", [field, field]),
            like([field] * 7) + [semaphores(6), semaphores(2)],
            tag("vmem", parts[1:]) + tag("hbm", [r2, w2, s1, z0, p1, z2]),
            "finish",
        )
    )


def solution(mesh):
    placed = (
        P("gz", "gy", None),
        P("gz", "gy", None),
        P("gz", "gy", None),
        P("gz", "gy", None),
        P(("gz", "gy"), None),
    )
    return jax.shard_map(
        on_device,
        mesh=mesh,
        in_specs=placed,
        out_specs=(P("gz", "gy", None), P("gz", "gy", None)),
        check_vma=False,
    )
```

```python
import math
from functools import partial

import jax
import jax.numpy as jnp
from jax import lax
from jax.experimental import pallas as pl
from jax.experimental.pallas import tpu as pltpu
from jax.sharding import PartitionSpec as P


S_DEV = 4
B_DEV = 16
SPAN = S_DEV + B_DEV
LANES = 128
GROUPS = 4
CODES = GROUPS * B_DEV
REGIONS = S_DEV + 3 * B_DEV
SCALARS = 96
DEPTH = 3
PIECE = 16

surface_tension = 0.5
shift_term = 0.05
gas_drop = 0.75
norm_floor = 0.25
highest = lax.Precision.HIGHEST
f32 = jnp.float32
i32 = jnp.int32
i8 = jnp.int8
bf16 = jnp.bfloat16


def iota(shape, dim):
    return lax.broadcasted_iota(i32, shape, dim)


def up_rows(field):
    return pltpu.roll(field, field.shape[0] - 1, 0)


def down_rows(field):
    return pltpu.roll(field, 1, 0)


def next_x(field):
    return pltpu.roll(field, field.shape[1] - 1, 1)


def prev_x(field):
    return pltpu.roll(field, 1, 1)


def total(field):
    rows, width = field.shape
    folded = field[:, :LANES]
    for start in range(LANES, width, LANES):
        folded = folded + field[:, start : start + LANES]
    return jnp.sum(folded.reshape(rows // 8, 8, LANES), axis=0)


def piece_sums(values, code):
    group = (code // B_DEV).astype(f32).astype(bf16)
    inner = (code % B_DEV).astype(f32).astype(bf16)
    high = values.astype(bf16)
    low = (values - high.astype(f32)).astype(bf16)
    zero, one = jnp.zeros_like(high), jnp.ones_like(high)
    left = [jnp.where(group == g, part, zero) for part in (high, low) for g in range(GROUPS)]
    right = [jnp.where(inner == i, one, zero) for i in range(B_DEV)]
    return lax.dot_general(
        jnp.concatenate(left, axis=0),
        jnp.concatenate(right, axis=0),
        (((1,), (1,)), ((), ())),
        preferred_element_type=f32,
    )


def region_row(value_ref, code_ref):
    planes, rows, _ = value_ref.shape

    def step(plane, acc):
        code = code_ref[plane].astype(i32)
        for start in range(0, rows, PIECE):
            acc = acc + piece_sums(value_ref[plane, start : start + PIECE, :], code[start : start + PIECE])
        return acc

    acc = lax.fori_loop(
        0, planes, step, jnp.zeros((2 * GROUPS * PIECE, B_DEV * PIECE), f32), unroll=planes
    )
    shape = acc.shape
    kept = jnp.where(iota(shape, 0) % PIECE == iota(shape, 1) % PIECE, acc, 0.0)
    folded = jnp.sum(kept.reshape(2 * GROUPS, PIECE, shape[1]), axis=1)
    shape = (shape[1], LANES)
    pick = jnp.where(iota(shape, 0) // PIECE == iota(shape, 1) % B_DEV, 1.0, 0.0)
    spread = jnp.dot(folded, pick, precision=highest, preferred_element_type=f32)
    shape = spread.shape
    lane = iota(shape, 1)
    mine = (iota(shape, 0) % GROUPS == lane // B_DEV) & (lane < CODES)
    return jnp.sum(jnp.where(mine, spread, 0.0), axis=0, keepdims=True)


def scalar_row(scalars):
    lane = iota((1, LANES), 1)
    row = jnp.zeros((1, LANES), f32)
    for index, value in enumerate(scalars):
        row = jnp.where(lane == SCALARS + index, value, row)
    return row


def lane_of(row, index):
    return jnp.sum(jnp.where(iota(row.shape, 1) == SCALARS + index, row, 0.0))


def lookup(table, index):
    rows, width = index.shape
    wide = jnp.broadcast_to(table, (rows, LANES))
    return jnp.concatenate(
        [
            jnp.take_along_axis(wide, index[:, start : start + LANES], axis=1)
            for start in range(0, width, LANES)
        ],
        axis=1,
    )


def start_all(copies):
    for copy in copies:
        copy.start()


def wait_all(copies):
    for copy in copies:
        copy.wait()


def coarse_parts(row, dest_ref):
    wide = jnp.broadcast_to(row, (8, LANES))

    def step(region, acc):
        lane = jnp.where(region < S_DEV, region, region + B_DEV - S_DEV)
        factor = jnp.take_along_axis(wide, jnp.full((8, LANES), lane, i32), axis=1)[0:1, :]
        return acc + factor * dest_ref[region]

    return lax.fori_loop(0, REGIONS, step, jnp.zeros(dest_ref.shape[1:], f32), unroll=4)


def destinations_kernel(columns, pair_ref, own_ref, near_ref, far_ref, dest_hbm, wide_ref, dest_ref, sems):
    devices = own_ref.shape[1]
    even_z = pair_ref[0] == 0
    wide_ref[...] = jnp.zeros(wide_ref.shape, f32)
    low_start = pl.multiple_of(jnp.where(even_z, 2 * B_DEV, 0), B_DEV) + S_DEV
    high_start = pl.multiple_of(jnp.where(even_z, 0, 2 * B_DEV), B_DEV) + S_DEV
    wide_ref[0:S_DEV, :, 0:SPAN] = own_ref[0:S_DEV]
    wide_ref[S_DEV + B_DEV : S_DEV + 2 * B_DEV, :, 0:SPAN] = own_ref[S_DEV:SPAN]
    wide_ref[pl.ds(low_start, B_DEV), :, 0:SPAN] = near_ref[...]
    wide_ref[pl.ds(high_start, B_DEV), :, 0:SPAN] = far_ref[...]
    lane = iota((devices, LANES), 1)

    def place(base, shift, first, count):
        moved = pltpu.roll(base, shift, 1) if shift else base
        return jnp.where((lane >= first) & (lane < first + count), moved, 0.0)

    def from_device(field, step):
        return pltpu.roll(field, (-step) % devices, 0) if step % devices else field

    def one(region, carry):
        base = wide_ref[region]
        bubbles = B_DEV - S_DEV
        table = place(base, 0, 0, S_DEV) + place(base, B_DEV + bubbles, 2 * B_DEV, B_DEV)
        table = table + from_device(
            place(base, S_DEV, S_DEV, S_DEV) + place(base, 2 * B_DEV + bubbles, 3 * B_DEV, B_DEV), columns
        )
        table = table + from_device(
            place(base, 2 * S_DEV, 2 * S_DEV, S_DEV) + place(base, bubbles, B_DEV, B_DEV), -columns
        )
        table = table + from_device(place(base, 3 * S_DEV, 3 * S_DEV, S_DEV), 1)
        table = table + from_device(place(base, 3 * B_DEV + bubbles, 4 * B_DEV, B_DEV), 2 * columns)
        table = table + from_device(place(base, 4 * B_DEV + bubbles, 5 * B_DEV, B_DEV), -2 * columns)
        own_codes = jnp.where((lane < S_DEV) | ((lane >= B_DEV) & (lane < CODES)), table, 0.0)
        dest_ref[region, pl.ds(0, devices, stride=2), :] = table
        dest_ref[region, pl.ds(1, devices, stride=2), :] = from_device(own_codes, -1)
        return carry

    lax.fori_loop(0, REGIONS, one, 0, unroll=4)
    write = pltpu.make_async_copy(dest_ref, dest_hbm, sems.at[0])
    write.start()
    write.wait()


def write_edges(even_z, even_y, value_ref, z_refs, y_refs, convert=lambda value: value):
    planes, rows, _ = value_ref.shape
    z_refs[0][...] = convert(value_ref[jnp.where(even_z, planes - 1, 0)])
    z_refs[1][...] = convert(value_ref[jnp.where(even_z, 0, planes - 1)])
    for plane in range(planes):
        first = convert(value_ref[plane, 0:1, :])
        last = convert(value_ref[plane, rows - 1 : rows, :])
        y_refs[0][plane : plane + 1, :] = jnp.where(even_y, last, first)
        y_refs[1][plane : plane + 1, :] = jnp.where(even_y, first, last)


def slices_kernel(edge_ref, frac_hbm, coarse_hbm, z0_ref, z1_ref, y0_ref, y1_ref, bubble_ref, frac_ref, coarse_ref, sems):
    planes, rows, _ = frac_ref.shape
    copies = [
        pltpu.make_async_copy(frac_hbm, frac_ref, sems.at[0]),
        pltpu.make_async_copy(coarse_hbm, coarse_ref, sems.at[1]),
    ]
    start_all(copies)
    even_z, even_y = edge_ref[7] == 0, edge_ref[8] == 0
    wait_all(copies)
    bubble_ref[...] = coarse_ref[S_DEV:SPAN, :]
    z0_ref[...] = frac_ref[pl.ds(jnp.where(even_z, planes - DEPTH, 0), DEPTH)]
    z1_ref[...] = frac_ref[pl.ds(jnp.where(even_z, 0, planes - DEPTH), DEPTH)]
    first, last = frac_ref[:, 0:DEPTH, :], frac_ref[:, rows - DEPTH : rows, :]
    y0_ref[...] = jnp.where(even_y, last, first)
    y1_ref[...] = jnp.where(even_y, first, last)


def setup_kernel(
    edge_ref, z0_in, z1_in, y0_in, y1_in, k0_in, k1_in, frac_hbm, source_hbm, label_hbm, sub_hbm, dest_hbm,
    ez0_ref, ez1_ref, ey0_ref, ey1_ref, send_ref,
    code_ref, cz_ref, cy_ref, cx_ref, inv_ref, south_ref, r_hbm, diag_hbm,
    frac_ref, source_ref, label_ref, sub_ref, dest_ref, r_ref, diag_ref, b_ref,
    deep_ref, nz_ref, flat_ref, kap_ref, fz_ref, work_ref, in_sems, out_sems,
):
    planes, rows, width = frac_ref.shape
    tall = rows + 8
    first_z, last_z, first_y, last_y = (edge_ref[i] == 1 for i in range(4))
    base, stride, sub_base = edge_ref[4], edge_ref[5], edge_ref[6]
    even_z, even_y = edge_ref[7] == 0, edge_ref[8] == 0
    pairs = [(frac_hbm, frac_ref), (label_hbm, label_ref), (sub_hbm, sub_ref), (source_hbm, source_ref), (dest_hbm, dest_ref)]
    reads = [pltpu.make_async_copy(a, b, in_sems.at[i]) for i, (a, b) in enumerate(pairs)]
    start_all(reads)
    row = iota((tall, width), 0)
    lane = iota((tall, width), 1)
    inside_y = ((row < rows) | ((row < rows + 4) & jnp.logical_not(last_y))) | (
        (row >= rows + 4) & jnp.logical_not(first_y)
    )
    first_plane = jnp.where(first_z, 0, -planes)
    last_plane = jnp.where(last_z, planes, 2 * planes)

    def right_of(field):
        return jnp.where(lane[: field.shape[0]] == width - 1, 0.0, next_x(field))

    def left_of(field):
        return jnp.where(lane[: field.shape[0]] == 0, 0.0, prev_x(field))

    deep_ref[:, rows:tall, :] = jnp.zeros((planes + 2 * DEPTH, 8, width), f32)
    near_z = jnp.where(even_z, planes + DEPTH, 0)
    far_z = jnp.where(even_z, 0, planes + DEPTH)
    deep_ref[pl.ds(near_z, DEPTH), 0:rows, :] = z0_in[...]
    deep_ref[pl.ds(far_z, DEPTH), 0:rows, :] = z1_in[...]
    high, low = slice(rows, rows + DEPTH), slice(tall - DEPTH, tall)

    def fill_rows(first, second):
        deep_ref[DEPTH : planes + DEPTH, first, :] = y0_in[...]
        deep_ref[DEPTH : planes + DEPTH, second, :] = y1_in[...]
        deep_ref[pl.ds(near_z, DEPTH), first, :] = k0_in[0]
        deep_ref[pl.ds(near_z, DEPTH), second, :] = k0_in[1]
        deep_ref[pl.ds(far_z, DEPTH), first, :] = k1_in[0]
        deep_ref[pl.ds(far_z, DEPTH), second, :] = k1_in[1]

    @pl.when(even_y)
    def _():
        fill_rows(high, low)

    @pl.when(jnp.logical_not(even_y))
    def _():
        fill_rows(low, high)

    reads[0].wait()
    deep_ref[DEPTH : planes + DEPTH, 0:rows, :] = frac_ref[...]

    def mask_plane(index, carry):
        keep = (index - DEPTH >= first_plane) & (index - DEPTH < last_plane)
        deep_ref[index] = jnp.where(inside_y & keep, deep_ref[index], 0.0)
        return carry

    lax.fori_loop(0, planes + 2 * DEPTH, mask_plane, 0)

    def normal_plane(index, carry):
        keep = (index - 2 >= first_plane) & (index - 2 < last_plane)
        here = deep_ref[index + 1]
        gz = 0.5 * (deep_ref[index + 2] - deep_ref[index])
        gy = 0.5 * (up_rows(here) - down_rows(here))
        gx = 0.5 * (right_of(here) - left_of(here))
        scale = jnp.minimum(lax.rsqrt(gz * gz + gy * gy + gx * gx), 1.0 / norm_floor)
        scale = jnp.where(inside_y & keep, scale, 0.0)
        ny = gy * scale
        nx = gx * scale
        nz_ref[index] = gz * scale
        flat_ref[index] = 0.5 * (up_rows(ny) - down_rows(ny)) + 0.5 * (right_of(nx) - left_of(nx))
        return carry

    lax.fori_loop(0, planes + 4, normal_plane, 0)

    def kappa_plane(index, carry):
        keep = (index - 1 >= first_plane) & (index - 1 < last_plane)
        value = -(0.5 * (nz_ref[index + 2] - nz_ref[index]) + flat_ref[index + 1])
        kap_ref[index] = jnp.where(inside_y & keep, value, 0.0)
        return carry

    lax.fori_loop(0, planes + 2, kappa_plane, 0)
    mid = pl.ds(0, rows)

    def z_face(index, carry):
        f_low = deep_ref[index + 2, mid, :]
        f_high = deep_ref[index + 3, mid, :]
        coef = 2.0 / ((1.0 - gas_drop * f_low) + (1.0 - gas_drop * f_high))
        cz_ref[index] = coef
        mean = 0.5 * (kap_ref[index, mid, :] + kap_ref[index + 1, mid, :])
        fz_ref[index] = coef * mean * (f_high - f_low)
        return carry

    lax.fori_loop(0, planes + 1, z_face, 0)
    row_mid = row[:rows]
    lane_mid = lane[:rows]
    wait_all(reads[1:])

    def assemble_plane(plane, carry):
        inv_before, g_before = carry
        f = deep_ref[plane + 3]
        k = kap_ref[plane + 1]
        d = 1.0 - gas_drop * f
        f_up = up_rows(f)
        cy = 2.0 / (d + (1.0 - gas_drop * f_up))
        fy = cy * (0.5 * (k + up_rows(k))) * (f_up - f)
        cyp, cym = cy[:rows], down_rows(cy)[:rows]
        sum_y = fy[:rows] - down_rows(fy)[:rows]
        f, k, d = f[:rows], k[:rows], d[:rows]
        f_right = right_of(f)
        cxp = 2.0 / (d + (1.0 - gas_drop * f_right))
        fx = cxp * (0.5 * (k + right_of(k))) * (f_right - f)
        outer = jnp.concatenate([2.0 / (d[:, :LANES] + 1.0), jnp.zeros((rows, width - LANES), f32)], axis=1)
        cxm = jnp.where(lane_mid == 0, outer, prev_x(cxp))
        fx_before = jnp.where(lane_mid == 0, outer * (0.5 * k) * f, prev_x(fx))
        terms = fz_ref[plane + 1] - fz_ref[plane] + sum_y + (fx - fx_before)
        rhs = source_ref[plane] - surface_tension * terms
        down = cz_ref[plane]
        diagonal = shift_term + (cz_ref[plane + 1] + down + cyp + cym + cxp + cxm)
        mult = down * inv_before
        inv = 1.0 / (diagonal - mult * down)
        g = rhs + mult * g_before
        r_ref[plane] = rhs
        diag_ref[plane] = diagonal
        inv_ref[plane] = inv
        work_ref[plane] = g
        cy_ref[plane] = jnp.where((row_mid == rows - 1) & last_y, 0.0, cyp)
        south_ref[pl.ds(plane, 1), :] = jnp.where(first_y, 0.0, cym[0:1, :])
        cx_ref[plane] = jnp.where(lane_mid == width - 1, 0.0, cxp)
        label = label_ref[plane]
        offset = label - base
        below = offset < 0
        above = offset >= stride
        group = jnp.where(below, 1, jnp.where(above, 3, 2))
        inner = jnp.where(below, offset + stride, jnp.where(above, offset - stride, offset))
        code = jnp.where(label >= 0, group * B_DEV + inner, sub_ref[plane] - sub_base)
        code_ref[plane] = (code & (CODES - 1)).astype(i8)
        return (inv, g)

    blank = jnp.zeros((rows, width), f32)
    lax.fori_loop(0, planes, assemble_plane, (blank, blank))

    def backward(step, after):
        plane = planes - 1 - step
        value = (work_ref[plane] + cz_ref[plane + 1] * after) * inv_ref[plane]
        b_ref[plane] = value
        return value

    lax.fori_loop(0, planes, backward, blank)
    cz_ref[0] = jnp.where(first_z, 0.0, cz_ref[0])
    cz_ref[planes] = jnp.where(last_z, 0.0, cz_ref[planes])
    writes = [
        pltpu.make_async_copy(r_ref, r_hbm, out_sems.at[0]), pltpu.make_async_copy(diag_ref, diag_hbm, out_sems.at[1])
    ]
    start_all(writes)
    write_edges(even_z, even_y, b_ref, [ez0_ref.at[0], ez1_ref.at[0]], [ey0_ref.at[0], ey1_ref.at[0]])
    for plane in range(planes):
        label_ref[plane] = code_ref[plane].astype(i32)
    write_edges(
        even_z, even_y, label_ref, [ez0_ref.at[1], ez1_ref.at[1]], [ey0_ref.at[1], ey1_ref.at[1]],
        convert=lambda value: value.astype(f32),
    )
    send_ref[...] = coarse_parts(region_row(r_ref, code_ref), dest_ref)
    wait_all(writes)


def table_rows(parts):
    folded = jnp.sum(parts.reshape(parts.shape[0] // 8, 8, LANES), axis=0)
    even = iota(folded.shape, 0) % 2 == 0
    return jnp.concatenate(
        [
            jnp.sum(jnp.where(even, folded, 0.0), axis=0, keepdims=True),
            jnp.sum(jnp.where(even, 0.0, folded), axis=0, keepdims=True),
        ],
        axis=0,
    )


def scalars_of(sums):
    alphas, betas, curves = [], [None], []
    for step, row in enumerate(sums):
        gamma = lane_of(row, 0)
        if step == 0:
            curve = lane_of(row, 1)
        else:
            beta = gamma / lane_of(sums[step - 1], 0)
            betas.append(beta)
            curve = lane_of(row, 1) + beta * (lane_of(row, 2) + beta * curves[-1])
        curves.append(curve)
        alphas.append(gamma / curve)
    return alphas, betas


def step_kernel(stage, *refs):
    refs = list(refs)

    def take(count):
        out = refs[:count]
        del refs[:count]
        return out

    (edge_ref,) = take(1)
    parts = take(stage + 1)
    halos = [take(4) for _ in range(stage + 1)]
    code_ref, cz_ref, cy_ref, cx_ref, inv_ref, south_ref = take(6)
    last = stage == 2
    names = (("r",), ("r", "w0", "z0"), ("r", "w1", "w0", "z1", "z0"))[stage] + (("diag",) if last else ("diag", "dest"))
    sources = dict(zip(names, take(len(names))))
    out_names = (("z", "w"), ("rn", "z", "w"), ("rn", "s", "p", "z", "w"))[stage]
    if not last:
        edges_z, edges_y = take(2), take(2)
    (send_ref,) = take(1)
    sinks = dict(zip(out_names, take(len(out_names))))
    held = dict(zip(names, take(len(names))))
    pad_ref, side_ref, work_ref, w_ref = take(4)
    made = {"z": pad_ref.at[pl.ds(1, pad_ref.shape[0] - 2)], "w": w_ref}
    for name in out_names[:-2]:
        (made[name],) = take(1)
    if not last:
        (u_ref,) = take(1)
    in_sems, out_sems = take(2)

    reads = {name: pltpu.make_async_copy(sources[name], held[name], in_sems.at[i]) for i, name in enumerate(names)}
    start_all(reads.values())
    writes = {name: pltpu.make_async_copy(made[name], sinks[name], out_sems.at[i]) for i, name in enumerate(out_names)}
    planes, rows, width = code_ref.shape
    even_z, even_y = edge_ref[7] == 0, edge_ref[8] == 0

    sums = [table_rows(part[...]) for part in parts]
    alphas, betas = scalars_of([row[0:1] for row in sums[1:]])
    table = sums[0]
    if stage >= 1:
        table = table - alphas[0] * sums[1]
    if stage == 2:
        table = table - alphas[1] * (sums[2] + betas[1] * sums[1])
    near, side = table[0:1], table[1:2]

    def combine(values):
        out = values[0]
        if stage >= 1:
            out = out - alphas[0] * values[1]
        if stage == 2:
            out = out - alphas[1] * (values[2] + betas[1] * values[1])
        return out

    for slot in range(2):
        upper = even_z if slot == 0 else jnp.logical_not(even_z)
        index = halos[0][slot][1].astype(i32)
        high = jnp.where(index < B_DEV, index + S_DEV, index + B_DEV)
        low = jnp.where(
            index < B_DEV, index + 2 * S_DEV, jnp.where(index < 2 * B_DEV, index + 4 * B_DEV, index - B_DEV)
        )
        block = combine([halos[0][slot][0]] + [halo[slot][...] for halo in halos[1:]])
        pad_ref[jnp.where(upper, planes + 1, 0)] = block + lookup(near, jnp.where(upper, high, low))
        upper = even_y if slot == 0 else jnp.logical_not(even_y)
        index = halos[0][2 + slot][1].astype(i32)
        block = combine([halos[0][2 + slot][0]] + [halo[2 + slot][...] for halo in halos[1:]])
        found = jnp.where(
            upper, lookup(near, (index & (B_DEV - 1)) + 3 * S_DEV), lookup(side, index)
        )
        side_ref[jnp.where(upper, 1, 0)] = block + found

    for name in names:
        if name not in ("diag", "dest"):
            reads[name].wait()
    empty = jnp.zeros((rows, width), f32)

    def residual(plane, before):
        value = held["r"][plane]
        if stage == 1:
            value = value - alphas[0] * held["w0"][plane]
            made["rn"][plane] = value
        if stage == 2:
            image = held["w1"][plane] + betas[1] * held["w0"][plane]
            made["s"][plane] = image
            made["p"][plane] = held["z1"][plane] + betas[1] * held["z0"][plane]
            value = value - alphas[1] * image
            made["rn"][plane] = value
        value = value + cz_ref[plane] * before
        work_ref[plane] = value
        return value * inv_ref[plane]

    lax.fori_loop(0, planes, residual, empty)
    for name in out_names[:-2]:
        writes[name].start()

    def direction(step, after):
        plane = planes - 1 - step
        value = (work_ref[plane] + cz_ref[plane + 1] * after) * inv_ref[plane]
        pad_ref[plane + 1] = value + lookup(near, code_ref[plane].astype(i32))
        return value

    lax.fori_loop(0, planes, direction, empty)
    writes["z"].start()
    reads["diag"].wait()
    row = iota((rows, width), 0)

    def image_plane(plane, carry):
        sums, before = carry
        here = pad_ref[plane + 1]
        cy, cx = cy_ref[plane], cx_ref[plane]
        north = jnp.where(row == rows - 1, side_ref[1, pl.ds(plane, 1), :], up_rows(here))
        below = south_ref[pl.ds(plane, 1), :] * side_ref[0, pl.ds(plane, 1), :]
        south = jnp.where(row == 0, below, down_rows(cy * here))
        image = held["diag"][plane] * here - (
            cz_ref[plane + 1] * pad_ref[plane + 2]
            + cz_ref[plane] * pad_ref[plane]
            + (cy * north + south)
            + (cx * next_x(here) + prev_x(cx * here))
        )
        w_ref[plane] = image
        new = made["rn"] if stage else held["r"]
        found = [total(new[plane] * here), total(here * image)]
        if stage == 1:
            found.append(total(here * held["w0"][plane] + held["z0"][plane] * image))
        if stage == 2:
            found.append(total(here * made["s"][plane] + made["p"][plane] * image))
        if not last:
            before = image + cz_ref[plane] * before
            work_ref[plane] = before
            before = before * inv_ref[plane]
        return tuple(old + new for old, new in zip(sums, found)), before

    blank = jnp.zeros((8, LANES), f32)
    dots, _ = lax.fori_loop(
        0, planes, image_plane, ((blank,) * (3 if stage else 2), blank if last else empty)
    )
    writes["w"].start()
    row = scalar_row([jnp.sum(value) for value in dots])
    if last:
        send_ref[...] = jnp.broadcast_to(row, send_ref.shape)
    else:

        def backward(step, after):
            plane = planes - 1 - step
            value = (work_ref[plane] + cz_ref[plane + 1] * after) * inv_ref[plane]
            u_ref[plane] = value
            return value

        lax.fori_loop(0, planes, backward, empty)
        write_edges(even_z, even_y, u_ref, edges_z, edges_y)
        reads["dest"].wait()
        parts = coarse_parts(region_row(w_ref, code_ref), held["dest"])
        send_ref[...] = parts + jnp.where(iota(parts.shape, 0) % 2 == 0, row, 0.0)
    wait_all(writes.values())


def final_kernel(
    d0_ref, d1_ref, d2_ref, r_hbm, w_hbm, s_hbm, z0_hbm, p_hbm, z_hbm, x_out, r_out,
    r_ref, w_ref, s_ref, z0_ref, p_ref, z_ref, x_ref, in_sems, out_sems,
):
    pairs = [(z0_hbm, z0_ref), (p_hbm, p_ref), (z_hbm, z_ref), (r_hbm, r_ref), (w_hbm, w_ref), (s_hbm, s_ref)]
    reads = [pltpu.make_async_copy(a, b, in_sems.at[i]) for i, (a, b) in enumerate(pairs)]
    start_all(reads)
    sums = [table_rows(d0_ref[...])[0:1], table_rows(d1_ref[...])[0:1], jnp.sum(d2_ref[...], axis=0, keepdims=True)]
    alphas, betas = scalars_of(sums)
    mixed = alphas[2] * betas[2]
    along = alphas[1] + mixed
    wait_all(reads[:3])
    x_ref[...] = alphas[0] * z0_ref[...] + along * p_ref[...] + alphas[2] * z_ref[...]
    x_write = pltpu.make_async_copy(x_ref, x_out, out_sems.at[0])
    x_write.start()
    wait_all(reads[3:])
    r_ref[...] = r_ref[...] - (alphas[2] * w_ref[...] + mixed * s_ref[...])
    r_write = pltpu.make_async_copy(r_ref, r_out, out_sems.at[1])
    r_write.start()
    x_write.wait()
    r_write.wait()


def call(kernel, outs, scratch, args):
    spaces = {"smem": pltpu.SMEM, "vmem": pltpu.VMEM, "kept": pltpu.VMEM, "hbm": pltpu.HBM}

    def specs(items):
        return [pl.BlockSpec(memory_space=spaces[space]) for space, _ in items]

    held = sum(4 * math.prod(ref.shape) for ref in scratch)
    places = {"hbm": pltpu.HBM, "kept": pltpu.VMEM}
    made = [places[space](out.shape, out.dtype) if space in places else out for space, out in outs]
    operands = [
        pltpu.with_memory_space_constraint(value, places[space]) if space in places else value for space, value in args
    ]
    return pl.pallas_call(
        kernel,
        out_shape=made,
        in_specs=specs(args),
        out_specs=specs(outs),
        scratch_shapes=scratch,
        compiler_params=pltpu.CompilerParams(vmem_limit_bytes=held + 12 * 1024 * 1024),
    )(*operands)


def swaps(axis, first):
    count = lax.axis_size(axis)
    pairs = []
    for i in range(first, count + first, 2):
        low, high = i % count, (i + 1) % count
        pairs += [(low, high), (high, low)]
    return pairs


def swap(block, axis, first):
    return lax.ppermute(block, axis, swaps(axis, first))


def solve(fraction, source, bubble_label, subdomain, coarse_inverse):
    planes, rows, width = fraction.shape
    slabs = lax.axis_size("gz")
    columns = lax.axis_size("gy")
    devices = slabs * columns
    slab = lax.axis_index("gz")
    column = lax.axis_index("gy")
    here = slab * columns + column
    even_z = slab % 2 == 0
    field = jax.ShapeDtypeStruct((planes, rows, width), f32)

    def shape(*dims, dtype=f32):
        return jax.ShapeDtypeStruct(dims, dtype)

    def vmem(*dims, dtype=f32):
        return pltpu.VMEM(dims, dtype)

    def like(items):
        return [vmem(*value.shape, dtype=value.dtype) for value in items]

    def semaphores(count):
        return pltpu.SemaphoreType.DMA((count,))

    def tag(space, items):
        return [(space, item) for item in items]

    edge = jnp.stack(
        [
            (slab == 0).astype(i32),
            (slab == slabs - 1).astype(i32),
            (column == 0).astype(i32),
            (column == columns - 1).astype(i32),
            here * B_DEV,
            jnp.int32(columns * B_DEV),
            here * S_DEV,
            slab % 2,
            column % 2,
        ]
    )

    top, bottom, *sides, bubbles = call(
        slices_kernel,
        tag("vmem", [shape(DEPTH, rows, width)] * 2 + [shape(planes, DEPTH, width)] * 2 + [shape(B_DEV, devices * SPAN)]),
        [vmem(planes, rows, width), vmem(SPAN, devices * SPAN), semaphores(2)],
        tag("smem", [edge]) + tag("hbm", [fraction, coarse_inverse]),
    )
    coarse_in = [swap(bubbles, "gz", 0), swap(bubbles, "gz", 1)]
    y_in = [swap(sides[0], "gy", 0), swap(sides[1], "gy", 1)]
    z_in = [swap(top, "gz", 0), swap(bottom, "gz", 1)]
    corner = jnp.stack(y_in)
    corner_top = jnp.where(even_z, corner[:, planes - DEPTH :], corner[:, :DEPTH])
    corner_bottom = jnp.where(even_z, corner[:, :DEPTH], corner[:, planes - DEPTH :])
    corner_in = [swap(corner_top, "gz", 0), swap(corner_bottom, "gz", 1)]

    def spread(matrix):
        return matrix.reshape(matrix.shape[0], devices, SPAN)

    dest_shape = shape(REGIONS, 2 * devices, LANES)
    spread_in = [spread(m) for m in [coarse_inverse] + coarse_in]
    (dest,) = call(
        partial(destinations_kernel, columns),
        tag("hbm", [dest_shape]),
        [vmem(REGIONS, devices, LANES)] + like([dest_shape]) + [semaphores(1)],
        tag("smem", [(slab % 2).reshape(1)]) + tag("vmem", spread_in),
    )
    codes = shape(planes, rows, width, dtype=i8)
    faces = shape(planes + 1, rows, width)
    inputs = [fraction, source, bubble_label, subdomain, dest]
    tall = rows + 8
    wide = shape(2 * devices, LANES)
    first_edges = [shape(2, rows, width)] * 2 + [shape(2, planes, width)] * 2
    later_edges = [shape(rows, width)] * 2 + [shape(planes, width)] * 2
    outs = tag("vmem", first_edges + [wide])
    outs += tag("kept", [codes, faces, field, field, field, shape(planes, width)]) + tag("hbm", [field, field])
    *sent, send, code, cz, cy, cx, inv, south, r0, diag = call(
        setup_kernel,
        outs,
        like(inputs)
        + like([field, field, field])
        + [
            vmem(planes + 2 * DEPTH, tall, width),
            vmem(planes + 4, tall, width),
            vmem(planes + 4, tall, width),
            vmem(planes + 2, tall, width),
            vmem(planes + 1, rows, width),
            vmem(planes, rows, width),
            semaphores(len(inputs)),
            semaphores(2),
        ],
        tag("smem", [edge]) + tag("vmem", z_in + y_in + corner_in) + tag("hbm", inputs),
    )
    matrix = [code, cz, cy, cx, inv, south]

    def exchange(parts):
        blocks = parts.reshape(devices, -1, LANES)
        return lax.all_to_all(blocks, ("gz", "gy"), 0, 0).reshape(parts.shape)

    def halos(sent):
        return [swap(sent[0], "gz", 0), swap(sent[1], "gz", 1), swap(sent[2], "gy", 0), swap(sent[3], "gy", 1)]

    def share(sent, send):
        edges = halos(sent)
        parts = [exchange(send)]
        return edges, parts

    def step(stage, parts, edges, state):
        last = stage == 2
        operands = state + ([diag] if last else [diag, dest])
        outs = [field] * (2, 3, 5)[stage]
        ends = [] if last else later_edges
        scratch = like(operands) + [vmem(planes + 2, rows, width), vmem(2, planes, width)] + like([field] * len(outs))
        if not last:
            scratch += like([field])
        scratch += [semaphores(len(operands)), semaphores(len(outs))]
        results = call(
            partial(step_kernel, stage),
            tag("vmem", ends + [shape(devices, LANES) if last else wide]) + tag("hbm", outs),
            scratch,
            tag("smem", [edge]) + tag("vmem", parts + edges) + tag("kept", matrix) + tag("hbm", operands),
        )
        return results[: len(ends)], results[len(ends)], results[len(ends) + 1 :]

    edges, parts = share(sent, send)
    sent, send, (z0, w0) = step(0, parts, edges, [r0])
    more_edges, more_parts = share(sent, send)
    edges, parts = edges + more_edges, parts + more_parts
    sent, send, (r1, z1, w1) = step(1, parts, edges, [r0, w0, z0])
    more_edges, more_parts = share(sent, send)
    edges, parts = edges + more_edges, parts + more_parts
    _, send, (r2, s1, p1, z2, w2) = step(2, parts, edges, [r1, w1, w0, z1, z0])
    parts = parts + [exchange(send)]
    return tuple(
        call(
            final_kernel,
            tag("hbm", [field, field]),
            like([field] * 7) + [semaphores(6), semaphores(2)],
            tag("vmem", parts[1:]) + tag("hbm", [r2, w2, s1, z0, p1, z2]),
        )
    )


def solution(mesh):
    placed = (
        P("gz", "gy", None),
        P("gz", "gy", None),
        P("gz", "gy", None),
        P("gz", "gy", None),
        P(("gz", "gy"), None),
    )
    return jax.shard_map(
        solve,
        mesh=mesh,
        in_specs=placed,
        out_specs=(P("gz", "gy", None), P("gz", "gy", None)),
        check_vma=False,
    )
```

```python
import math
from functools import partial

import jax
import jax.numpy as jnp
from jax import lax
from jax.experimental import pallas as pl
from jax.experimental.pallas import tpu as pltpu
from jax.sharding import PartitionSpec as P


S_DEV = 4
B_DEV = 16
SPAN = S_DEV + B_DEV
LANES = 128
GROUPS = 4
CODES = GROUPS * B_DEV
REGIONS = S_DEV + 3 * B_DEV
SCALARS = 96
DEPTH = 3
PIECE = 16

surface_tension = 0.5
shift_term = 0.05
gas_drop = 0.75
norm_floor = 0.25
highest = lax.Precision.HIGHEST
f32 = jnp.float32
i32 = jnp.int32
i8 = jnp.int8
bf16 = jnp.bfloat16


def iota(shape, dim):
    return lax.broadcasted_iota(i32, shape, dim)


def up_rows(field):
    return pltpu.roll(field, field.shape[0] - 1, 0)


def down_rows(field):
    return pltpu.roll(field, 1, 0)


def next_x(field):
    return pltpu.roll(field, field.shape[1] - 1, 1)


def prev_x(field):
    return pltpu.roll(field, 1, 1)


def total(field):
    rows, width = field.shape
    folded = field[:, :LANES]
    for start in range(LANES, width, LANES):
        folded = folded + field[:, start : start + LANES]
    return jnp.sum(folded.reshape(rows // 8, 8, LANES), axis=0)


def digits(code):
    forms = []
    rest = code.astype(f32).astype(bf16)
    bits = []
    for power in (32, 16, 8, 4, 2, 1):
        bit = rest if power == 1 else jnp.clip(rest - (power - 1), 0, 1)
        bits.append(bit)
        rest = rest - power * bit
    for high, low in zip(bits[::2], bits[1::2]):
        no_high, no_low = 1 - high, 1 - low
        forms.append([no_high * no_low, no_high * low, high * no_low, high * low])
    return forms


def piece_sums(values, code):
    groups, outer, inner = digits(code)
    high = values.astype(bf16)
    low = (values - high.astype(f32)).astype(bf16)
    left = [group * part for part in (high, low) for group in groups]
    right = [first * second for first in outer for second in inner]
    return lax.dot_general(
        jnp.concatenate(left, axis=0),
        jnp.concatenate(right, axis=0),
        (((1,), (1,)), ((), ())),
        preferred_element_type=f32,
    )


def region_row(value_ref, code_ref):
    planes, rows, _ = value_ref.shape

    def step(plane, acc):
        code = code_ref[plane].astype(i32)
        for start in range(0, rows, PIECE):
            acc = acc + piece_sums(value_ref[plane, start : start + PIECE, :], code[start : start + PIECE])
        return acc

    acc = lax.fori_loop(
        0, planes, step, jnp.zeros((2 * GROUPS * PIECE, B_DEV * PIECE), f32), unroll=planes
    )
    shape = acc.shape
    kept = jnp.where(iota(shape, 0) % PIECE == iota(shape, 1) % PIECE, acc, 0.0)
    folded = jnp.sum(kept.reshape(2 * GROUPS, PIECE, shape[1]), axis=1)
    shape = (shape[1], LANES)
    pick = jnp.where(iota(shape, 0) // PIECE == iota(shape, 1) % B_DEV, 1.0, 0.0)
    spread = jnp.dot(folded, pick, precision=highest, preferred_element_type=f32)
    shape = spread.shape
    lane = iota(shape, 1)
    mine = (iota(shape, 0) % GROUPS == lane // B_DEV) & (lane < CODES)
    return jnp.sum(jnp.where(mine, spread, 0.0), axis=0, keepdims=True)


def scalar_row(scalars):
    lane = iota((1, LANES), 1)
    row = jnp.zeros((1, LANES), f32)
    for index, value in enumerate(scalars):
        row = jnp.where(lane == SCALARS + index, value, row)
    return row


def lane_of(row, index):
    return jnp.sum(jnp.where(iota(row.shape, 1) == SCALARS + index, row, 0.0))


def lookup(table, index):
    rows, width = index.shape
    wide = jnp.broadcast_to(table, (rows, LANES))
    return jnp.concatenate(
        [
            jnp.take_along_axis(wide, index[:, start : start + LANES], axis=1)
            for start in range(0, width, LANES)
        ],
        axis=1,
    )


class Place:
    def __init__(self):
        slab, column = lax.axis_index("gz"), lax.axis_index("gy")
        slabs, columns = lax.axis_size("gz"), lax.axis_size("gy")
        here = slab * columns + column
        self.first_z, self.last_z = slab == 0, slab == slabs - 1
        self.first_y, self.last_y = column == 0, column == columns - 1
        self.base, self.stride, self.sub_base = here * B_DEV, columns * B_DEV, here * S_DEV
        self.even_z, self.even_y = slab % 2 == 0, column % 2 == 0


def start_all(copies):
    @pl.when(lax.axis_index("gz") >= 0)
    def _():
        for copy in copies:
            copy.start()


def wait_all(copies):
    for copy in copies:
        copy.wait()


def coarse_parts(row, dest_ref):
    wide = jnp.broadcast_to(row, (8, LANES))

    def step(region, acc):
        lane = jnp.where(region < S_DEV, region, region + B_DEV - S_DEV)
        factor = jnp.take_along_axis(wide, jnp.full((8, LANES), lane, i32), axis=1)[0:1, :]
        return acc + factor * dest_ref[region]

    small = dest_ref.shape[1] <= 64
    return lax.fori_loop(0, REGIONS, step, jnp.zeros(dest_ref.shape[1:], f32), unroll=REGIONS if small else 4)


def destinations_kernel(columns, own_ref, near_ref, far_ref, dest_hbm, wide_ref, dest_ref, sems):
    devices = own_ref.shape[1]
    even_z = Place().even_z
    wide_ref[...] = jnp.zeros(wide_ref.shape, f32)
    low_start = pl.multiple_of(jnp.where(even_z, 2 * B_DEV, 0), B_DEV) + S_DEV
    high_start = pl.multiple_of(jnp.where(even_z, 0, 2 * B_DEV), B_DEV) + S_DEV
    wide_ref[0:S_DEV, :, 0:SPAN] = own_ref[0:S_DEV]
    wide_ref[S_DEV + B_DEV : S_DEV + 2 * B_DEV, :, 0:SPAN] = own_ref[S_DEV:SPAN]
    wide_ref[pl.ds(low_start, B_DEV), :, 0:SPAN] = near_ref[...]
    wide_ref[pl.ds(high_start, B_DEV), :, 0:SPAN] = far_ref[...]
    lane = iota((devices, LANES), 1)

    def place(base, shift, first, count):
        moved = pltpu.roll(base, shift, 1) if shift else base
        return jnp.where((lane >= first) & (lane < first + count), moved, 0.0)

    def from_device(field, step):
        return pltpu.roll(field, (-step) % devices, 0) if step % devices else field

    def one(region, carry):
        base = wide_ref[region]
        bubbles = B_DEV - S_DEV
        table = place(base, 0, 0, S_DEV) + place(base, B_DEV + bubbles, 2 * B_DEV, B_DEV)
        table = table + from_device(
            place(base, S_DEV, S_DEV, S_DEV) + place(base, 2 * B_DEV + bubbles, 3 * B_DEV, B_DEV), columns
        )
        table = table + from_device(
            place(base, 2 * S_DEV, 2 * S_DEV, S_DEV) + place(base, bubbles, B_DEV, B_DEV), -columns
        )
        table = table + from_device(place(base, 3 * S_DEV, 3 * S_DEV, S_DEV), 1)
        table = table + from_device(place(base, 3 * B_DEV + bubbles, 4 * B_DEV, B_DEV), 2 * columns)
        table = table + from_device(place(base, 4 * B_DEV + bubbles, 5 * B_DEV, B_DEV), -2 * columns)
        own_codes = jnp.where((lane < S_DEV) | ((lane >= B_DEV) & (lane < CODES)), table, 0.0)
        dest_ref[region, pl.ds(0, devices, stride=2), :] = table
        dest_ref[region, pl.ds(1, devices, stride=2), :] = from_device(own_codes, -1)
        return carry

    lax.fori_loop(0, REGIONS, one, 0, unroll=4)
    write = pltpu.make_async_copy(dest_ref, dest_hbm, sems.at[0])
    write.start()
    write.wait()


def write_edges(even_z, even_y, value_ref, z_refs, y_refs, convert=lambda value: value):
    planes, rows, _ = value_ref.shape
    z_refs[0][...] = convert(value_ref[jnp.where(even_z, planes - 1, 0)])
    z_refs[1][...] = convert(value_ref[jnp.where(even_z, 0, planes - 1)])
    for plane in range(planes):
        first = convert(value_ref[plane, 0:1, :])
        last = convert(value_ref[plane, rows - 1 : rows, :])
        y_refs[0][plane : plane + 1, :] = jnp.where(even_y, last, first)
        y_refs[1][plane : plane + 1, :] = jnp.where(even_y, first, last)


def slices_kernel(frac_hbm, coarse_hbm, z0_ref, z1_ref, y0_ref, y1_ref, bubble_ref, frac_ref, coarse_ref, sems):
    planes, rows, _ = frac_ref.shape
    copies = [
        pltpu.make_async_copy(frac_hbm, frac_ref, sems.at[0]),
        pltpu.make_async_copy(coarse_hbm, coarse_ref, sems.at[1]),
    ]
    start_all(copies)
    place = Place()
    even_z, even_y = place.even_z, place.even_y
    wait_all(copies)
    bubble_ref[...] = coarse_ref[S_DEV:SPAN, :]
    z0_ref[...] = frac_ref[pl.ds(jnp.where(even_z, planes - DEPTH, 0), DEPTH)]
    z1_ref[...] = frac_ref[pl.ds(jnp.where(even_z, 0, planes - DEPTH), DEPTH)]
    first, last = frac_ref[:, 0:DEPTH, :], frac_ref[:, rows - DEPTH : rows, :]
    y0_ref[...] = jnp.where(even_y, last, first)
    y1_ref[...] = jnp.where(even_y, first, last)


def setup_kernel(
    z0_in, z1_in, y0_in, y1_in, k0_in, k1_in, frac_hbm, source_hbm, label_hbm, sub_hbm, dest_hbm,
    ez0_ref, ez1_ref, ey0_ref, ey1_ref, send_ref,
    code_ref, cz_ref, cy_ref, cx_ref, inv_ref, south_ref, r_hbm, diag_hbm,
    frac_ref, source_ref, label_ref, sub_ref, dest_ref, r_ref, diag_ref, b_ref,
    deep_ref, nz_ref, flat_ref, kap_ref, fz_ref, work_ref, in_sems, out_sems,
):
    planes, rows, width = frac_ref.shape
    tall = rows + 8
    place = Place()
    first_z, last_z, first_y, last_y = place.first_z, place.last_z, place.first_y, place.last_y
    base, stride, sub_base = place.base, place.stride, place.sub_base
    even_z, even_y = place.even_z, place.even_y
    pairs = [(frac_hbm, frac_ref), (label_hbm, label_ref), (sub_hbm, sub_ref), (source_hbm, source_ref), (dest_hbm, dest_ref)]
    reads = [pltpu.make_async_copy(a, b, in_sems.at[i]) for i, (a, b) in enumerate(pairs)]
    start_all(reads)
    row = iota((tall, width), 0)
    lane = iota((tall, width), 1)
    inside_y = ((row < rows) | ((row < rows + 4) & jnp.logical_not(last_y))) | (
        (row >= rows + 4) & jnp.logical_not(first_y)
    )
    first_plane = jnp.where(first_z, 0, -planes)
    last_plane = jnp.where(last_z, planes, 2 * planes)

    def right_of(field):
        moved = next_x(field)
        tile = lane[: field.shape[0], :LANES]
        ended = jnp.where(tile == LANES - 1, 0.0, moved[:, width - LANES :])
        return jnp.concatenate([moved[:, : width - LANES], ended], axis=1)

    def left_of(field):
        moved = prev_x(field)
        tile = lane[: field.shape[0], :LANES]
        return jnp.concatenate([jnp.where(tile == 0, 0.0, moved[:, :LANES]), moved[:, LANES:]], axis=1)

    deep_ref[:, rows:tall, :] = jnp.zeros((planes + 2 * DEPTH, 8, width), f32)
    near_z = jnp.where(even_z, planes + DEPTH, 0)
    far_z = jnp.where(even_z, 0, planes + DEPTH)
    out_near, out_far = jnp.where(even_z, last_z, first_z), jnp.where(even_z, first_z, last_z)
    deep_ref[pl.ds(near_z, DEPTH), 0:rows, :] = jnp.where(out_near, 0.0, z0_in[...])
    deep_ref[pl.ds(far_z, DEPTH), 0:rows, :] = jnp.where(out_far, 0.0, z1_in[...])
    high, low = slice(rows, rows + DEPTH), slice(tall - DEPTH, tall)

    def fill_rows(first, second, out_first, out_second):
        deep_ref[DEPTH : planes + DEPTH, first, :] = jnp.where(out_first, 0.0, y0_in[...])
        deep_ref[DEPTH : planes + DEPTH, second, :] = jnp.where(out_second, 0.0, y1_in[...])
        for start, corner, out in ((near_z, k0_in, out_near), (far_z, k1_in, out_far)):
            deep_ref[pl.ds(start, DEPTH), first, :] = jnp.where(out | out_first, 0.0, corner[0])
            deep_ref[pl.ds(start, DEPTH), second, :] = jnp.where(out | out_second, 0.0, corner[1])

    @pl.when(even_y)
    def _():
        fill_rows(high, low, last_y, first_y)

    @pl.when(jnp.logical_not(even_y))
    def _():
        fill_rows(low, high, first_y, last_y)

    reads[0].wait()
    deep_ref[DEPTH : planes + DEPTH, 0:rows, :] = frac_ref[...]

    def normal_plane(index, carry):
        keep = (index - 2 >= first_plane) & (index - 2 < last_plane)
        here = deep_ref[index + 1]
        gz = deep_ref[index + 2] - deep_ref[index]
        gy = up_rows(here) - down_rows(here)
        gx = right_of(here) - left_of(here)
        scale = jnp.minimum(lax.rsqrt(gz * gz + gy * gy + gx * gx), 0.5 / norm_floor)
        scale = jnp.where(inside_y & keep, scale, 0.0)
        ny = gy * scale
        nx = gx * scale
        nz_ref[index] = gz * scale
        flat_ref[index] = (up_rows(ny) - down_rows(ny)) + (right_of(nx) - left_of(nx))
        return carry

    lax.fori_loop(0, planes + 4, normal_plane, 0)

    def kappa_plane(index, carry):
        keep = (index - 1 >= first_plane) & (index - 1 < last_plane)
        value = -0.5 * ((nz_ref[index + 2] - nz_ref[index]) + flat_ref[index + 1])
        kap_ref[index] = jnp.where(inside_y & keep, value, 0.0)
        return carry

    lax.fori_loop(0, planes + 2, kappa_plane, 0)
    mid = pl.ds(0, rows)

    def z_face(index, carry):
        f_low = deep_ref[index + 2, mid, :]
        f_high = deep_ref[index + 3, mid, :]
        coef = 2.0 * pl.reciprocal((1.0 - gas_drop * f_low) + (1.0 - gas_drop * f_high))
        cz_ref[index] = coef
        mean = 0.5 * (kap_ref[index, mid, :] + kap_ref[index + 1, mid, :])
        fz_ref[index] = coef * mean * (f_high - f_low)
        return carry

    lax.fori_loop(0, planes + 1, z_face, 0)
    row_mid = row[:rows]
    lane_mid = lane[:rows]
    wait_all(reads[1:])

    def assemble_plane(plane, carry):
        inv_before, g_before = carry
        f = deep_ref[plane + 3]
        k = kap_ref[plane + 1]
        d = 1.0 - gas_drop * f
        f_up = up_rows(f)
        cy = 2.0 * pl.reciprocal(d + (1.0 - gas_drop * f_up))
        fy = cy * (0.5 * (k + up_rows(k))) * (f_up - f)
        cyp, cym = cy[:rows], down_rows(cy)[:rows]
        sum_y = fy[:rows] - down_rows(fy)[:rows]
        f, k, d = f[:rows], k[:rows], d[:rows]
        f_right = right_of(f)
        cxp = 2.0 * pl.reciprocal(d + (1.0 - gas_drop * f_right))
        fx = cxp * (0.5 * (k + right_of(k))) * (f_right - f)
        outer = jnp.concatenate([2.0 / (d[:, :LANES] + 1.0), jnp.zeros((rows, width - LANES), f32)], axis=1)
        cxm = jnp.where(lane_mid == 0, outer, prev_x(cxp))
        fx_before = jnp.where(lane_mid == 0, outer * (0.5 * k) * f, prev_x(fx))
        terms = fz_ref[plane + 1] - fz_ref[plane] + sum_y + (fx - fx_before)
        rhs = source_ref[plane] - surface_tension * terms
        down = cz_ref[plane]
        diagonal = shift_term + (cz_ref[plane + 1] + down + cyp + cym + cxp + cxm)
        mult = down * inv_before
        inv = pl.reciprocal(diagonal - mult * down)
        g = rhs + mult * g_before
        r_ref[plane] = rhs
        diag_ref[plane] = diagonal
        inv_ref[plane] = inv
        work_ref[plane] = g
        cy_ref[plane] = jnp.where((row_mid == rows - 1) & last_y, 0.0, cyp)
        south_ref[pl.ds(plane, 1), :] = jnp.where(first_y, 0.0, cym[0:1, :])
        cx_ref[plane] = jnp.where(lane_mid == width - 1, 0.0, cxp)
        label = label_ref[plane]
        offset = label - base
        below = offset < 0
        above = offset >= stride
        group = jnp.where(below, 1, jnp.where(above, 3, 2))
        inner = jnp.where(below, offset + stride, jnp.where(above, offset - stride, offset))
        code = jnp.where(label >= 0, group * B_DEV + inner, sub_ref[plane] - sub_base)
        code_ref[plane] = (code & (CODES - 1)).astype(i8)
        return (inv, g)

    blank = jnp.zeros((rows, width), f32)
    lax.fori_loop(0, planes, assemble_plane, (blank, blank))

    def backward(step, after):
        plane = planes - 1 - step
        value = (work_ref[plane] + cz_ref[plane + 1] * after) * inv_ref[plane]
        b_ref[plane] = value
        return value

    lax.fori_loop(0, planes, backward, blank)
    cz_ref[0] = jnp.where(first_z, 0.0, cz_ref[0])
    cz_ref[planes] = jnp.where(last_z, 0.0, cz_ref[planes])
    writes = [
        pltpu.make_async_copy(r_ref, r_hbm, out_sems.at[0]), pltpu.make_async_copy(diag_ref, diag_hbm, out_sems.at[1])
    ]
    start_all(writes)
    write_edges(even_z, even_y, b_ref, [ez0_ref.at[0], ez1_ref.at[0]], [ey0_ref.at[0], ey1_ref.at[0]])
    for plane in range(planes):
        label_ref[plane] = code_ref[plane].astype(i32)
    write_edges(
        even_z, even_y, label_ref, [ez0_ref.at[1], ez1_ref.at[1]], [ey0_ref.at[1], ey1_ref.at[1]],
        convert=lambda value: value.astype(f32),
    )
    send_ref[...] = coarse_parts(region_row(r_ref, code_ref), dest_ref)
    wait_all(writes)


def table_rows(parts):
    folded = jnp.sum(parts.reshape(parts.shape[0] // 8, 8, LANES), axis=0)
    even = iota(folded.shape, 0) % 2 == 0
    return jnp.concatenate(
        [
            jnp.sum(jnp.where(even, folded, 0.0), axis=0, keepdims=True),
            jnp.sum(jnp.where(even, 0.0, folded), axis=0, keepdims=True),
        ],
        axis=0,
    )


def scalars_of(sums):
    alphas, betas, curves = [], [None], []
    for step, row in enumerate(sums):
        gamma = lane_of(row, 0)
        if step == 0:
            curve = lane_of(row, 1)
        else:
            beta = gamma / lane_of(sums[step - 1], 0)
            betas.append(beta)
            curve = lane_of(row, 1) + beta * (lane_of(row, 2) + beta * curves[-1])
        curves.append(curve)
        alphas.append(gamma / curve)
    return alphas, betas


def step_kernel(stage, *refs):
    refs = list(refs)

    def take(count):
        out = refs[:count]
        del refs[:count]
        return out

    parts = take(stage + 1)
    halos = [take(4) for _ in range(stage + 1)]
    code_ref, cz_ref, cy_ref, cx_ref, inv_ref, south_ref = take(6)
    last = stage == 2
    names = (("r",), ("r", "w0", "z0"), ("r", "w1", "w0", "z1", "z0"))[stage] + (("diag",) if last else ("diag", "dest"))
    sources = dict(zip(names, take(len(names))))
    out_names = (("z", "w"), ("rn", "z", "w"), ("rn", "s", "p", "z", "w"))[stage]
    if not last:
        edges_z, edges_y = take(2), take(2)
    (send_ref,) = take(1)
    if last:
        pad_ref, w_ref, *others = take(6)
        made = dict(zip(("rn", "s", "p", "x"), others))
        out_names = ()
        held = dict(zip(names, take(len(names))))
        side_ref, work_ref, in_sems = take(3)
        out_sems = None
    else:
        sinks = dict(zip(out_names, take(len(out_names))))
        held = dict(zip(names, take(len(names))))
        pad_ref, side_ref, work_ref, w_ref = take(4)
        made = {"z": pad_ref.at[pl.ds(1, pad_ref.shape[0] - 2)], "w": w_ref}
        for name in out_names[:-2]:
            (made[name],) = take(1)
        u_ref, in_sems, out_sems = take(3)

    reads = {name: pltpu.make_async_copy(sources[name], held[name], in_sems.at[i]) for i, name in enumerate(names)}
    start_all(reads.values())
    writes = {name: pltpu.make_async_copy(made[name], sinks[name], out_sems.at[i]) for i, name in enumerate(out_names)}
    planes, rows, width = code_ref.shape
    place = Place()
    even_z, even_y = place.even_z, place.even_y

    sums = [table_rows(part[...]) for part in parts]
    alphas, betas = scalars_of([row[0:1] for row in sums[1:]])
    table = sums[0]
    if stage >= 1:
        table = table - alphas[0] * sums[1]
    if stage == 2:
        table = table - alphas[1] * (sums[2] + betas[1] * sums[1])
    near, side = table[0:1], table[1:2]

    def combine(values):
        out = values[0]
        if stage >= 1:
            out = out - alphas[0] * values[1]
        if stage == 2:
            out = out - alphas[1] * (values[2] + betas[1] * values[1])
        return out

    for slot in range(2):
        upper = even_z if slot == 0 else jnp.logical_not(even_z)
        index = halos[0][slot][1].astype(i32)
        high = jnp.where(index < B_DEV, index + S_DEV, index + B_DEV)
        low = jnp.where(
            index < B_DEV, index + 2 * S_DEV, jnp.where(index < 2 * B_DEV, index + 4 * B_DEV, index - B_DEV)
        )
        block = combine([halos[0][slot][0]] + [halo[slot][...] for halo in halos[1:]])
        pad_ref[jnp.where(upper, planes + 1, 0)] = block + lookup(near, jnp.where(upper, high, low))
        upper = even_y if slot == 0 else jnp.logical_not(even_y)
        index = halos[0][2 + slot][1].astype(i32)
        block = combine([halos[0][2 + slot][0]] + [halo[2 + slot][...] for halo in halos[1:]])
        found = jnp.where(
            upper, lookup(near, (index & (B_DEV - 1)) + 3 * S_DEV), lookup(side, index)
        )
        side_ref[jnp.where(upper, 1, 0)] = block + found

    for name in names:
        if name not in ("diag", "dest"):
            reads[name].wait()
    empty = jnp.zeros((rows, width), f32)

    def residual(plane, before):
        value = held["r"][plane]
        if stage == 1:
            value = value - alphas[0] * held["w0"][plane]
            made["rn"][plane] = value
        if stage == 2:
            image = held["w1"][plane] + betas[1] * held["w0"][plane]
            made["s"][plane] = image
            along = held["z1"][plane] + betas[1] * held["z0"][plane]
            made["p"][plane] = along
            made["x"][plane] = alphas[0] * held["z0"][plane] + alphas[1] * along
            value = value - alphas[1] * image
            made["rn"][plane] = value
        value = value + cz_ref[plane] * before
        work_ref[plane] = value
        return value * inv_ref[plane]

    lax.fori_loop(0, planes, residual, empty)
    start_all([writes[name] for name in out_names[:-2]])

    def direction(step, after):
        plane = planes - 1 - step
        value = (work_ref[plane] + cz_ref[plane + 1] * after) * inv_ref[plane]
        pad_ref[plane + 1] = value + lookup(near, code_ref[plane].astype(i32))
        return value

    lax.fori_loop(0, planes, direction, empty)
    if not last:
        writes["z"].start()
    reads["diag"].wait()
    row = iota((rows, width), 0)

    def image_plane(plane, carry):
        sums, before = carry
        here = pad_ref[plane + 1]
        cy, cx = cy_ref[plane], cx_ref[plane]
        north = jnp.where(row == rows - 1, side_ref[1, pl.ds(plane, 1), :], up_rows(here))
        below = south_ref[pl.ds(plane, 1), :] * side_ref[0, pl.ds(plane, 1), :]
        south = jnp.where(row == 0, below, down_rows(cy * here))
        image = held["diag"][plane] * here - (
            cz_ref[plane + 1] * pad_ref[plane + 2]
            + cz_ref[plane] * pad_ref[plane]
            + (cy * north + south)
            + (cx * next_x(here) + prev_x(cx * here))
        )
        w_ref[plane] = image
        new = made["rn"] if stage else held["r"]
        found = [total(new[plane] * here), total(here * image)]
        if stage == 1:
            found.append(total(here * held["w0"][plane] + held["z0"][plane] * image))
        if stage == 2:
            found.append(total(here * made["s"][plane] + made["p"][plane] * image))
        if not last:
            before = image + cz_ref[plane] * before
            work_ref[plane] = before
            before = before * inv_ref[plane]
        return tuple(old + new for old, new in zip(sums, found)), before

    blank = jnp.zeros((8, LANES), f32)
    dots, _ = lax.fori_loop(
        0, planes, image_plane, ((blank,) * (3 if stage else 2), blank if last else empty)
    )
    if not last:
        writes["w"].start()
    row = scalar_row([jnp.sum(value) for value in dots])
    if last:
        send_ref[...] = jnp.broadcast_to(row, send_ref.shape)
    else:

        def backward(step, after):
            plane = planes - 1 - step
            value = (work_ref[plane] + cz_ref[plane + 1] * after) * inv_ref[plane]
            u_ref[plane] = value
            return value

        lax.fori_loop(0, planes, backward, empty)
        write_edges(even_z, even_y, u_ref, edges_z, edges_y)
        reads["dest"].wait()
        parts = coarse_parts(region_row(w_ref, code_ref), held["dest"])
        send_ref[...] = parts + jnp.where(iota(parts.shape, 0) % 2 == 0, row, 0.0)
    wait_all(writes.values())


def final_kernel(
    d0_ref, d1_ref, d2_ref, z_ref, w_ref, r_ref, s_ref, p_ref, part_ref, x_out, r_out, x_new, r_new, sems
):
    sums = [table_rows(d0_ref[...])[0:1], table_rows(d1_ref[...])[0:1], jnp.sum(d2_ref[...], axis=0, keepdims=True)]
    alphas, betas = scalars_of(sums)
    mixed = alphas[2] * betas[2]
    planes = r_ref.shape[0]
    writes = []
    for half in range(2):
        low, high = half * planes // 2, (half + 1) * planes // 2
        x_new[low:high] = part_ref[low:high] + alphas[2] * z_ref[low + 1 : high + 1] + mixed * p_ref[low:high]
        r_new[low:high] = r_ref[low:high] - alphas[2] * w_ref[low:high] - mixed * s_ref[low:high]
        piece = pl.ds(low, high - low)
        pairs = [(x_new.at[piece], x_out.at[piece]), (r_new.at[piece], r_out.at[piece])]
        copies = [pltpu.make_async_copy(a, b, sems.at[2 * half + i]) for i, (a, b) in enumerate(pairs)]
        start_all(copies)
        writes += copies
    wait_all(writes)


def call(kernel, outs, scratch, args):
    spaces = {"smem": pltpu.SMEM, "vmem": pltpu.VMEM, "kept": pltpu.VMEM, "hbm": pltpu.HBM}

    def specs(items):
        return [pl.BlockSpec(memory_space=spaces[space]) for space, _ in items]

    held = sum(4 * math.prod(ref.shape) for ref in scratch)
    places = {"hbm": pltpu.HBM, "kept": pltpu.VMEM}
    made = [places[space](out.shape, out.dtype) if space in places else out for space, out in outs]
    operands = [
        pltpu.with_memory_space_constraint(value, places[space]) if space in places else value for space, value in args
    ]
    return pl.pallas_call(
        kernel,
        out_shape=made,
        in_specs=specs(args),
        out_specs=specs(outs),
        scratch_shapes=scratch,
        compiler_params=pltpu.CompilerParams(vmem_limit_bytes=held + 12 * 1024 * 1024),
    )(*operands)


def swaps(axis, first):
    count = lax.axis_size(axis)
    pairs = []
    for i in range(first, count + first, 2):
        low, high = i % count, (i + 1) % count
        pairs += [(low, high), (high, low)]
    return pairs


def swap(block, axis, first):
    return lax.ppermute(block, axis, swaps(axis, first))


def solve(fraction, source, bubble_label, subdomain, coarse_inverse):
    planes, rows, width = fraction.shape
    slabs = lax.axis_size("gz")
    columns = lax.axis_size("gy")
    devices = slabs * columns
    slab = lax.axis_index("gz")
    even_z = slab % 2 == 0
    field = jax.ShapeDtypeStruct((planes, rows, width), f32)

    def shape(*dims, dtype=f32):
        return jax.ShapeDtypeStruct(dims, dtype)

    def vmem(*dims, dtype=f32):
        return pltpu.VMEM(dims, dtype)

    def like(items):
        return [vmem(*value.shape, dtype=value.dtype) for value in items]

    def semaphores(count):
        return pltpu.SemaphoreType.DMA((count,))

    def tag(space, items):
        return [(space, item) for item in items]

    top, bottom, *sides, bubbles = call(
        slices_kernel,
        tag("vmem", [shape(DEPTH, rows, width)] * 2 + [shape(planes, DEPTH, width)] * 2 + [shape(B_DEV, devices * SPAN)]),
        [vmem(planes, rows, width), vmem(SPAN, devices * SPAN), semaphores(2)],
        tag("hbm", [fraction, coarse_inverse]),
    )
    coarse_in = [swap(bubbles, "gz", 0), swap(bubbles, "gz", 1)]
    y_in = [swap(sides[0], "gy", 0), swap(sides[1], "gy", 1)]
    z_in = [swap(top, "gz", 0), swap(bottom, "gz", 1)]
    corner = jnp.stack(y_in)
    corner_top = jnp.where(even_z, corner[:, planes - DEPTH :], corner[:, :DEPTH])
    corner_bottom = jnp.where(even_z, corner[:, :DEPTH], corner[:, planes - DEPTH :])
    corner_in = [swap(corner_top, "gz", 0), swap(corner_bottom, "gz", 1)]

    def spread(matrix):
        return matrix.reshape(matrix.shape[0], devices, SPAN)

    dest_shape = shape(REGIONS, 2 * devices, LANES)
    spread_in = [spread(m) for m in [coarse_inverse] + coarse_in]
    (dest,) = call(
        partial(destinations_kernel, columns),
        tag("hbm", [dest_shape]),
        [vmem(REGIONS, devices, LANES)] + like([dest_shape]) + [semaphores(1)],
        tag("vmem", spread_in),
    )
    codes = shape(planes, rows, width, dtype=i8)
    faces = shape(planes + 1, rows, width)
    inputs = [fraction, source, bubble_label, subdomain, dest]
    tall = rows + 8
    wide = shape(2 * devices, LANES)
    first_edges = [shape(2, rows, width)] * 2 + [shape(2, planes, width)] * 2
    later_edges = [shape(rows, width)] * 2 + [shape(planes, width)] * 2
    outs = tag("vmem", first_edges + [wide])
    outs += tag("kept", [codes, faces, field, field, field, shape(planes, width)]) + tag("hbm", [field, field])
    *sent, send, code, cz, cy, cx, inv, south, r0, diag = call(
        setup_kernel,
        outs,
        like(inputs)
        + like([field, field, field])
        + [
            vmem(planes + 2 * DEPTH, tall, width),
            vmem(planes + 4, tall, width),
            vmem(planes + 4, tall, width),
            vmem(planes + 2, tall, width),
            vmem(planes + 1, rows, width),
            vmem(planes, rows, width),
            semaphores(len(inputs)),
            semaphores(2),
        ],
        tag("vmem", z_in + y_in + corner_in) + tag("hbm", inputs),
    )
    matrix = [code, cz, cy, cx, inv, south]

    def exchange(parts):
        blocks = parts.reshape(devices, -1, LANES)
        return lax.all_to_all(blocks, ("gz", "gy"), 0, 0).reshape(parts.shape)

    def halos(sent):
        return [swap(sent[0], "gz", 0), swap(sent[1], "gz", 1), swap(sent[2], "gy", 0), swap(sent[3], "gy", 1)]

    def share(sent, send):
        edges = halos(sent)
        parts = [exchange(send)]
        return edges, parts

    def step(stage, parts, edges, state):
        last = stage == 2
        operands = state + ([diag] if last else [diag, dest])
        tall_field = shape(planes + 2, rows, width)
        sides = vmem(2, planes, width)
        if last:
            outs = tag("vmem", [shape(devices, LANES)]) + tag("kept", [tall_field] + [field] * 5)
            scratch = like(operands) + [sides] + like([field]) + [semaphores(len(operands))]
            count = 0
        else:
            fields = [field] * (2 + stage)
            outs = tag("vmem", later_edges + [wide]) + tag("hbm", fields)
            scratch = like(operands) + like([tall_field]) + [sides] + like([field] * (len(fields) + 1))
            scratch += [semaphores(len(operands)), semaphores(len(fields))]
            count = len(later_edges)
        results = call(
            partial(step_kernel, stage),
            outs,
            scratch,
            tag("vmem", parts + edges) + tag("kept", matrix) + tag("hbm", operands),
        )
        return results[:count], results[count], results[count + 1 :]

    edges, parts = share(sent, send)
    sent, send, (z0, w0) = step(0, parts, edges, [r0])
    more_edges, more_parts = share(sent, send)
    edges, parts = edges + more_edges, parts + more_parts
    sent, send, (r1, z1, w1) = step(1, parts, edges, [r0, w0, z0])
    more_edges, more_parts = share(sent, send)
    edges, parts = edges + more_edges, parts + more_parts
    _, send, kept = step(2, parts, edges, [r1, w1, w0, z1, z0])
    parts = parts + [exchange(send)]
    return tuple(
        call(
            final_kernel,
            tag("hbm", [field, field]),
            like([field, field]) + [semaphores(4)],
            tag("vmem", parts[1:]) + tag("kept", kept),
        )
    )


def solution(mesh):
    placed = (
        P("gz", "gy", None),
        P("gz", "gy", None),
        P("gz", "gy", None),
        P("gz", "gy", None),
        P(("gz", "gy"), None),
    )
    return jax.shard_map(
        solve,
        mesh=mesh,
        in_specs=placed,
        out_specs=(P("gz", "gy", None), P("gz", "gy", None)),
        check_vma=False,
    )
```

```python
import math
from functools import partial

import jax
import jax.numpy as jnp
from jax import lax
from jax.experimental import pallas as pl
from jax.experimental.pallas import tpu as pltpu
from jax.sharding import PartitionSpec as P


S_DEV = 4
B_DEV = 16
SPAN = S_DEV + B_DEV
LANES = 128
GROUPS = 4
CODES = GROUPS * B_DEV
REGIONS = S_DEV + 3 * B_DEV
SCALARS = 96
DEPTH = 3
PIECE = 16

surface_tension = 0.5
shift_term = 0.05
gas_drop = 0.75
norm_floor = 0.25
highest = lax.Precision.HIGHEST
f32 = jnp.float32
i32 = jnp.int32
i8 = jnp.int8
bf16 = jnp.bfloat16


def iota(shape, dim):
    return lax.broadcasted_iota(i32, shape, dim)


def up_rows(field):
    return pltpu.roll(field, field.shape[0] - 1, 0)


def down_rows(field):
    return pltpu.roll(field, 1, 0)


def next_x(field):
    return pltpu.roll(field, field.shape[1] - 1, 1)


def prev_x(field):
    return pltpu.roll(field, 1, 1)


def total(field):
    rows, width = field.shape
    folded = field[:, :LANES]
    for start in range(LANES, width, LANES):
        folded = folded + field[:, start : start + LANES]
    return jnp.sum(folded.reshape(rows // 8, 8, LANES), axis=0)


def digits(code):
    forms = []
    rest = code.astype(f32).astype(bf16)
    bits = []
    for power in (32, 16, 8, 4, 2, 1):
        bit = rest if power == 1 else jnp.clip(rest - (power - 1), 0, 1)
        bits.append(bit)
        rest = rest - power * bit
    for high, low in zip(bits[::2], bits[1::2]):
        no_high, no_low = 1 - high, 1 - low
        forms.append([no_high * no_low, no_high * low, high * no_low, high * low])
    return forms


def piece_sums(values, code):
    groups, outer, inner = digits(code)
    high = values.astype(bf16)
    low = (values - high.astype(f32)).astype(bf16)
    left = [group * part for part in (high, low) for group in groups]
    right = [first * second for first in outer for second in inner]
    return lax.dot_general(
        jnp.concatenate(left, axis=0),
        jnp.concatenate(right, axis=0),
        (((1,), (1,)), ((), ())),
        preferred_element_type=f32,
    )


def region_row(value_ref, code_ref):
    planes, rows, _ = value_ref.shape

    def step(plane, acc):
        code = code_ref[plane].astype(i32)
        for start in range(0, rows, PIECE):
            acc = acc + piece_sums(value_ref[plane, start : start + PIECE, :], code[start : start + PIECE])
        return acc

    acc = lax.fori_loop(
        0, planes, step, jnp.zeros((2 * GROUPS * PIECE, B_DEV * PIECE), f32), unroll=planes
    )
    shape = acc.shape
    kept = jnp.where(iota(shape, 0) % PIECE == iota(shape, 1) % PIECE, acc, 0.0)
    folded = jnp.sum(kept.reshape(2 * GROUPS, PIECE, shape[1]), axis=1)
    shape = (shape[1], LANES)
    pick = jnp.where(iota(shape, 0) // PIECE == iota(shape, 1) % B_DEV, 1.0, 0.0)
    spread = jnp.dot(folded, pick, precision=highest, preferred_element_type=f32)
    shape = spread.shape
    lane = iota(shape, 1)
    mine = (iota(shape, 0) % GROUPS == lane // B_DEV) & (lane < CODES)
    return jnp.sum(jnp.where(mine, spread, 0.0), axis=0, keepdims=True)


def scalar_row(scalars):
    lane = iota((1, LANES), 1)
    row = jnp.zeros((1, LANES), f32)
    for index, value in enumerate(scalars):
        row = jnp.where(lane == SCALARS + index, value, row)
    return row


def lane_of(row, index):
    return jnp.sum(jnp.where(iota(row.shape, 1) == SCALARS + index, row, 0.0))


def lookup(table, index):
    rows, width = index.shape
    wide = jnp.broadcast_to(table, (rows, LANES))
    return jnp.concatenate(
        [
            jnp.take_along_axis(wide, index[:, start : start + LANES], axis=1)
            for start in range(0, width, LANES)
        ],
        axis=1,
    )


class Place:
    def __init__(self):
        slab, column = lax.axis_index("gz"), lax.axis_index("gy")
        slabs, columns = lax.axis_size("gz"), lax.axis_size("gy")
        here = slab * columns + column
        self.first_z, self.last_z = slab == 0, slab == slabs - 1
        self.first_y, self.last_y = column == 0, column == columns - 1
        self.base, self.stride, self.sub_base = here * B_DEV, columns * B_DEV, here * S_DEV
        self.even_z, self.even_y = slab % 2 == 0, column % 2 == 0


def start_all(copies):
    @pl.when(lax.axis_index("gz") >= 0)
    def _():
        for copy in copies:
            copy.start()


def wait_all(copies):
    for copy in copies:
        copy.wait()


def coarse_parts(row, dest_ref):
    wide = jnp.broadcast_to(row, (8, LANES))

    def step(region, acc):
        lane = jnp.where(region < S_DEV, region, region + B_DEV - S_DEV)
        factor = jnp.take_along_axis(wide, jnp.full((8, LANES), lane, i32), axis=1)[0:1, :]
        return acc + factor * dest_ref[region]

    small = dest_ref.shape[1] <= 64
    return lax.fori_loop(0, REGIONS, step, jnp.zeros(dest_ref.shape[1:], f32), unroll=REGIONS if small else 4)


def destinations_kernel(columns, own_ref, near_ref, far_ref, dest_hbm, wide_ref, dest_ref, sems):
    devices = own_ref.shape[1]
    even_z = Place().even_z
    wide_ref[...] = jnp.zeros(wide_ref.shape, f32)
    low_start = pl.multiple_of(jnp.where(even_z, 2 * B_DEV, 0), B_DEV) + S_DEV
    high_start = pl.multiple_of(jnp.where(even_z, 0, 2 * B_DEV), B_DEV) + S_DEV
    wide_ref[0:S_DEV, :, 0:SPAN] = own_ref[0:S_DEV]
    wide_ref[S_DEV + B_DEV : S_DEV + 2 * B_DEV, :, 0:SPAN] = own_ref[S_DEV:SPAN]
    wide_ref[pl.ds(low_start, B_DEV), :, 0:SPAN] = near_ref[...]
    wide_ref[pl.ds(high_start, B_DEV), :, 0:SPAN] = far_ref[...]
    lane = iota((devices, LANES), 1)

    def place(base, shift, first, count):
        moved = pltpu.roll(base, shift, 1) if shift else base
        return jnp.where((lane >= first) & (lane < first + count), moved, 0.0)

    def from_device(field, step):
        return pltpu.roll(field, (-step) % devices, 0) if step % devices else field

    def one(region, carry):
        base = wide_ref[region]
        bubbles = B_DEV - S_DEV
        table = place(base, 0, 0, S_DEV) + place(base, B_DEV + bubbles, 2 * B_DEV, B_DEV)
        table = table + from_device(
            place(base, S_DEV, S_DEV, S_DEV) + place(base, 2 * B_DEV + bubbles, 3 * B_DEV, B_DEV), columns
        )
        table = table + from_device(
            place(base, 2 * S_DEV, 2 * S_DEV, S_DEV) + place(base, bubbles, B_DEV, B_DEV), -columns
        )
        table = table + from_device(place(base, 3 * S_DEV, 3 * S_DEV, S_DEV), 1)
        table = table + from_device(place(base, 3 * B_DEV + bubbles, 4 * B_DEV, B_DEV), 2 * columns)
        table = table + from_device(place(base, 4 * B_DEV + bubbles, 5 * B_DEV, B_DEV), -2 * columns)
        own_codes = jnp.where((lane < S_DEV) | ((lane >= B_DEV) & (lane < CODES)), table, 0.0)
        dest_ref[region, pl.ds(0, devices, stride=2), :] = table
        dest_ref[region, pl.ds(1, devices, stride=2), :] = from_device(own_codes, -1)
        return carry

    lax.fori_loop(0, REGIONS, one, 0, unroll=4)
    write = pltpu.make_async_copy(dest_ref, dest_hbm, sems.at[0])
    write.start()
    write.wait()


def write_edges(even_z, even_y, value_ref, z_refs, y_refs, convert=lambda value: value):
    planes, rows, _ = value_ref.shape
    z_refs[0][...] = convert(value_ref[jnp.where(even_z, planes - 1, 0)])
    z_refs[1][...] = convert(value_ref[jnp.where(even_z, 0, planes - 1)])
    for plane in range(planes):
        first = convert(value_ref[plane, 0:1, :])
        last = convert(value_ref[plane, rows - 1 : rows, :])
        y_refs[0][plane : plane + 1, :] = jnp.where(even_y, last, first)
        y_refs[1][plane : plane + 1, :] = jnp.where(even_y, first, last)


def slices_kernel(frac_hbm, coarse_hbm, z0_ref, z1_ref, y0_ref, y1_ref, bubble_ref, frac_ref, coarse_ref, sems):
    planes, rows, _ = frac_ref.shape
    copies = [
        pltpu.make_async_copy(frac_hbm, frac_ref, sems.at[0]),
        pltpu.make_async_copy(coarse_hbm, coarse_ref, sems.at[1]),
    ]
    start_all(copies)
    place = Place()
    even_z, even_y = place.even_z, place.even_y
    wait_all(copies)
    bubble_ref[...] = coarse_ref[S_DEV:SPAN, :]
    z0_ref[...] = frac_ref[pl.ds(jnp.where(even_z, planes - DEPTH, 0), DEPTH)]
    z1_ref[...] = frac_ref[pl.ds(jnp.where(even_z, 0, planes - DEPTH), DEPTH)]
    first, last = frac_ref[:, 0:DEPTH, :], frac_ref[:, rows - DEPTH : rows, :]
    y0_ref[...] = jnp.where(even_y, last, first)
    y1_ref[...] = jnp.where(even_y, first, last)


def setup_kernel(
    z0_in, z1_in, y0_in, y1_in, k0_in, k1_in, frac_hbm, source_hbm, label_hbm, sub_hbm, dest_hbm,
    ez0_ref, ez1_ref, ey0_ref, ey1_ref, send_ref,
    code_ref, cz_ref, cy_ref, cx_ref, inv_ref, south_ref, r_hbm, diag_hbm,
    frac_ref, source_ref, label_ref, sub_ref, dest_ref, r_ref, diag_ref, b_ref,
    deep_ref, nz_ref, flat_ref, kap_ref, fz_ref, work_ref, in_sems, out_sems,
):
    planes, rows, width = frac_ref.shape
    tall = rows + 8
    place = Place()
    first_z, last_z, first_y, last_y = place.first_z, place.last_z, place.first_y, place.last_y
    base, stride, sub_base = place.base, place.stride, place.sub_base
    even_z, even_y = place.even_z, place.even_y
    pairs = [(frac_hbm, frac_ref), (label_hbm, label_ref), (sub_hbm, sub_ref), (source_hbm, source_ref), (dest_hbm, dest_ref)]
    reads = [pltpu.make_async_copy(a, b, in_sems.at[i]) for i, (a, b) in enumerate(pairs)]
    start_all(reads)
    row = iota((tall, width), 0)
    lane = iota((tall, width), 1)
    inside_y = ((row < rows) | ((row < rows + 4) & jnp.logical_not(last_y))) | (
        (row >= rows + 4) & jnp.logical_not(first_y)
    )
    first_plane = jnp.where(first_z, 0, -planes)
    last_plane = jnp.where(last_z, planes, 2 * planes)

    def right_of(field):
        moved = next_x(field)
        tile = lane[: field.shape[0], :LANES]
        ended = jnp.where(tile == LANES - 1, 0.0, moved[:, width - LANES :])
        return jnp.concatenate([moved[:, : width - LANES], ended], axis=1)

    def left_of(field):
        moved = prev_x(field)
        tile = lane[: field.shape[0], :LANES]
        return jnp.concatenate([jnp.where(tile == 0, 0.0, moved[:, :LANES]), moved[:, LANES:]], axis=1)

    deep_ref[:, rows:tall, :] = jnp.zeros((planes + 2 * DEPTH, 8, width), f32)
    near_z = jnp.where(even_z, planes + DEPTH, 0)
    far_z = jnp.where(even_z, 0, planes + DEPTH)
    out_near, out_far = jnp.where(even_z, last_z, first_z), jnp.where(even_z, first_z, last_z)
    deep_ref[pl.ds(near_z, DEPTH), 0:rows, :] = jnp.where(out_near, 0.0, z0_in[...])
    deep_ref[pl.ds(far_z, DEPTH), 0:rows, :] = jnp.where(out_far, 0.0, z1_in[...])
    high, low = slice(rows, rows + DEPTH), slice(tall - DEPTH, tall)

    def fill_rows(first, second, out_first, out_second):
        deep_ref[DEPTH : planes + DEPTH, first, :] = jnp.where(out_first, 0.0, y0_in[...])
        deep_ref[DEPTH : planes + DEPTH, second, :] = jnp.where(out_second, 0.0, y1_in[...])
        for start, corner, out in ((near_z, k0_in, out_near), (far_z, k1_in, out_far)):
            deep_ref[pl.ds(start, DEPTH), first, :] = jnp.where(out | out_first, 0.0, corner[0])
            deep_ref[pl.ds(start, DEPTH), second, :] = jnp.where(out | out_second, 0.0, corner[1])

    @pl.when(even_y)
    def _():
        fill_rows(high, low, last_y, first_y)

    @pl.when(jnp.logical_not(even_y))
    def _():
        fill_rows(low, high, first_y, last_y)

    reads[0].wait()
    deep_ref[DEPTH : planes + DEPTH, 0:rows, :] = frac_ref[...]

    def normal_plane(index, carry):
        keep = (index - 2 >= first_plane) & (index - 2 < last_plane)
        here = deep_ref[index + 1]
        gz = deep_ref[index + 2] - deep_ref[index]
        gy = up_rows(here) - down_rows(here)
        gx = right_of(here) - left_of(here)
        scale = jnp.minimum(lax.rsqrt(gz * gz + gy * gy + gx * gx), 0.5 / norm_floor)
        scale = jnp.where(inside_y & keep, scale, 0.0)
        ny = gy * scale
        nx = gx * scale
        nz_ref[index] = gz * scale
        flat_ref[index] = (up_rows(ny) - down_rows(ny)) + (right_of(nx) - left_of(nx))
        return carry

    lax.fori_loop(0, planes + 4, normal_plane, 0, unroll=2)

    def kappa_plane(index, carry):
        keep = (index - 1 >= first_plane) & (index - 1 < last_plane)
        value = -0.5 * ((nz_ref[index + 2] - nz_ref[index]) + flat_ref[index + 1])
        kap_ref[index] = jnp.where(inside_y & keep, value, 0.0)
        return carry

    lax.fori_loop(0, planes + 2, kappa_plane, 0)
    mid = pl.ds(0, rows)

    def z_face(index, carry):
        f_low = deep_ref[index + 2, mid, :]
        f_high = deep_ref[index + 3, mid, :]
        coef = 2.0 * pl.reciprocal((1.0 - gas_drop * f_low) + (1.0 - gas_drop * f_high))
        cz_ref[index] = coef
        mean = 0.5 * (kap_ref[index, mid, :] + kap_ref[index + 1, mid, :])
        fz_ref[index] = coef * mean * (f_high - f_low)
        return carry

    lax.fori_loop(0, planes + 1, z_face, 0)
    row_mid = row[:rows]
    lane_mid = lane[:rows]
    wait_all(reads[1:])

    def assemble_plane(plane, carry):
        inv_before, g_before = carry
        f = deep_ref[plane + 3]
        k = kap_ref[plane + 1]
        d = 1.0 - gas_drop * f
        f_up = up_rows(f)
        cy = 2.0 * pl.reciprocal(d + (1.0 - gas_drop * f_up))
        fy = cy * (0.5 * (k + up_rows(k))) * (f_up - f)
        cyp, cym = cy[:rows], down_rows(cy)[:rows]
        sum_y = fy[:rows] - down_rows(fy)[:rows]
        f, k, d = f[:rows], k[:rows], d[:rows]
        f_right = right_of(f)
        cxp = 2.0 * pl.reciprocal(d + (1.0 - gas_drop * f_right))
        fx = cxp * (0.5 * (k + right_of(k))) * (f_right - f)
        outer = jnp.concatenate([2.0 / (d[:, :LANES] + 1.0), jnp.zeros((rows, width - LANES), f32)], axis=1)
        cxm = jnp.where(lane_mid == 0, outer, prev_x(cxp))
        fx_before = jnp.where(lane_mid == 0, outer * (0.5 * k) * f, prev_x(fx))
        terms = fz_ref[plane + 1] - fz_ref[plane] + sum_y + (fx - fx_before)
        rhs = source_ref[plane] - surface_tension * terms
        down = cz_ref[plane]
        diagonal = shift_term + (cz_ref[plane + 1] + down + cyp + cym + cxp + cxm)
        mult = down * inv_before
        inv = pl.reciprocal(diagonal - mult * down)
        g = rhs + mult * g_before
        r_ref[plane] = rhs
        diag_ref[plane] = diagonal
        inv_ref[plane] = inv
        work_ref[plane] = g
        cy_ref[plane] = jnp.where((row_mid == rows - 1) & last_y, 0.0, cyp)
        south_ref[pl.ds(plane, 1), :] = jnp.where(first_y, 0.0, cym[0:1, :])
        cx_ref[plane] = jnp.where(lane_mid == width - 1, 0.0, cxp)
        label = label_ref[plane]
        offset = label - base
        below = offset < 0
        above = offset >= stride
        group = jnp.where(below, 1, jnp.where(above, 3, 2))
        inner = jnp.where(below, offset + stride, jnp.where(above, offset - stride, offset))
        code = jnp.where(label >= 0, group * B_DEV + inner, sub_ref[plane] - sub_base)
        code_ref[plane] = (code & (CODES - 1)).astype(i8)
        return (inv, g)

    blank = jnp.zeros((rows, width), f32)
    lax.fori_loop(0, planes, assemble_plane, (blank, blank))

    def backward(step, after):
        plane = planes - 1 - step
        value = (work_ref[plane] + cz_ref[plane + 1] * after) * inv_ref[plane]
        b_ref[plane] = value
        return value

    lax.fori_loop(0, planes, backward, blank)
    cz_ref[0] = jnp.where(first_z, 0.0, cz_ref[0])
    cz_ref[planes] = jnp.where(last_z, 0.0, cz_ref[planes])
    writes = [
        pltpu.make_async_copy(r_ref, r_hbm, out_sems.at[0]), pltpu.make_async_copy(diag_ref, diag_hbm, out_sems.at[1])
    ]
    start_all(writes)
    write_edges(even_z, even_y, b_ref, [ez0_ref.at[0], ez1_ref.at[0]], [ey0_ref.at[0], ey1_ref.at[0]])
    for plane in range(planes):
        label_ref[plane] = code_ref[plane].astype(i32)
    write_edges(
        even_z, even_y, label_ref, [ez0_ref.at[1], ez1_ref.at[1]], [ey0_ref.at[1], ey1_ref.at[1]],
        convert=lambda value: value.astype(f32),
    )
    send_ref[...] = coarse_parts(region_row(r_ref, code_ref), dest_ref)
    wait_all(writes)


def table_rows(parts):
    folded = jnp.sum(parts.reshape(parts.shape[0] // 8, 8, LANES), axis=0)
    even = iota(folded.shape, 0) % 2 == 0
    return jnp.concatenate(
        [
            jnp.sum(jnp.where(even, folded, 0.0), axis=0, keepdims=True),
            jnp.sum(jnp.where(even, 0.0, folded), axis=0, keepdims=True),
        ],
        axis=0,
    )


def scalars_of(sums):
    alphas, betas, curves = [], [None], []
    for step, row in enumerate(sums):
        gamma = lane_of(row, 0)
        if step == 0:
            curve = lane_of(row, 1)
        else:
            beta = gamma / lane_of(sums[step - 1], 0)
            betas.append(beta)
            curve = lane_of(row, 1) + beta * (lane_of(row, 2) + beta * curves[-1])
        curves.append(curve)
        alphas.append(gamma / curve)
    return alphas, betas


def step_kernel(stage, *refs):
    refs = list(refs)

    def take(count):
        out = refs[:count]
        del refs[:count]
        return out

    parts = take(stage + 1)
    halos = [take(4) for _ in range(stage + 1)]
    code_ref, cz_ref, cy_ref, cx_ref, inv_ref, south_ref = take(6)
    last = stage == 2
    names = (("r",), ("r", "w0", "z0"), ("r", "w1", "w0", "z1", "z0"))[stage] + (("diag",) if last else ("diag", "dest"))
    sources = dict(zip(names, take(len(names))))
    out_names = (("z", "w"), ("rn", "z", "w"), ("rn", "s", "p", "z", "w"))[stage]
    if not last:
        edges_z, edges_y = take(2), take(2)
    (send_ref,) = take(1)
    if last:
        pad_ref, w_ref, *others = take(6)
        made = dict(zip(("rn", "s", "p", "x"), others))
        out_names = ()
        held = dict(zip(names, take(len(names))))
        side_ref, work_ref, in_sems = take(3)
        out_sems = None
    else:
        sinks = dict(zip(out_names, take(len(out_names))))
        held = dict(zip(names, take(len(names))))
        pad_ref, side_ref, work_ref, w_ref = take(4)
        made = {"z": pad_ref.at[pl.ds(1, pad_ref.shape[0] - 2)], "w": w_ref}
        for name in out_names[:-2]:
            (made[name],) = take(1)
        u_ref, in_sems, out_sems = take(3)

    reads = {name: pltpu.make_async_copy(sources[name], held[name], in_sems.at[i]) for i, name in enumerate(names)}
    start_all(reads.values())
    writes = {name: pltpu.make_async_copy(made[name], sinks[name], out_sems.at[i]) for i, name in enumerate(out_names)}
    planes, rows, width = code_ref.shape
    place = Place()
    even_z, even_y = place.even_z, place.even_y

    sums = [table_rows(part[...]) for part in parts]
    alphas, betas = scalars_of([row[0:1] for row in sums[1:]])
    table = sums[0]
    if stage >= 1:
        table = table - alphas[0] * sums[1]
    if stage == 2:
        table = table - alphas[1] * (sums[2] + betas[1] * sums[1])
    near, side = table[0:1], table[1:2]

    def combine(values):
        out = values[0]
        if stage >= 1:
            out = out - alphas[0] * values[1]
        if stage == 2:
            out = out - alphas[1] * (values[2] + betas[1] * values[1])
        return out

    for slot in range(2):
        upper = even_z if slot == 0 else jnp.logical_not(even_z)
        index = halos[0][slot][1].astype(i32)
        high = jnp.where(index < B_DEV, index + S_DEV, index + B_DEV)
        low = jnp.where(
            index < B_DEV, index + 2 * S_DEV, jnp.where(index < 2 * B_DEV, index + 4 * B_DEV, index - B_DEV)
        )
        block = combine([halos[0][slot][0]] + [halo[slot][...] for halo in halos[1:]])
        pad_ref[jnp.where(upper, planes + 1, 0)] = block + lookup(near, jnp.where(upper, high, low))
        upper = even_y if slot == 0 else jnp.logical_not(even_y)
        index = halos[0][2 + slot][1].astype(i32)
        block = combine([halos[0][2 + slot][0]] + [halo[2 + slot][...] for halo in halos[1:]])
        found = jnp.where(
            upper, lookup(near, (index & (B_DEV - 1)) + 3 * S_DEV), lookup(side, index)
        )
        side_ref[jnp.where(upper, 1, 0)] = block + found

    early = tuple(name for name in names if name[0] in "rw")
    for name in early:
        reads[name].wait()
    empty = jnp.zeros((rows, width), f32)

    def residual(plane, before):
        value = held["r"][plane]
        if stage == 1:
            value = value - alphas[0] * held["w0"][plane]
            made["rn"][plane] = value
        if stage == 2:
            image = held["w1"][plane] + betas[1] * held["w0"][plane]
            made["s"][plane] = image
            value = value - alphas[1] * image
            made["rn"][plane] = value
        value = value + cz_ref[plane] * before
        work_ref[plane] = value
        return value * inv_ref[plane]

    lax.fori_loop(0, planes, residual, empty)
    start_all([writes[name] for name in out_names[:-2]])

    def direction(step, after):
        plane = planes - 1 - step
        value = (work_ref[plane] + cz_ref[plane + 1] * after) * inv_ref[plane]
        pad_ref[plane + 1] = value + lookup(near, code_ref[plane].astype(i32))
        return value

    lax.fori_loop(0, planes, direction, empty)
    if not last:
        writes["z"].start()
    for name in names:
        if name not in early and name != "dest":
            reads[name].wait()
    row = iota((rows, width), 0)

    def image_plane(plane, carry):
        sums, before = carry
        here = pad_ref[plane + 1]
        cy, cx = cy_ref[plane], cx_ref[plane]
        north = jnp.where(row == rows - 1, side_ref[1, pl.ds(plane, 1), :], up_rows(here))
        below = south_ref[pl.ds(plane, 1), :] * side_ref[0, pl.ds(plane, 1), :]
        south = jnp.where(row == 0, below, down_rows(cy * here))
        image = held["diag"][plane] * here - (
            cz_ref[plane + 1] * pad_ref[plane + 2]
            + cz_ref[plane] * pad_ref[plane]
            + (cy * north + south)
            + (cx * next_x(here) + prev_x(cx * here))
        )
        w_ref[plane] = image
        new = made["rn"] if stage else held["r"]
        found = [total(new[plane] * here), total(here * image)]
        if stage == 1:
            found.append(total(here * held["w0"][plane] + held["z0"][plane] * image))
        if stage == 2:
            along = held["z1"][plane] + betas[1] * held["z0"][plane]
            made["p"][plane] = along
            made["x"][plane] = alphas[0] * held["z0"][plane] + alphas[1] * along
            found.append(total(here * made["s"][plane] + along * image))
        if not last:
            before = image + cz_ref[plane] * before
            work_ref[plane] = before
            before = before * inv_ref[plane]
        return tuple(old + new for old, new in zip(sums, found)), before

    blank = jnp.zeros((8, LANES), f32)
    dots, _ = lax.fori_loop(
        0, planes, image_plane, ((blank,) * (3 if stage else 2), blank if last else empty), unroll=2
    )
    if not last:
        writes["w"].start()
    row = scalar_row([jnp.sum(value) for value in dots])
    if last:
        send_ref[...] = jnp.broadcast_to(row, send_ref.shape)
    else:

        def backward(step, after):
            plane = planes - 1 - step
            value = (work_ref[plane] + cz_ref[plane + 1] * after) * inv_ref[plane]
            u_ref[plane] = value
            return value

        lax.fori_loop(0, planes, backward, empty)
        write_edges(even_z, even_y, u_ref, edges_z, edges_y)
        reads["dest"].wait()
        parts = coarse_parts(region_row(w_ref, code_ref), held["dest"])
        send_ref[...] = parts + jnp.where(iota(parts.shape, 0) % 2 == 0, row, 0.0)
    wait_all(writes.values())


def final_kernel(
    d0_ref, d1_ref, d2_ref, z_ref, w_ref, r_ref, s_ref, p_ref, part_ref, x_out, r_out, x_new, r_new, sems
):
    sums = [table_rows(d0_ref[...])[0:1], table_rows(d1_ref[...])[0:1], jnp.sum(d2_ref[...], axis=0, keepdims=True)]
    alphas, betas = scalars_of(sums)
    mixed = alphas[2] * betas[2]
    planes = r_ref.shape[0]
    writes = []
    for half in range(2):
        low, high = half * planes // 2, (half + 1) * planes // 2
        x_new[low:high] = part_ref[low:high] + alphas[2] * z_ref[low + 1 : high + 1] + mixed * p_ref[low:high]
        r_new[low:high] = r_ref[low:high] - alphas[2] * w_ref[low:high] - mixed * s_ref[low:high]
        piece = pl.ds(low, high - low)
        pairs = [(x_new.at[piece], x_out.at[piece]), (r_new.at[piece], r_out.at[piece])]
        copies = [pltpu.make_async_copy(a, b, sems.at[2 * half + i]) for i, (a, b) in enumerate(pairs)]
        start_all(copies)
        writes += copies
    wait_all(writes)


def call(kernel, outs, scratch, args):
    spaces = {"smem": pltpu.SMEM, "vmem": pltpu.VMEM, "kept": pltpu.VMEM, "hbm": pltpu.HBM}

    def specs(items):
        return [pl.BlockSpec(memory_space=spaces[space]) for space, _ in items]

    held = sum(4 * math.prod(ref.shape) for ref in scratch)
    places = {"hbm": pltpu.HBM, "kept": pltpu.VMEM}
    made = [places[space](out.shape, out.dtype) if space in places else out for space, out in outs]
    operands = [
        pltpu.with_memory_space_constraint(value, places[space]) if space in places else value for space, value in args
    ]
    return pl.pallas_call(
        kernel,
        out_shape=made,
        in_specs=specs(args),
        out_specs=specs(outs),
        scratch_shapes=scratch,
        compiler_params=pltpu.CompilerParams(vmem_limit_bytes=held + 12 * 1024 * 1024),
    )(*operands)


def swaps(axis, first):
    count = lax.axis_size(axis)
    pairs = []
    for i in range(first, count + first, 2):
        low, high = i % count, (i + 1) % count
        pairs += [(low, high), (high, low)]
    return pairs


def swap(block, axis, first):
    return lax.ppermute(block, axis, swaps(axis, first))


def solve(fraction, source, bubble_label, subdomain, coarse_inverse):
    planes, rows, width = fraction.shape
    slabs = lax.axis_size("gz")
    columns = lax.axis_size("gy")
    devices = slabs * columns
    slab = lax.axis_index("gz")
    even_z = slab % 2 == 0
    field = jax.ShapeDtypeStruct((planes, rows, width), f32)

    def shape(*dims, dtype=f32):
        return jax.ShapeDtypeStruct(dims, dtype)

    def vmem(*dims, dtype=f32):
        return pltpu.VMEM(dims, dtype)

    def like(items):
        return [vmem(*value.shape, dtype=value.dtype) for value in items]

    def semaphores(count):
        return pltpu.SemaphoreType.DMA((count,))

    def tag(space, items):
        return [(space, item) for item in items]

    top, bottom, *sides, bubbles = call(
        slices_kernel,
        tag("vmem", [shape(DEPTH, rows, width)] * 2 + [shape(planes, DEPTH, width)] * 2 + [shape(B_DEV, devices * SPAN)]),
        [vmem(planes, rows, width), vmem(SPAN, devices * SPAN), semaphores(2)],
        tag("hbm", [fraction, coarse_inverse]),
    )
    coarse_in = [swap(bubbles, "gz", 0), swap(bubbles, "gz", 1)]
    y_in = [swap(sides[0], "gy", 0), swap(sides[1], "gy", 1)]
    z_in = [swap(top, "gz", 0), swap(bottom, "gz", 1)]
    corner = jnp.stack(y_in)
    corner_top = jnp.where(even_z, corner[:, planes - DEPTH :], corner[:, :DEPTH])
    corner_bottom = jnp.where(even_z, corner[:, :DEPTH], corner[:, planes - DEPTH :])
    corner_in = [swap(corner_top, "gz", 0), swap(corner_bottom, "gz", 1)]

    def spread(matrix):
        return matrix.reshape(matrix.shape[0], devices, SPAN)

    dest_shape = shape(REGIONS, 2 * devices, LANES)
    spread_in = [spread(m) for m in [coarse_inverse] + coarse_in]
    (dest,) = call(
        partial(destinations_kernel, columns),
        tag("hbm", [dest_shape]),
        [vmem(REGIONS, devices, LANES)] + like([dest_shape]) + [semaphores(1)],
        tag("vmem", spread_in),
    )
    codes = shape(planes, rows, width, dtype=i8)
    faces = shape(planes + 1, rows, width)
    inputs = [fraction, source, bubble_label, subdomain, dest]
    tall = rows + 8
    wide = shape(2 * devices, LANES)
    first_edges = [shape(2, rows, width)] * 2 + [shape(2, planes, width)] * 2
    later_edges = [shape(rows, width)] * 2 + [shape(planes, width)] * 2
    outs = tag("vmem", first_edges + [wide])
    outs += tag("kept", [codes, faces, field, field, field, shape(planes, width)]) + tag("hbm", [field, field])
    *sent, send, code, cz, cy, cx, inv, south, r0, diag = call(
        setup_kernel,
        outs,
        like(inputs)
        + like([field, field, field])
        + [
            vmem(planes + 2 * DEPTH, tall, width),
            vmem(planes + 4, tall, width),
            vmem(planes + 4, tall, width),
            vmem(planes + 2, tall, width),
            vmem(planes + 1, rows, width),
            vmem(planes, rows, width),
            semaphores(len(inputs)),
            semaphores(2),
        ],
        tag("vmem", z_in + y_in + corner_in) + tag("hbm", inputs),
    )
    matrix = [code, cz, cy, cx, inv, south]

    def exchange(parts):
        blocks = parts.reshape(devices, -1, LANES)
        return lax.all_to_all(blocks, ("gz", "gy"), 0, 0).reshape(parts.shape)

    def share(sent, send):
        edges = [swap(sent[0], "gz", 0), swap(sent[1], "gz", 1)]
        edges += [swap(sent[2], "gy", 0), swap(sent[3], "gy", 1)]
        parts = [exchange(send)]
        return edges, parts

    def step(stage, parts, edges, state):
        last = stage == 2
        operands = state + ([diag] if last else [diag, dest])
        tall_field = shape(planes + 2, rows, width)
        sides = vmem(2, planes, width)
        if last:
            outs = tag("vmem", [shape(devices, LANES)]) + tag("kept", [tall_field] + [field] * 5)
            scratch = like(operands) + [sides] + like([field]) + [semaphores(len(operands))]
            count = 0
        else:
            fields = [field] * (2 + stage)
            outs = tag("vmem", later_edges + [wide]) + tag("hbm", fields)
            scratch = like(operands) + like([tall_field]) + [sides] + like([field] * (len(fields) + 1))
            scratch += [semaphores(len(operands)), semaphores(len(fields))]
            count = len(later_edges)
        results = call(
            partial(step_kernel, stage),
            outs,
            scratch,
            tag("vmem", parts + edges) + tag("kept", matrix) + tag("hbm", operands),
        )
        return results[:count], results[count], results[count + 1 :]

    edges, parts = share(sent, send)
    sent, send, (z0, w0) = step(0, parts, edges, [r0])
    more_edges, more_parts = share(sent, send)
    edges, parts = edges + more_edges, parts + more_parts
    sent, send, (r1, z1, w1) = step(1, parts, edges, [r0, w0, z0])
    more_edges, more_parts = share(sent, send)
    edges, parts = edges + more_edges, parts + more_parts
    _, send, kept = step(2, parts, edges, [r1, w1, w0, z1, z0])
    parts = parts + [exchange(send)]
    return tuple(
        call(
            final_kernel,
            tag("hbm", [field, field]),
            like([field, field]) + [semaphores(4)],
            tag("vmem", parts[1:]) + tag("kept", kept),
        )
    )


def solution(mesh):
    placed = (
        P("gz", "gy", None),
        P("gz", "gy", None),
        P("gz", "gy", None),
        P("gz", "gy", None),
        P(("gz", "gy"), None),
    )
    return jax.shard_map(
        solve,
        mesh=mesh,
        in_specs=placed,
        out_specs=(P("gz", "gy", None), P("gz", "gy", None)),
        check_vma=False,
    )
```

```python
import math
from functools import partial

import jax
import jax.numpy as jnp
from jax import lax
from jax.experimental import pallas as pl
from jax.experimental.pallas import tpu as pltpu
from jax.sharding import PartitionSpec as P


S_DEV = 4
B_DEV = 16
SPAN = S_DEV + B_DEV
LANES = 128
GROUPS = 4
CODES = GROUPS * B_DEV
REGIONS = S_DEV + 3 * B_DEV
SCALARS = 96
DEPTH = 3
PIECE = 16

surface_tension = 0.5
shift_term = 0.05
gas_drop = 0.75
norm_floor = 0.25
highest = lax.Precision.HIGHEST
f32 = jnp.float32
i32 = jnp.int32
i8 = jnp.int8
bf16 = jnp.bfloat16


def iota(shape, dim):
    return lax.broadcasted_iota(i32, shape, dim)


def up_rows(field):
    return pltpu.roll(field, field.shape[0] - 1, 0)


def down_rows(field):
    return pltpu.roll(field, 1, 0)


def next_x(field):
    return pltpu.roll(field, field.shape[1] - 1, 1)


def prev_x(field):
    return pltpu.roll(field, 1, 1)


def total(field):
    rows, width = field.shape
    folded = field[:, :LANES]
    for start in range(LANES, width, LANES):
        folded = folded + field[:, start : start + LANES]
    return jnp.sum(folded.reshape(rows // 8, 8, LANES), axis=0)


def digits(code):
    forms = []
    rest = code.astype(f32).astype(bf16)
    bits = []
    for power in (32, 16, 8, 4, 2, 1):
        bit = rest if power == 1 else jnp.clip(rest - (power - 1), 0, 1)
        bits.append(bit)
        rest = rest - power * bit
    for high, low in zip(bits[::2], bits[1::2]):
        no_high, no_low = 1 - high, 1 - low
        forms.append([no_high * no_low, no_high * low, high * no_low, high * low])
    return forms


def piece_sums(values, code):
    groups, outer, inner = digits(code)
    high = values.astype(bf16)
    low = (values - high.astype(f32)).astype(bf16)
    left = [group * part for part in (high, low) for group in groups]
    right = [first * second for first in outer for second in inner]
    return lax.dot_general(
        jnp.concatenate(left, axis=0),
        jnp.concatenate(right, axis=0),
        (((1,), (1,)), ((), ())),
        preferred_element_type=f32,
    )


def region_row(value_ref, code_ref):
    planes, rows, _ = value_ref.shape

    def step(plane, acc):
        code = code_ref[plane].astype(i32)
        for start in range(0, rows, PIECE):
            acc = acc + piece_sums(value_ref[plane, start : start + PIECE, :], code[start : start + PIECE])
        return acc

    acc = lax.fori_loop(
        0, planes, step, jnp.zeros((2 * GROUPS * PIECE, B_DEV * PIECE), f32), unroll=planes
    )
    shape = acc.shape
    kept = jnp.where(iota(shape, 0) % PIECE == iota(shape, 1) % PIECE, acc, 0.0)
    folded = jnp.sum(kept.reshape(2 * GROUPS, PIECE, shape[1]), axis=1)
    shape = (shape[1], LANES)
    pick = jnp.where(iota(shape, 0) // PIECE == iota(shape, 1) % B_DEV, 1.0, 0.0)
    spread = jnp.dot(folded, pick, precision=highest, preferred_element_type=f32)
    shape = spread.shape
    lane = iota(shape, 1)
    mine = (iota(shape, 0) % GROUPS == lane // B_DEV) & (lane < CODES)
    return jnp.sum(jnp.where(mine, spread, 0.0), axis=0, keepdims=True)


def scalar_row(scalars):
    lane = iota((1, LANES), 1)
    row = jnp.zeros((1, LANES), f32)
    for index, value in enumerate(scalars):
        row = jnp.where(lane == SCALARS + index, value, row)
    return row


def lane_of(row, index):
    return jnp.sum(jnp.where(iota(row.shape, 1) == SCALARS + index, row, 0.0))


def lookup(table, index):
    rows, width = index.shape
    wide = jnp.broadcast_to(table, (rows, LANES))
    return jnp.concatenate(
        [
            jnp.take_along_axis(wide, index[:, start : start + LANES], axis=1)
            for start in range(0, width, LANES)
        ],
        axis=1,
    )


class Place:
    def __init__(self):
        slab, column = lax.axis_index("gz"), lax.axis_index("gy")
        slabs, columns = lax.axis_size("gz"), lax.axis_size("gy")
        here = slab * columns + column
        self.first_z, self.last_z = slab == 0, slab == slabs - 1
        self.first_y, self.last_y = column == 0, column == columns - 1
        self.base, self.stride, self.sub_base = here * B_DEV, columns * B_DEV, here * S_DEV
        self.even_z, self.even_y = slab % 2 == 0, column % 2 == 0


def start_all(copies):
    @pl.when(lax.axis_index("gz") >= 0)
    def _():
        for copy in copies:
            copy.start()


def wait_all(copies):
    for copy in copies:
        copy.wait()


def coarse_parts(row, dest_ref):
    wide = jnp.broadcast_to(row, (8, LANES))

    def step(region, acc):
        lane = jnp.where(region < S_DEV, region, region + B_DEV - S_DEV)
        factor = jnp.take_along_axis(wide, jnp.full((8, LANES), lane, i32), axis=1)[0:1, :]
        return acc + factor * dest_ref[region]

    small = dest_ref.shape[1] <= 64
    return lax.fori_loop(0, REGIONS, step, jnp.zeros(dest_ref.shape[1:], f32), unroll=REGIONS if small else 4)


def destinations_kernel(columns, own_ref, near_ref, far_ref, dest_hbm, wide_ref, dest_ref, sems):
    devices = own_ref.shape[1]
    even_z = Place().even_z
    wide_ref[...] = jnp.zeros(wide_ref.shape, f32)
    low_start = pl.multiple_of(jnp.where(even_z, 2 * B_DEV, 0), B_DEV) + S_DEV
    high_start = pl.multiple_of(jnp.where(even_z, 0, 2 * B_DEV), B_DEV) + S_DEV
    wide_ref[0:S_DEV, :, 0:SPAN] = own_ref[0:S_DEV]
    wide_ref[S_DEV + B_DEV : S_DEV + 2 * B_DEV, :, 0:SPAN] = own_ref[S_DEV:SPAN]
    wide_ref[pl.ds(low_start, B_DEV), :, 0:SPAN] = near_ref[...]
    wide_ref[pl.ds(high_start, B_DEV), :, 0:SPAN] = far_ref[...]
    lane = iota((devices, LANES), 1)

    def place(base, shift, first, count):
        moved = pltpu.roll(base, shift, 1) if shift else base
        return jnp.where((lane >= first) & (lane < first + count), moved, 0.0)

    def from_device(field, step):
        return pltpu.roll(field, (-step) % devices, 0) if step % devices else field

    def one(region, carry):
        base = wide_ref[region]
        bubbles = B_DEV - S_DEV
        table = place(base, 0, 0, S_DEV) + place(base, B_DEV + bubbles, 2 * B_DEV, B_DEV)
        table = table + from_device(
            place(base, S_DEV, S_DEV, S_DEV) + place(base, 2 * B_DEV + bubbles, 3 * B_DEV, B_DEV), columns
        )
        table = table + from_device(
            place(base, 2 * S_DEV, 2 * S_DEV, S_DEV) + place(base, bubbles, B_DEV, B_DEV), -columns
        )
        table = table + from_device(place(base, 3 * S_DEV, 3 * S_DEV, S_DEV), 1)
        table = table + from_device(place(base, 3 * B_DEV + bubbles, 4 * B_DEV, B_DEV), 2 * columns)
        table = table + from_device(place(base, 4 * B_DEV + bubbles, 5 * B_DEV, B_DEV), -2 * columns)
        own_codes = jnp.where((lane < S_DEV) | ((lane >= B_DEV) & (lane < CODES)), table, 0.0)
        dest_ref[region, pl.ds(0, devices, stride=2), :] = table
        dest_ref[region, pl.ds(1, devices, stride=2), :] = from_device(own_codes, -1)
        return carry

    lax.fori_loop(0, REGIONS, one, 0, unroll=4)
    write = pltpu.make_async_copy(dest_ref, dest_hbm, sems.at[0])
    write.start()
    write.wait()


def write_edges(even_z, even_y, value_ref, z_refs, y_refs, convert=lambda value: value):
    planes, rows, _ = value_ref.shape
    z_refs[0][...] = convert(value_ref[jnp.where(even_z, planes - 1, 0)])
    z_refs[1][...] = convert(value_ref[jnp.where(even_z, 0, planes - 1)])
    for plane in range(planes):
        first = convert(value_ref[plane, 0:1, :])
        last = convert(value_ref[plane, rows - 1 : rows, :])
        y_refs[0][plane : plane + 1, :] = jnp.where(even_y, last, first)
        y_refs[1][plane : plane + 1, :] = jnp.where(even_y, first, last)


def slices_kernel(frac_hbm, coarse_hbm, z0_ref, z1_ref, y0_ref, y1_ref, bubble_ref, frac_ref, coarse_ref, sems):
    planes, rows, _ = frac_ref.shape
    copies = [
        pltpu.make_async_copy(frac_hbm, frac_ref, sems.at[0]),
        pltpu.make_async_copy(coarse_hbm, coarse_ref, sems.at[1]),
    ]
    start_all(copies)
    place = Place()
    even_z, even_y = place.even_z, place.even_y
    wait_all(copies)
    bubble_ref[...] = coarse_ref[S_DEV:SPAN, :]
    z0_ref[...] = frac_ref[pl.ds(jnp.where(even_z, planes - DEPTH, 0), DEPTH)]
    z1_ref[...] = frac_ref[pl.ds(jnp.where(even_z, 0, planes - DEPTH), DEPTH)]
    first, last = frac_ref[:, 0:DEPTH, :], frac_ref[:, rows - DEPTH : rows, :]
    y0_ref[...] = jnp.where(even_y, last, first)
    y1_ref[...] = jnp.where(even_y, first, last)


def setup_kernel(
    z0_in, z1_in, y0_in, y1_in, k0_in, k1_in, frac_hbm, source_hbm, label_hbm, sub_hbm, dest_hbm,
    ez0_ref, ez1_ref, ey0_ref, ey1_ref, send_ref,
    code_ref, cz_ref, cy_ref, cx_ref, inv_ref, south_ref, r_hbm, diag_hbm,
    frac_ref, source_ref, label_ref, sub_ref, dest_ref, r_ref, diag_ref, b_ref,
    deep_ref, nz_ref, flat_ref, kap_ref, fz_ref, work_ref, in_sems, out_sems,
):
    planes, rows, width = frac_ref.shape
    tall = rows + 8
    place = Place()
    first_z, last_z, first_y, last_y = place.first_z, place.last_z, place.first_y, place.last_y
    base, stride, sub_base = place.base, place.stride, place.sub_base
    even_z, even_y = place.even_z, place.even_y
    pairs = [(frac_hbm, frac_ref), (label_hbm, label_ref), (sub_hbm, sub_ref), (source_hbm, source_ref), (dest_hbm, dest_ref)]
    reads = [pltpu.make_async_copy(a, b, in_sems.at[i]) for i, (a, b) in enumerate(pairs)]
    start_all(reads)
    row = iota((tall, width), 0)
    lane = iota((tall, width), 1)
    inside_y = ((row < rows) | ((row < rows + 4) & jnp.logical_not(last_y))) | (
        (row >= rows + 4) & jnp.logical_not(first_y)
    )
    first_plane = jnp.where(first_z, 0, -planes)
    last_plane = jnp.where(last_z, planes, 2 * planes)

    def right_of(field):
        moved = next_x(field)
        tile = lane[: field.shape[0], :LANES]
        ended = jnp.where(tile == LANES - 1, 0.0, moved[:, width - LANES :])
        return jnp.concatenate([moved[:, : width - LANES], ended], axis=1)

    def left_of(field):
        moved = prev_x(field)
        tile = lane[: field.shape[0], :LANES]
        return jnp.concatenate([jnp.where(tile == 0, 0.0, moved[:, :LANES]), moved[:, LANES:]], axis=1)

    deep_ref[:, rows:tall, :] = jnp.zeros((planes + 2 * DEPTH, 8, width), f32)
    near_z = jnp.where(even_z, planes + DEPTH, 0)
    far_z = jnp.where(even_z, 0, planes + DEPTH)
    out_near, out_far = jnp.where(even_z, last_z, first_z), jnp.where(even_z, first_z, last_z)
    deep_ref[pl.ds(near_z, DEPTH), 0:rows, :] = jnp.where(out_near, 0.0, z0_in[...])
    deep_ref[pl.ds(far_z, DEPTH), 0:rows, :] = jnp.where(out_far, 0.0, z1_in[...])
    high, low = slice(rows, rows + DEPTH), slice(tall - DEPTH, tall)

    def fill_rows(first, second, out_first, out_second):
        deep_ref[DEPTH : planes + DEPTH, first, :] = jnp.where(out_first, 0.0, y0_in[...])
        deep_ref[DEPTH : planes + DEPTH, second, :] = jnp.where(out_second, 0.0, y1_in[...])
        for start, corner, out in ((near_z, k0_in, out_near), (far_z, k1_in, out_far)):
            deep_ref[pl.ds(start, DEPTH), first, :] = jnp.where(out | out_first, 0.0, corner[0])
            deep_ref[pl.ds(start, DEPTH), second, :] = jnp.where(out | out_second, 0.0, corner[1])

    @pl.when(even_y)
    def _():
        fill_rows(high, low, last_y, first_y)

    @pl.when(jnp.logical_not(even_y))
    def _():
        fill_rows(low, high, first_y, last_y)

    reads[0].wait()
    deep_ref[DEPTH : planes + DEPTH, 0:rows, :] = frac_ref[...]

    def normal_plane(index, carry):
        keep = (index - 2 >= first_plane) & (index - 2 < last_plane)
        here = deep_ref[index + 1]
        gz = deep_ref[index + 2] - deep_ref[index]
        gy = up_rows(here) - down_rows(here)
        gx = right_of(here) - left_of(here)
        scale = jnp.minimum(lax.rsqrt(gz * gz + gy * gy + gx * gx), 0.5 / norm_floor)
        scale = jnp.where(inside_y & keep, scale, 0.0)
        ny = gy * scale
        nx = gx * scale
        nz_ref[index] = gz * scale
        flat_ref[index] = (up_rows(ny) - down_rows(ny)) + (right_of(nx) - left_of(nx))
        return carry

    lax.fori_loop(0, planes + 4, normal_plane, 0, unroll=2)

    def kappa_plane(index, carry):
        keep = (index - 1 >= first_plane) & (index - 1 < last_plane)
        value = -0.5 * ((nz_ref[index + 2] - nz_ref[index]) + flat_ref[index + 1])
        kap_ref[index] = jnp.where(inside_y & keep, value, 0.0)
        return carry

    lax.fori_loop(0, planes + 2, kappa_plane, 0)
    mid = pl.ds(0, rows)

    def z_face(index, carry):
        f_low = deep_ref[index + 2, mid, :]
        f_high = deep_ref[index + 3, mid, :]
        coef = 2.0 * pl.reciprocal((1.0 - gas_drop * f_low) + (1.0 - gas_drop * f_high))
        cz_ref[index] = coef
        mean = 0.5 * (kap_ref[index, mid, :] + kap_ref[index + 1, mid, :])
        fz_ref[index] = coef * mean * (f_high - f_low)
        return carry

    lax.fori_loop(0, planes + 1, z_face, 0)
    row_mid = row[:rows]
    lane_mid = lane[:rows]
    wait_all(reads[1:])

    def assemble_plane(plane, carry):
        inv_before, g_before = carry
        f = deep_ref[plane + 3]
        k = kap_ref[plane + 1]
        d = 1.0 - gas_drop * f
        f_up = up_rows(f)
        cy = 2.0 * pl.reciprocal(d + (1.0 - gas_drop * f_up))
        fy = cy * (0.5 * (k + up_rows(k))) * (f_up - f)
        cyp, cym = cy[:rows], down_rows(cy)[:rows]
        sum_y = fy[:rows] - down_rows(fy)[:rows]
        f, k, d = f[:rows], k[:rows], d[:rows]
        f_right = right_of(f)
        cxp = 2.0 * pl.reciprocal(d + (1.0 - gas_drop * f_right))
        fx = cxp * (0.5 * (k + right_of(k))) * (f_right - f)
        outer = jnp.concatenate([2.0 / (d[:, :LANES] + 1.0), jnp.zeros((rows, width - LANES), f32)], axis=1)
        cxm = jnp.where(lane_mid == 0, outer, prev_x(cxp))
        fx_before = jnp.where(lane_mid == 0, outer * (0.5 * k) * f, prev_x(fx))
        terms = fz_ref[plane + 1] - fz_ref[plane] + sum_y + (fx - fx_before)
        rhs = source_ref[plane] - surface_tension * terms
        down = cz_ref[plane]
        diagonal = shift_term + (cz_ref[plane + 1] + down + cyp + cym + cxp + cxm)
        mult = down * inv_before
        inv = pl.reciprocal(diagonal - mult * down)
        g = rhs + mult * g_before
        r_ref[plane] = rhs
        diag_ref[plane] = diagonal
        inv_ref[plane] = inv
        work_ref[plane] = g
        cy_ref[plane] = jnp.where((row_mid == rows - 1) & last_y, 0.0, cyp)
        south_ref[pl.ds(plane, 1), :] = jnp.where(first_y, 0.0, cym[0:1, :])
        cx_ref[plane] = jnp.where(lane_mid == width - 1, 0.0, cxp)
        label = label_ref[plane]
        offset = label - base
        below = offset < 0
        above = offset >= stride
        group = jnp.where(below, 1, jnp.where(above, 3, 2))
        inner = jnp.where(below, offset + stride, jnp.where(above, offset - stride, offset))
        code = jnp.where(label >= 0, group * B_DEV + inner, sub_ref[plane] - sub_base)
        code_ref[plane] = (code & (CODES - 1)).astype(i8)
        return (inv, g)

    blank = jnp.zeros((rows, width), f32)
    lax.fori_loop(0, planes, assemble_plane, (blank, blank))

    def backward(step, after):
        plane = planes - 1 - step
        value = (work_ref[plane] + cz_ref[plane + 1] * after) * inv_ref[plane]
        b_ref[plane] = value
        return value

    lax.fori_loop(0, planes, backward, blank)
    cz_ref[0] = jnp.where(first_z, 0.0, cz_ref[0])
    cz_ref[planes] = jnp.where(last_z, 0.0, cz_ref[planes])
    writes = [
        pltpu.make_async_copy(r_ref, r_hbm, out_sems.at[0]), pltpu.make_async_copy(diag_ref, diag_hbm, out_sems.at[1])
    ]
    start_all(writes)
    write_edges(even_z, even_y, b_ref, [ez0_ref.at[0], ez1_ref.at[0]], [ey0_ref.at[0], ey1_ref.at[0]])
    for plane in range(planes):
        label_ref[plane] = code_ref[plane].astype(i32)
    write_edges(
        even_z, even_y, label_ref, [ez0_ref.at[1], ez1_ref.at[1]], [ey0_ref.at[1], ey1_ref.at[1]],
        convert=lambda value: value.astype(f32),
    )
    send_ref[...] = coarse_parts(region_row(r_ref, code_ref), dest_ref)
    wait_all(writes)


def table_rows(parts):
    folded = jnp.sum(parts.reshape(parts.shape[0] // 8, 8, LANES), axis=0)
    even = iota(folded.shape, 0) % 2 == 0
    return jnp.concatenate(
        [
            jnp.sum(jnp.where(even, folded, 0.0), axis=0, keepdims=True),
            jnp.sum(jnp.where(even, 0.0, folded), axis=0, keepdims=True),
        ],
        axis=0,
    )


def scalars_of(sums):
    alphas, betas, curves = [], [None], []
    for step, row in enumerate(sums):
        gamma = lane_of(row, 0)
        if step == 0:
            curve = lane_of(row, 1)
        else:
            beta = gamma / lane_of(sums[step - 1], 0)
            betas.append(beta)
            curve = lane_of(row, 1) + beta * (lane_of(row, 2) + beta * curves[-1])
        curves.append(curve)
        alphas.append(gamma / curve)
    return alphas, betas


def step_kernel(stage, *refs):
    refs = list(refs)

    def take(count):
        out = refs[:count]
        del refs[:count]
        return out

    parts = take(stage + 1)
    halos = [take(4) for _ in range(stage + 1)]
    code_ref, cz_ref, cy_ref, cx_ref, inv_ref, south_ref = take(6)
    last = stage == 2
    names = (("r",), ("r", "w0", "z0"), ("r", "w1", "w0", "z1", "z0"))[stage] + (("diag",) if last else ("diag", "dest"))
    sources = dict(zip(names, take(len(names))))
    out_names = (("z", "w"), ("rn", "z", "w"), ("rn", "s", "p", "z", "w"))[stage]
    if not last:
        edges_z, edges_y = take(2), take(2)
    (send_ref,) = take(1)
    if last:
        pad_ref, w_ref, *others = take(6)
        made = dict(zip(("rn", "s", "p", "x"), others))
        out_names = ()
        held = dict(zip(names, take(len(names))))
        side_ref, work_ref, in_sems = take(3)
        out_sems = None
    else:
        sinks = dict(zip(out_names, take(len(out_names))))
        held = dict(zip(names, take(len(names))))
        pad_ref, side_ref, work_ref, w_ref = take(4)
        made = {"z": pad_ref.at[pl.ds(1, pad_ref.shape[0] - 2)], "w": w_ref}
        for name in out_names[:-2]:
            (made[name],) = take(1)
        u_ref, in_sems, out_sems = take(3)

    reads = {name: pltpu.make_async_copy(sources[name], held[name], in_sems.at[i]) for i, name in enumerate(names)}
    start_all(reads.values())
    writes = {name: pltpu.make_async_copy(made[name], sinks[name], out_sems.at[i]) for i, name in enumerate(out_names)}
    planes, rows, width = code_ref.shape
    place = Place()
    even_z, even_y = place.even_z, place.even_y

    sums = [table_rows(part[...]) for part in parts]
    alphas, betas = scalars_of([row[0:1] for row in sums[1:]])
    table = sums[0]
    if stage >= 1:
        table = table - alphas[0] * sums[1]
    if stage == 2:
        table = table - alphas[1] * (sums[2] + betas[1] * sums[1])
    near, side = table[0:1], table[1:2]

    def combine(values):
        out = values[0]
        if stage >= 1:
            out = out - alphas[0] * values[1]
        if stage == 2:
            out = out - alphas[1] * (values[2] + betas[1] * values[1])
        return out

    for slot in range(2):
        upper = even_z if slot == 0 else jnp.logical_not(even_z)
        index = halos[0][slot][1].astype(i32)
        high = jnp.where(index < B_DEV, index + S_DEV, index + B_DEV)
        low = jnp.where(
            index < B_DEV, index + 2 * S_DEV, jnp.where(index < 2 * B_DEV, index + 4 * B_DEV, index - B_DEV)
        )
        block = combine([halos[0][slot][0]] + [halo[slot][...] for halo in halos[1:]])
        pad_ref[jnp.where(upper, planes + 1, 0)] = block + lookup(near, jnp.where(upper, high, low))
        upper = even_y if slot == 0 else jnp.logical_not(even_y)
        index = halos[0][2 + slot][1].astype(i32)
        block = combine([halos[0][2 + slot][0]] + [halo[2 + slot][...] for halo in halos[1:]])
        found = jnp.where(
            upper, lookup(near, (index & (B_DEV - 1)) + 3 * S_DEV), lookup(side, index)
        )
        side_ref[jnp.where(upper, 1, 0)] = block + found

    early = tuple(name for name in names if name[0] in "rw")
    for name in early:
        reads[name].wait()
    empty = jnp.zeros((rows, width), f32)

    def residual(plane, before):
        value = held["r"][plane]
        if stage == 1:
            value = value - alphas[0] * held["w0"][plane]
            made["rn"][plane] = value
        if stage == 2:
            image = held["w1"][plane] + betas[1] * held["w0"][plane]
            made["s"][plane] = image
            value = value - alphas[1] * image
            made["rn"][plane] = value
        value = value + cz_ref[plane] * before
        work_ref[plane] = value
        return value * inv_ref[plane]

    lax.fori_loop(0, planes, residual, empty)
    start_all([writes[name] for name in out_names[:-2]])

    def direction(step, after):
        plane = planes - 1 - step
        value = (work_ref[plane] + cz_ref[plane + 1] * after) * inv_ref[plane]
        pad_ref[plane + 1] = value + lookup(near, code_ref[plane].astype(i32))
        return value

    lax.fori_loop(0, planes, direction, empty)
    if not last:
        writes["z"].start()
    for name in names:
        if name not in early and name != "dest":
            reads[name].wait()
    row = iota((rows, width), 0)

    def image_plane(plane, carry):
        sums, before = carry
        here = pad_ref[plane + 1]
        cy, cx = cy_ref[plane], cx_ref[plane]
        north = jnp.where(row == rows - 1, side_ref[1, pl.ds(plane, 1), :], up_rows(here))
        below = south_ref[pl.ds(plane, 1), :] * side_ref[0, pl.ds(plane, 1), :]
        south = jnp.where(row == 0, below, down_rows(cy * here))
        image = held["diag"][plane] * here - (
            cz_ref[plane + 1] * pad_ref[plane + 2]
            + cz_ref[plane] * pad_ref[plane]
            + (cy * north + south)
            + (cx * next_x(here) + prev_x(cx * here))
        )
        w_ref[plane] = image
        new = made["rn"] if stage else held["r"]
        found = [total(new[plane] * here), total(here * image)]
        if stage == 1:
            found.append(total(here * held["w0"][plane] + held["z0"][plane] * image))
        if stage == 2:
            along = held["z1"][plane] + betas[1] * held["z0"][plane]
            made["p"][plane] = along
            made["x"][plane] = alphas[0] * held["z0"][plane] + alphas[1] * along
            found.append(total(here * made["s"][plane] + along * image))
        if not last:
            before = image + cz_ref[plane] * before
            work_ref[plane] = before
            before = before * inv_ref[plane]
        return tuple(old + new for old, new in zip(sums, found)), before

    blank = jnp.zeros((8, LANES), f32)
    dots, _ = lax.fori_loop(
        0, planes, image_plane, ((blank,) * (3 if stage else 2), blank if last else empty), unroll=2
    )
    if not last:
        writes["w"].start()
    row = scalar_row([jnp.sum(value) for value in dots])
    if last:
        send_ref[...] = jnp.broadcast_to(row, send_ref.shape)
    else:

        def backward(step, after):
            plane = planes - 1 - step
            value = (work_ref[plane] + cz_ref[plane + 1] * after) * inv_ref[plane]
            u_ref[plane] = value
            return value

        lax.fori_loop(0, planes, backward, empty)
        write_edges(even_z, even_y, u_ref, edges_z, edges_y)
        reads["dest"].wait()
        parts = coarse_parts(region_row(w_ref, code_ref), held["dest"])
        send_ref[...] = parts + jnp.where(iota(parts.shape, 0) % 2 == 0, row, 0.0)
    wait_all(writes.values())


def final_kernel(
    d0_ref, d1_ref, d2_ref, z_ref, w_ref, r_ref, s_ref, p_ref, part_ref, x_out, r_out, x_new, r_new, sems
):
    sums = [table_rows(d0_ref[...])[0:1], table_rows(d1_ref[...])[0:1], jnp.sum(d2_ref[...], axis=0, keepdims=True)]
    alphas, betas = scalars_of(sums)
    mixed = alphas[2] * betas[2]
    planes = r_ref.shape[0]
    writes = []
    for half in range(2):
        low, high = half * planes // 2, (half + 1) * planes // 2
        x_new[low:high] = part_ref[low:high] + alphas[2] * z_ref[low + 1 : high + 1] + mixed * p_ref[low:high]
        r_new[low:high] = r_ref[low:high] - alphas[2] * w_ref[low:high] - mixed * s_ref[low:high]
        piece = pl.ds(low, high - low)
        pairs = [(x_new.at[piece], x_out.at[piece]), (r_new.at[piece], r_out.at[piece])]
        copies = [pltpu.make_async_copy(a, b, sems.at[2 * half + i]) for i, (a, b) in enumerate(pairs)]
        start_all(copies)
        writes += copies
    wait_all(writes)


def call(kernel, outs, scratch, args):
    spaces = {"smem": pltpu.SMEM, "vmem": pltpu.VMEM, "kept": pltpu.VMEM, "hbm": pltpu.HBM}

    def specs(items):
        return [pl.BlockSpec(memory_space=spaces[space]) for space, _ in items]

    held = sum(4 * math.prod(ref.shape) for ref in scratch)
    places = {"hbm": pltpu.HBM, "kept": pltpu.VMEM}
    made = [places[space](out.shape, out.dtype) if space in places else out for space, out in outs]
    operands = [
        pltpu.with_memory_space_constraint(value, places[space]) if space in places else value for space, value in args
    ]
    return pl.pallas_call(
        kernel,
        out_shape=made,
        in_specs=specs(args),
        out_specs=specs(outs),
        scratch_shapes=scratch,
        compiler_params=pltpu.CompilerParams(vmem_limit_bytes=held + 12 * 1024 * 1024),
    )(*operands)


def swaps(axis, first):
    count = lax.axis_size(axis)
    pairs = []
    for i in range(first, count + first, 2):
        low, high = i % count, (i + 1) % count
        pairs += [(low, high), (high, low)]
    return pairs


def swap(block, axis, first):
    if axis == "gz" and first == 1:
        return lax.ppermute(block, ("gz", "gy"), inner_swaps())
    return lax.ppermute(block, axis, swaps(axis, first))


def inner_swaps():
    slabs, columns = lax.axis_size("gz"), lax.axis_size("gy")
    pairs = []
    for slab in range(slabs):
        for column in range(columns):
            if slab in (0, slabs - 1):
                target = slab * columns + (column ^ 1)
            else:
                target = (slab + 1 if slab % 2 else slab - 1) * columns + column
            pairs.append((slab * columns + column, target))
    return pairs


def solve(fraction, source, bubble_label, subdomain, coarse_inverse):
    planes, rows, width = fraction.shape
    slabs = lax.axis_size("gz")
    columns = lax.axis_size("gy")
    devices = slabs * columns
    slab = lax.axis_index("gz")
    even_z = slab % 2 == 0
    field = jax.ShapeDtypeStruct((planes, rows, width), f32)

    def shape(*dims, dtype=f32):
        return jax.ShapeDtypeStruct(dims, dtype)

    def vmem(*dims, dtype=f32):
        return pltpu.VMEM(dims, dtype)

    def like(items):
        return [vmem(*value.shape, dtype=value.dtype) for value in items]

    def semaphores(count):
        return pltpu.SemaphoreType.DMA((count,))

    def tag(space, items):
        return [(space, item) for item in items]

    top, bottom, *sides, bubbles = call(
        slices_kernel,
        tag("vmem", [shape(DEPTH, rows, width)] * 2 + [shape(planes, DEPTH, width)] * 2 + [shape(B_DEV, devices * SPAN)]),
        [vmem(planes, rows, width), vmem(SPAN, devices * SPAN), semaphores(2)],
        tag("hbm", [fraction, coarse_inverse]),
    )
    coarse_in = [swap(bubbles, "gz", 0), swap(bubbles, "gz", 1)]
    y_in = [swap(sides[0], "gy", 0), swap(sides[1], "gy", 1)]
    z_in = [swap(top, "gz", 0), swap(bottom, "gz", 1)]
    corner = jnp.stack(y_in)
    corner_top = jnp.where(even_z, corner[:, planes - DEPTH :], corner[:, :DEPTH])
    corner_bottom = jnp.where(even_z, corner[:, :DEPTH], corner[:, planes - DEPTH :])
    corner_in = [swap(corner_top, "gz", 0), swap(corner_bottom, "gz", 1)]

    def spread(matrix):
        return matrix.reshape(matrix.shape[0], devices, SPAN)

    dest_shape = shape(REGIONS, 2 * devices, LANES)
    spread_in = [spread(m) for m in [coarse_inverse] + coarse_in]
    (dest,) = call(
        partial(destinations_kernel, columns),
        tag("hbm", [dest_shape]),
        [vmem(REGIONS, devices, LANES)] + like([dest_shape]) + [semaphores(1)],
        tag("vmem", spread_in),
    )
    codes = shape(planes, rows, width, dtype=i8)
    faces = shape(planes + 1, rows, width)
    inputs = [fraction, source, bubble_label, subdomain, dest]
    tall = rows + 8
    wide = shape(2 * devices, LANES)
    first_edges = [shape(2, rows, width)] * 2 + [shape(2, planes, width)] * 2
    later_edges = [shape(rows, width)] * 2 + [shape(planes, width)] * 2
    outs = tag("vmem", first_edges + [wide])
    outs += tag("kept", [codes, faces, field, field, field, shape(planes, width)]) + tag("hbm", [field, field])
    *sent, send, code, cz, cy, cx, inv, south, r0, diag = call(
        setup_kernel,
        outs,
        like(inputs)
        + like([field, field, field])
        + [
            vmem(planes + 2 * DEPTH, tall, width),
            vmem(planes + 4, tall, width),
            vmem(planes + 4, tall, width),
            vmem(planes + 2, tall, width),
            vmem(planes + 1, rows, width),
            vmem(planes, rows, width),
            semaphores(len(inputs)),
            semaphores(2),
        ],
        tag("vmem", z_in + y_in + corner_in) + tag("hbm", inputs),
    )
    matrix = [code, cz, cy, cx, inv, south]

    def exchange(parts):
        blocks = parts.reshape(devices, -1, LANES)
        return lax.all_to_all(blocks, ("gz", "gy"), 0, 0).reshape(parts.shape)

    def share(sent, send):
        edges = [swap(sent[0], "gz", 0), swap(sent[1], "gz", 1)]
        edges += [swap(sent[2], "gy", 0), swap(sent[3], "gy", 1)]
        parts = [exchange(send)]
        return edges, parts

    def step(stage, parts, edges, state):
        last = stage == 2
        operands = state + ([diag] if last else [diag, dest])
        tall_field = shape(planes + 2, rows, width)
        sides = vmem(2, planes, width)
        if last:
            outs = tag("vmem", [shape(devices, LANES)]) + tag("kept", [tall_field] + [field] * 5)
            scratch = like(operands) + [sides] + like([field]) + [semaphores(len(operands))]
            count = 0
        else:
            fields = [field] * (2 + stage)
            outs = tag("vmem", later_edges + [wide]) + tag("hbm", fields)
            scratch = like(operands) + like([tall_field]) + [sides] + like([field] * (len(fields) + 1))
            scratch += [semaphores(len(operands)), semaphores(len(fields))]
            count = len(later_edges)
        results = call(
            partial(step_kernel, stage),
            outs,
            scratch,
            tag("vmem", parts + edges) + tag("kept", matrix) + tag("hbm", operands),
        )
        return results[:count], results[count], results[count + 1 :]

    edges, parts = share(sent, send)
    sent, send, (z0, w0) = step(0, parts, edges, [r0])
    more_edges, more_parts = share(sent, send)
    edges, parts = edges + more_edges, parts + more_parts
    sent, send, (r1, z1, w1) = step(1, parts, edges, [r0, w0, z0])
    more_edges, more_parts = share(sent, send)
    edges, parts = edges + more_edges, parts + more_parts
    _, send, kept = step(2, parts, edges, [r1, w1, w0, z1, z0])
    parts = parts + [exchange(send)]
    return tuple(
        call(
            final_kernel,
            tag("hbm", [field, field]),
            like([field, field]) + [semaphores(4)],
            tag("vmem", parts[1:]) + tag("kept", kept),
        )
    )


def solution(mesh):
    placed = (
        P("gz", "gy", None),
        P("gz", "gy", None),
        P("gz", "gy", None),
        P("gz", "gy", None),
        P(("gz", "gy"), None),
    )
    return jax.shard_map(
        solve,
        mesh=mesh,
        in_specs=placed,
        out_specs=(P("gz", "gy", None), P("gz", "gy", None)),
        check_vma=False,
    )
```

```python
import math
from functools import partial

import jax
import jax.numpy as jnp
from jax import lax
from jax.experimental import pallas as pl
from jax.experimental.pallas import tpu as pltpu
from jax.sharding import PartitionSpec as P


S_DEV = 4
B_DEV = 16
SPAN = S_DEV + B_DEV
LANES = 128
GROUPS = 4
CODES = GROUPS * B_DEV
REGIONS = S_DEV + 3 * B_DEV
SCALARS = 96
DEPTH = 3
PIECE = 16

surface_tension = 0.5
shift_term = 0.05
gas_drop = 0.75
norm_floor = 0.25
highest = lax.Precision.HIGHEST
f32 = jnp.float32
i32 = jnp.int32
i8 = jnp.int8
bf16 = jnp.bfloat16


def iota(shape, dim):
    return lax.broadcasted_iota(i32, shape, dim)


def up_rows(field):
    return pltpu.roll(field, field.shape[0] - 1, 0)


def down_rows(field):
    return pltpu.roll(field, 1, 0)


def next_x(field):
    return pltpu.roll(field, field.shape[1] - 1, 1)


def prev_x(field):
    return pltpu.roll(field, 1, 1)


def total(field):
    rows, width = field.shape
    folded = field[:, :LANES]
    for start in range(LANES, width, LANES):
        folded = folded + field[:, start : start + LANES]
    return jnp.sum(folded.reshape(rows // 8, 8, LANES), axis=0)


def digits(code):
    forms = []
    rest = code.astype(f32).astype(bf16)
    bits = []
    for power in (32, 16, 8, 4, 2, 1):
        bit = rest if power == 1 else jnp.clip(rest - (power - 1), 0, 1)
        bits.append(bit)
        rest = rest - power * bit
    for high, low in zip(bits[::2], bits[1::2]):
        no_high, no_low = 1 - high, 1 - low
        forms.append([no_high * no_low, no_high * low, high * no_low, high * low])
    return forms


def piece_sums(values, code):
    groups, outer, inner = digits(code)
    high = values.astype(bf16)
    low = (values - high.astype(f32)).astype(bf16)
    left = [group * part for part in (high, low) for group in groups]
    right = [first * second for first in outer for second in inner]
    return lax.dot_general(
        jnp.concatenate(left, axis=0),
        jnp.concatenate(right, axis=0),
        (((1,), (1,)), ((), ())),
        preferred_element_type=f32,
    )


def region_row(value_ref, code_ref):
    planes, rows, _ = value_ref.shape

    def step(plane, acc):
        code = code_ref[plane].astype(i32)
        for start in range(0, rows, PIECE):
            acc = acc + piece_sums(value_ref[plane, start : start + PIECE, :], code[start : start + PIECE])
        return acc

    acc = lax.fori_loop(
        0, planes, step, jnp.zeros((2 * GROUPS * PIECE, B_DEV * PIECE), f32), unroll=planes
    )
    shape = acc.shape
    kept = jnp.where(iota(shape, 0) % PIECE == iota(shape, 1) % PIECE, acc, 0.0)
    folded = jnp.sum(kept.reshape(2 * GROUPS, PIECE, shape[1]), axis=1)
    shape = (shape[1], LANES)
    pick = jnp.where(iota(shape, 0) // PIECE == iota(shape, 1) % B_DEV, 1.0, 0.0)
    spread = jnp.dot(folded, pick, precision=highest, preferred_element_type=f32)
    shape = spread.shape
    lane = iota(shape, 1)
    mine = (iota(shape, 0) % GROUPS == lane // B_DEV) & (lane < CODES)
    return jnp.sum(jnp.where(mine, spread, 0.0), axis=0, keepdims=True)


def scalar_row(scalars):
    lane = iota((1, LANES), 1)
    row = jnp.zeros((1, LANES), f32)
    for index, value in enumerate(scalars):
        row = jnp.where(lane == SCALARS + index, value, row)
    return row


def lane_of(row, index):
    return jnp.sum(jnp.where(iota(row.shape, 1) == SCALARS + index, row, 0.0))


def lookup(table, index):
    rows, width = index.shape
    wide = jnp.broadcast_to(table, (rows, LANES))
    return jnp.concatenate(
        [
            jnp.take_along_axis(wide, index[:, start : start + LANES], axis=1)
            for start in range(0, width, LANES)
        ],
        axis=1,
    )


class Place:
    def __init__(self):
        slab, column = lax.axis_index("gz"), lax.axis_index("gy")
        slabs, columns = lax.axis_size("gz"), lax.axis_size("gy")
        here = slab * columns + column
        self.first_z, self.last_z = slab == 0, slab == slabs - 1
        self.first_y, self.last_y = column == 0, column == columns - 1
        self.base, self.stride, self.sub_base = here * B_DEV, columns * B_DEV, here * S_DEV
        self.even_z, self.even_y = slab % 2 == 0, column % 2 == 0


def start_all(copies):
    @pl.when(lax.axis_index("gz") >= 0)
    def _():
        for copy in copies:
            copy.start()


def wait_all(copies):
    for copy in copies:
        copy.wait()


def coarse_parts(row, dest_ref):
    wide = jnp.broadcast_to(row, (8, LANES))

    def step(region, acc):
        lane = jnp.where(region < S_DEV, region, region + B_DEV - S_DEV)
        factor = jnp.take_along_axis(wide, jnp.full((8, LANES), lane, i32), axis=1)[0:1, :]
        return acc + factor * dest_ref[region]

    small = dest_ref.shape[1] <= 64
    return lax.fori_loop(0, REGIONS, step, jnp.zeros(dest_ref.shape[1:], f32), unroll=REGIONS if small else 4)


def destinations_kernel(columns, own_ref, near_ref, far_ref, dest_hbm, wide_ref, dest_ref, sems):
    devices = own_ref.shape[1]
    even_z = Place().even_z
    wide_ref[...] = jnp.zeros(wide_ref.shape, f32)
    low_start = pl.multiple_of(jnp.where(even_z, 2 * B_DEV, 0), B_DEV) + S_DEV
    high_start = pl.multiple_of(jnp.where(even_z, 0, 2 * B_DEV), B_DEV) + S_DEV
    wide_ref[0:S_DEV, :, 0:SPAN] = own_ref[0:S_DEV]
    wide_ref[S_DEV + B_DEV : S_DEV + 2 * B_DEV, :, 0:SPAN] = own_ref[S_DEV:SPAN]
    wide_ref[pl.ds(low_start, B_DEV), :, 0:SPAN] = near_ref[...]
    wide_ref[pl.ds(high_start, B_DEV), :, 0:SPAN] = far_ref[...]
    lane = iota((devices, LANES), 1)

    def place(base, shift, first, count):
        moved = pltpu.roll(base, shift, 1) if shift else base
        return jnp.where((lane >= first) & (lane < first + count), moved, 0.0)

    def from_device(field, step):
        return pltpu.roll(field, (-step) % devices, 0) if step % devices else field

    def one(region, carry):
        base = wide_ref[region]
        bubbles = B_DEV - S_DEV
        table = place(base, 0, 0, S_DEV) + place(base, B_DEV + bubbles, 2 * B_DEV, B_DEV)
        table = table + from_device(
            place(base, S_DEV, S_DEV, S_DEV) + place(base, 2 * B_DEV + bubbles, 3 * B_DEV, B_DEV), columns
        )
        table = table + from_device(
            place(base, 2 * S_DEV, 2 * S_DEV, S_DEV) + place(base, bubbles, B_DEV, B_DEV), -columns
        )
        table = table + from_device(place(base, 3 * S_DEV, 3 * S_DEV, S_DEV), 1)
        table = table + from_device(place(base, 3 * B_DEV + bubbles, 4 * B_DEV, B_DEV), 2 * columns)
        table = table + from_device(place(base, 4 * B_DEV + bubbles, 5 * B_DEV, B_DEV), -2 * columns)
        own_codes = jnp.where((lane < S_DEV) | ((lane >= B_DEV) & (lane < CODES)), table, 0.0)
        dest_ref[region, pl.ds(0, devices, stride=2), :] = table
        dest_ref[region, pl.ds(1, devices, stride=2), :] = from_device(own_codes, -1)
        return carry

    lax.fori_loop(0, REGIONS, one, 0, unroll=4)
    write = pltpu.make_async_copy(dest_ref, dest_hbm, sems.at[0])
    write.start()
    write.wait()


def write_edges(even_z, even_y, value_ref, z_refs, y_refs, convert=lambda value: value):
    planes, rows, _ = value_ref.shape
    z_refs[0][...] = convert(value_ref[jnp.where(even_z, planes - 1, 0)])
    z_refs[1][...] = convert(value_ref[jnp.where(even_z, 0, planes - 1)])
    for plane in range(planes):
        first = convert(value_ref[plane, 0:1, :])
        last = convert(value_ref[plane, rows - 1 : rows, :])
        y_refs[0][plane : plane + 1, :] = jnp.where(even_y, last, first)
        y_refs[1][plane : plane + 1, :] = jnp.where(even_y, first, last)


def slices_kernel(frac_hbm, coarse_hbm, z0_ref, z1_ref, y0_ref, y1_ref, bubble_ref, frac_ref, coarse_ref, sems):
    planes, rows, _ = frac_ref.shape
    copies = [
        pltpu.make_async_copy(frac_hbm, frac_ref, sems.at[0]),
        pltpu.make_async_copy(coarse_hbm, coarse_ref, sems.at[1]),
    ]
    start_all(copies)
    place = Place()
    even_z, even_y = place.even_z, place.even_y
    wait_all(copies)
    bubble_ref[...] = coarse_ref[S_DEV:SPAN, :]
    z0_ref[...] = frac_ref[pl.ds(jnp.where(even_z, planes - DEPTH, 0), DEPTH)]
    z1_ref[...] = frac_ref[pl.ds(jnp.where(even_z, 0, planes - DEPTH), DEPTH)]
    first, last = frac_ref[:, 0:DEPTH, :], frac_ref[:, rows - DEPTH : rows, :]
    y0_ref[...] = jnp.where(even_y, last, first)
    y1_ref[...] = jnp.where(even_y, first, last)


def setup_kernel(
    z0_in, z1_in, y0_in, y1_in, k0_in, k1_in, frac_hbm, source_hbm, label_hbm, sub_hbm, dest_hbm,
    ez0_ref, ez1_ref, ey0_ref, ey1_ref, send_ref,
    code_ref, cz_ref, cy_ref, cx_ref, inv_ref, south_ref, r_hbm, diag_hbm,
    frac_ref, source_ref, label_ref, sub_ref, dest_ref, r_ref, diag_ref, b_ref,
    deep_ref, nz_ref, flat_ref, kap_ref, fz_ref, work_ref, in_sems, out_sems,
):
    planes, rows, width = frac_ref.shape
    tall = rows + 8
    place = Place()
    first_z, last_z, first_y, last_y = place.first_z, place.last_z, place.first_y, place.last_y
    base, stride, sub_base = place.base, place.stride, place.sub_base
    even_z, even_y = place.even_z, place.even_y
    pairs = [(frac_hbm, frac_ref), (label_hbm, label_ref), (sub_hbm, sub_ref), (source_hbm, source_ref), (dest_hbm, dest_ref)]
    reads = [pltpu.make_async_copy(a, b, in_sems.at[i]) for i, (a, b) in enumerate(pairs)]
    start_all(reads)
    row = iota((tall, width), 0)
    lane = iota((tall, width), 1)
    inside_y = ((row < rows) | ((row < rows + 4) & jnp.logical_not(last_y))) | (
        (row >= rows + 4) & jnp.logical_not(first_y)
    )
    first_plane = jnp.where(first_z, 0, -planes)
    last_plane = jnp.where(last_z, planes, 2 * planes)

    def right_of(field):
        moved = next_x(field)
        tile = lane[: field.shape[0], :LANES]
        ended = jnp.where(tile == LANES - 1, 0.0, moved[:, width - LANES :])
        return jnp.concatenate([moved[:, : width - LANES], ended], axis=1)

    def left_of(field):
        moved = prev_x(field)
        tile = lane[: field.shape[0], :LANES]
        return jnp.concatenate([jnp.where(tile == 0, 0.0, moved[:, :LANES]), moved[:, LANES:]], axis=1)

    deep_ref[:, rows:tall, :] = jnp.zeros((planes + 2 * DEPTH, 8, width), f32)
    near_z = jnp.where(even_z, planes + DEPTH, 0)
    far_z = jnp.where(even_z, 0, planes + DEPTH)
    out_near, out_far = jnp.where(even_z, last_z, first_z), jnp.where(even_z, first_z, last_z)
    deep_ref[pl.ds(near_z, DEPTH), 0:rows, :] = jnp.where(out_near, 0.0, z0_in[...])
    deep_ref[pl.ds(far_z, DEPTH), 0:rows, :] = jnp.where(out_far, 0.0, z1_in[...])
    high, low = slice(rows, rows + DEPTH), slice(tall - DEPTH, tall)

    def fill_rows(first, second, out_first, out_second):
        deep_ref[DEPTH : planes + DEPTH, first, :] = jnp.where(out_first, 0.0, y0_in[...])
        deep_ref[DEPTH : planes + DEPTH, second, :] = jnp.where(out_second, 0.0, y1_in[...])
        for start, corner, out in ((near_z, k0_in, out_near), (far_z, k1_in, out_far)):
            deep_ref[pl.ds(start, DEPTH), first, :] = jnp.where(out | out_first, 0.0, corner[0])
            deep_ref[pl.ds(start, DEPTH), second, :] = jnp.where(out | out_second, 0.0, corner[1])

    @pl.when(even_y)
    def _():
        fill_rows(high, low, last_y, first_y)

    @pl.when(jnp.logical_not(even_y))
    def _():
        fill_rows(low, high, first_y, last_y)

    reads[0].wait()
    deep_ref[DEPTH : planes + DEPTH, 0:rows, :] = frac_ref[...]

    def normal_plane(index, carry):
        keep = (index - 2 >= first_plane) & (index - 2 < last_plane)
        here = deep_ref[index + 1]
        gz = deep_ref[index + 2] - deep_ref[index]
        gy = up_rows(here) - down_rows(here)
        gx = right_of(here) - left_of(here)
        scale = jnp.minimum(lax.rsqrt(gz * gz + gy * gy + gx * gx), 0.5 / norm_floor)
        scale = jnp.where(inside_y & keep, scale, 0.0)
        ny = gy * scale
        nx = gx * scale
        nz_ref[index] = gz * scale
        flat_ref[index] = (up_rows(ny) - down_rows(ny)) + (right_of(nx) - left_of(nx))
        return carry

    lax.fori_loop(0, planes + 4, normal_plane, 0, unroll=2)

    def kappa_plane(index, carry):
        keep = (index - 1 >= first_plane) & (index - 1 < last_plane)
        value = -0.5 * ((nz_ref[index + 2] - nz_ref[index]) + flat_ref[index + 1])
        kap_ref[index] = jnp.where(inside_y & keep, value, 0.0)
        return carry

    lax.fori_loop(0, planes + 2, kappa_plane, 0, unroll=2)
    mid = pl.ds(0, rows)

    def z_face(index, carry):
        f_low = deep_ref[index + 2, mid, :]
        f_high = deep_ref[index + 3, mid, :]
        coef = 2.0 * pl.reciprocal((1.0 - gas_drop * f_low) + (1.0 - gas_drop * f_high))
        cz_ref[index] = coef
        mean = 0.5 * (kap_ref[index, mid, :] + kap_ref[index + 1, mid, :])
        fz_ref[index] = coef * mean * (f_high - f_low)
        return carry

    lax.fori_loop(0, planes + 1, z_face, 0, unroll=3)
    row_mid = row[:rows]
    lane_mid = lane[:rows]
    wait_all(reads[1:])

    def assemble_plane(plane, carry):
        inv_before, g_before = carry
        f = deep_ref[plane + 3]
        k = kap_ref[plane + 1]
        d = 1.0 - gas_drop * f
        f_up = up_rows(f)
        cy = 2.0 * pl.reciprocal(d + (1.0 - gas_drop * f_up))
        fy = cy * (0.5 * (k + up_rows(k))) * (f_up - f)
        cyp, cym = cy[:rows], down_rows(cy)[:rows]
        sum_y = fy[:rows] - down_rows(fy)[:rows]
        f, k, d = f[:rows], k[:rows], d[:rows]
        f_right = right_of(f)
        cxp = 2.0 * pl.reciprocal(d + (1.0 - gas_drop * f_right))
        fx = cxp * (0.5 * (k + right_of(k))) * (f_right - f)
        outer = jnp.concatenate([2.0 / (d[:, :LANES] + 1.0), jnp.zeros((rows, width - LANES), f32)], axis=1)
        cxm = jnp.where(lane_mid == 0, outer, prev_x(cxp))
        fx_before = jnp.where(lane_mid == 0, outer * (0.5 * k) * f, prev_x(fx))
        terms = fz_ref[plane + 1] - fz_ref[plane] + sum_y + (fx - fx_before)
        rhs = source_ref[plane] - surface_tension * terms
        down = cz_ref[plane]
        diagonal = shift_term + (cz_ref[plane + 1] + down + cyp + cym + cxp + cxm)
        mult = down * inv_before
        inv = pl.reciprocal(diagonal - mult * down)
        g = rhs + mult * g_before
        r_ref[plane] = rhs
        diag_ref[plane] = diagonal
        inv_ref[plane] = inv
        work_ref[plane] = g
        cy_ref[plane] = jnp.where((row_mid == rows - 1) & last_y, 0.0, cyp)
        south_ref[pl.ds(plane, 1), :] = jnp.where(first_y, 0.0, cym[0:1, :])
        cx_ref[plane] = jnp.where(lane_mid == width - 1, 0.0, cxp)
        label = label_ref[plane]
        offset = label - base
        below = offset < 0
        above = offset >= stride
        group = jnp.where(below, 1, jnp.where(above, 3, 2))
        inner = jnp.where(below, offset + stride, jnp.where(above, offset - stride, offset))
        code = jnp.where(label >= 0, group * B_DEV + inner, sub_ref[plane] - sub_base)
        code_ref[plane] = (code & (CODES - 1)).astype(i8)
        return (inv, g)

    blank = jnp.zeros((rows, width), f32)
    lax.fori_loop(0, planes, assemble_plane, (blank, blank), unroll=2)

    def backward(step, after):
        plane = planes - 1 - step
        value = (work_ref[plane] + cz_ref[plane + 1] * after) * inv_ref[plane]
        b_ref[plane] = value
        return value

    lax.fori_loop(0, planes, backward, blank, unroll=4)
    cz_ref[0] = jnp.where(first_z, 0.0, cz_ref[0])
    cz_ref[planes] = jnp.where(last_z, 0.0, cz_ref[planes])
    writes = [
        pltpu.make_async_copy(r_ref, r_hbm, out_sems.at[0]), pltpu.make_async_copy(diag_ref, diag_hbm, out_sems.at[1])
    ]
    start_all(writes)
    write_edges(even_z, even_y, b_ref, [ez0_ref.at[0], ez1_ref.at[0]], [ey0_ref.at[0], ey1_ref.at[0]])
    for plane in range(planes):
        label_ref[plane] = code_ref[plane].astype(i32)
    write_edges(
        even_z, even_y, label_ref, [ez0_ref.at[1], ez1_ref.at[1]], [ey0_ref.at[1], ey1_ref.at[1]],
        convert=lambda value: value.astype(f32),
    )
    send_ref[...] = coarse_parts(region_row(r_ref, code_ref), dest_ref)
    wait_all(writes)


def table_rows(parts):
    folded = jnp.sum(parts.reshape(parts.shape[0] // 8, 8, LANES), axis=0)
    even = iota(folded.shape, 0) % 2 == 0
    return jnp.concatenate(
        [
            jnp.sum(jnp.where(even, folded, 0.0), axis=0, keepdims=True),
            jnp.sum(jnp.where(even, 0.0, folded), axis=0, keepdims=True),
        ],
        axis=0,
    )


def scalars_of(sums):
    alphas, betas, curves = [], [None], []
    for step, row in enumerate(sums):
        gamma = lane_of(row, 0)
        if step == 0:
            curve = lane_of(row, 1)
        else:
            beta = gamma / lane_of(sums[step - 1], 0)
            betas.append(beta)
            curve = lane_of(row, 1) + beta * (lane_of(row, 2) + beta * curves[-1])
        curves.append(curve)
        alphas.append(gamma / curve)
    return alphas, betas


def step_kernel(stage, *refs):
    refs = list(refs)

    def take(count):
        out = refs[:count]
        del refs[:count]
        return out

    parts = take(stage + 1)
    halos = [take(4) for _ in range(stage + 1)]
    code_ref, cz_ref, cy_ref, cx_ref, inv_ref, south_ref = take(6)
    last = stage == 2
    names = (("r",), ("r", "w0", "z0"), ("r", "w1", "w0", "z1", "z0"))[stage] + (("diag",) if last else ("diag", "dest"))
    sources = dict(zip(names, take(len(names))))
    out_names = (("z", "w"), ("rn", "z", "w"), ("rn", "s", "p", "z", "w"))[stage]
    if not last:
        edges_z, edges_y = take(2), take(2)
    (send_ref,) = take(1)
    if last:
        pad_ref, w_ref, *others = take(6)
        made = dict(zip(("rn", "s", "p", "x"), others))
        out_names = ()
        held = dict(zip(names, take(len(names))))
        side_ref, work_ref, in_sems = take(3)
        out_sems = None
    else:
        sinks = dict(zip(out_names, take(len(out_names))))
        held = dict(zip(names, take(len(names))))
        pad_ref, side_ref, work_ref, w_ref = take(4)
        made = {"z": pad_ref.at[pl.ds(1, pad_ref.shape[0] - 2)], "w": w_ref}
        for name in out_names[:-2]:
            (made[name],) = take(1)
        u_ref, in_sems, out_sems = take(3)

    reads = {name: pltpu.make_async_copy(sources[name], held[name], in_sems.at[i]) for i, name in enumerate(names)}
    start_all(reads.values())
    writes = {name: pltpu.make_async_copy(made[name], sinks[name], out_sems.at[i]) for i, name in enumerate(out_names)}
    planes, rows, width = code_ref.shape
    place = Place()
    even_z, even_y = place.even_z, place.even_y

    sums = [table_rows(part[...]) for part in parts]
    alphas, betas = scalars_of([row[0:1] for row in sums[1:]])
    table = sums[0]
    if stage >= 1:
        table = table - alphas[0] * sums[1]
    if stage == 2:
        table = table - alphas[1] * (sums[2] + betas[1] * sums[1])
    near, side = table[0:1], table[1:2]

    def combine(values):
        out = values[0]
        if stage >= 1:
            out = out - alphas[0] * values[1]
        if stage == 2:
            out = out - alphas[1] * (values[2] + betas[1] * values[1])
        return out

    for slot in range(2):
        upper = even_z if slot == 0 else jnp.logical_not(even_z)
        index = halos[0][slot][1].astype(i32)
        high = jnp.where(index < B_DEV, index + S_DEV, index + B_DEV)
        low = jnp.where(
            index < B_DEV, index + 2 * S_DEV, jnp.where(index < 2 * B_DEV, index + 4 * B_DEV, index - B_DEV)
        )
        block = combine([halos[0][slot][0]] + [halo[slot][...] for halo in halos[1:]])
        pad_ref[jnp.where(upper, planes + 1, 0)] = block + lookup(near, jnp.where(upper, high, low))
        upper = even_y if slot == 0 else jnp.logical_not(even_y)
        index = halos[0][2 + slot][1].astype(i32)
        block = combine([halos[0][2 + slot][0]] + [halo[2 + slot][...] for halo in halos[1:]])
        found = jnp.where(
            upper, lookup(near, (index & (B_DEV - 1)) + 3 * S_DEV), lookup(side, index)
        )
        side_ref[jnp.where(upper, 1, 0)] = block + found

    early = tuple(name for name in names if name[0] in "rw")
    for name in early:
        reads[name].wait()
    empty = jnp.zeros((rows, width), f32)

    def residual(plane, before):
        value = held["r"][plane]
        if stage == 1:
            value = value - alphas[0] * held["w0"][plane]
            made["rn"][plane] = value
        if stage == 2:
            image = held["w1"][plane] + betas[1] * held["w0"][plane]
            made["s"][plane] = image
            value = value - alphas[1] * image
            made["rn"][plane] = value
        value = value + cz_ref[plane] * before
        work_ref[plane] = value
        return value * inv_ref[plane]

    lax.fori_loop(0, planes, residual, empty, unroll=4)
    start_all([writes[name] for name in out_names[:-2]])

    def direction(step, after):
        plane = planes - 1 - step
        value = (work_ref[plane] + cz_ref[plane + 1] * after) * inv_ref[plane]
        pad_ref[plane + 1] = value + lookup(near, code_ref[plane].astype(i32))
        return value

    lax.fori_loop(0, planes, direction, empty)
    if not last:
        writes["z"].start()
    for name in names:
        if name not in early and name != "dest":
            reads[name].wait()
    row = iota((rows, width), 0)

    def image_plane(plane, carry):
        sums, before = carry
        here = pad_ref[plane + 1]
        cy, cx = cy_ref[plane], cx_ref[plane]
        north = jnp.where(row == rows - 1, side_ref[1, pl.ds(plane, 1), :], up_rows(here))
        below = south_ref[pl.ds(plane, 1), :] * side_ref[0, pl.ds(plane, 1), :]
        south = jnp.where(row == 0, below, down_rows(cy * here))
        image = held["diag"][plane] * here - (
            cz_ref[plane + 1] * pad_ref[plane + 2]
            + cz_ref[plane] * pad_ref[plane]
            + (cy * north + south)
            + (cx * next_x(here) + prev_x(cx * here))
        )
        w_ref[plane] = image
        new = made["rn"] if stage else held["r"]
        found = [total(new[plane] * here), total(here * image)]
        if stage == 1:
            found.append(total(here * held["w0"][plane] + held["z0"][plane] * image))
        if stage == 2:
            along = held["z1"][plane] + betas[1] * held["z0"][plane]
            made["p"][plane] = along
            made["x"][plane] = alphas[0] * held["z0"][plane] + alphas[1] * along
            found.append(total(here * made["s"][plane] + along * image))
        if not last:
            before = image + cz_ref[plane] * before
            work_ref[plane] = before
            before = before * inv_ref[plane]
        return tuple(old + new for old, new in zip(sums, found)), before

    blank = jnp.zeros((8, LANES), f32)
    dots, _ = lax.fori_loop(
        0, planes, image_plane, ((blank,) * (3 if stage else 2), blank if last else empty), unroll=2
    )
    if not last:
        writes["w"].start()
    row = scalar_row([jnp.sum(value) for value in dots])
    if last:
        send_ref[...] = jnp.broadcast_to(row, send_ref.shape)
    else:

        def backward(step, after):
            plane = planes - 1 - step
            value = (work_ref[plane] + cz_ref[plane + 1] * after) * inv_ref[plane]
            u_ref[plane] = value
            return value

        lax.fori_loop(0, planes, backward, empty, unroll=4)
        write_edges(even_z, even_y, u_ref, edges_z, edges_y)
        reads["dest"].wait()
        parts = coarse_parts(region_row(w_ref, code_ref), held["dest"])
        send_ref[...] = parts + jnp.where(iota(parts.shape, 0) % 2 == 0, row, 0.0)
    wait_all(writes.values())


def final_kernel(
    d0_ref, d1_ref, d2_ref, z_ref, w_ref, r_ref, s_ref, p_ref, part_ref, x_out, r_out, x_new, r_new, sems
):
    sums = [table_rows(d0_ref[...])[0:1], table_rows(d1_ref[...])[0:1], jnp.sum(d2_ref[...], axis=0, keepdims=True)]
    alphas, betas = scalars_of(sums)
    mixed = alphas[2] * betas[2]
    planes = r_ref.shape[0]
    writes = []
    for half in range(2):
        low, high = half * planes // 2, (half + 1) * planes // 2
        x_new[low:high] = part_ref[low:high] + alphas[2] * z_ref[low + 1 : high + 1] + mixed * p_ref[low:high]
        r_new[low:high] = r_ref[low:high] - alphas[2] * w_ref[low:high] - mixed * s_ref[low:high]
        piece = pl.ds(low, high - low)
        pairs = [(x_new.at[piece], x_out.at[piece]), (r_new.at[piece], r_out.at[piece])]
        copies = [pltpu.make_async_copy(a, b, sems.at[2 * half + i]) for i, (a, b) in enumerate(pairs)]
        start_all(copies)
        writes += copies
    wait_all(writes)


def call(kernel, outs, scratch, args):
    spaces = {"smem": pltpu.SMEM, "vmem": pltpu.VMEM, "kept": pltpu.VMEM, "hbm": pltpu.HBM}

    def specs(items):
        return [pl.BlockSpec(memory_space=spaces[space]) for space, _ in items]

    held = sum(4 * math.prod(ref.shape) for ref in scratch)
    places = {"hbm": pltpu.HBM, "kept": pltpu.VMEM}
    made = [places[space](out.shape, out.dtype) if space in places else out for space, out in outs]
    operands = [
        pltpu.with_memory_space_constraint(value, places[space]) if space in places else value for space, value in args
    ]
    return pl.pallas_call(
        kernel,
        out_shape=made,
        in_specs=specs(args),
        out_specs=specs(outs),
        scratch_shapes=scratch,
        compiler_params=pltpu.CompilerParams(vmem_limit_bytes=held + 12 * 1024 * 1024),
    )(*operands)


def swaps(axis, first):
    count = lax.axis_size(axis)
    pairs = []
    for i in range(first, count + first, 2):
        low, high = i % count, (i + 1) % count
        pairs += [(low, high), (high, low)]
    return pairs


def swap(block, axis, first):
    if axis == "gz" and first == 1:
        return lax.ppermute(block, ("gz", "gy"), inner_swaps())
    return lax.ppermute(block, axis, swaps(axis, first))


def inner_swaps():
    slabs, columns = lax.axis_size("gz"), lax.axis_size("gy")
    pairs = []
    for slab in range(slabs):
        for column in range(columns):
            if slab in (0, slabs - 1):
                target = slab * columns + (column ^ 1)
            else:
                target = (slab + 1 if slab % 2 else slab - 1) * columns + column
            pairs.append((slab * columns + column, target))
    return pairs


def solve(fraction, source, bubble_label, subdomain, coarse_inverse):
    planes, rows, width = fraction.shape
    slabs = lax.axis_size("gz")
    columns = lax.axis_size("gy")
    devices = slabs * columns
    slab = lax.axis_index("gz")
    even_z = slab % 2 == 0
    field = jax.ShapeDtypeStruct((planes, rows, width), f32)

    def shape(*dims, dtype=f32):
        return jax.ShapeDtypeStruct(dims, dtype)

    def vmem(*dims, dtype=f32):
        return pltpu.VMEM(dims, dtype)

    def like(items):
        return [vmem(*value.shape, dtype=value.dtype) for value in items]

    def semaphores(count):
        return pltpu.SemaphoreType.DMA((count,))

    def tag(space, items):
        return [(space, item) for item in items]

    top, bottom, *sides, bubbles = call(
        slices_kernel,
        tag("vmem", [shape(DEPTH, rows, width)] * 2 + [shape(planes, DEPTH, width)] * 2 + [shape(B_DEV, devices * SPAN)]),
        [vmem(planes, rows, width), vmem(SPAN, devices * SPAN), semaphores(2)],
        tag("hbm", [fraction, coarse_inverse]),
    )
    coarse_in = [swap(bubbles, "gz", 0), swap(bubbles, "gz", 1)]
    y_in = [swap(sides[0], "gy", 0), swap(sides[1], "gy", 1)]
    z_in = [swap(top, "gz", 0), swap(bottom, "gz", 1)]
    corner = jnp.stack(y_in)
    corner_top = jnp.where(even_z, corner[:, planes - DEPTH :], corner[:, :DEPTH])
    corner_bottom = jnp.where(even_z, corner[:, :DEPTH], corner[:, planes - DEPTH :])
    corner_in = [swap(corner_top, "gz", 0), swap(corner_bottom, "gz", 1)]

    def spread(matrix):
        return matrix.reshape(matrix.shape[0], devices, SPAN)

    dest_shape = shape(REGIONS, 2 * devices, LANES)
    spread_in = [spread(m) for m in [coarse_inverse] + coarse_in]
    (dest,) = call(
        partial(destinations_kernel, columns),
        tag("hbm", [dest_shape]),
        [vmem(REGIONS, devices, LANES)] + like([dest_shape]) + [semaphores(1)],
        tag("vmem", spread_in),
    )
    codes = shape(planes, rows, width, dtype=i8)
    faces = shape(planes + 1, rows, width)
    inputs = [fraction, source, bubble_label, subdomain, dest]
    tall = rows + 8
    wide = shape(2 * devices, LANES)
    first_edges = [shape(2, rows, width)] * 2 + [shape(2, planes, width)] * 2
    later_edges = [shape(rows, width)] * 2 + [shape(planes, width)] * 2
    outs = tag("vmem", first_edges + [wide])
    outs += tag("kept", [codes, faces, field, field, field, shape(planes, width)]) + tag("hbm", [field, field])
    *sent, send, code, cz, cy, cx, inv, south, r0, diag = call(
        setup_kernel,
        outs,
        like(inputs)
        + like([field, field, field])
        + [
            vmem(planes + 2 * DEPTH, tall, width),
            vmem(planes + 4, tall, width),
            vmem(planes + 4, tall, width),
            vmem(planes + 2, tall, width),
            vmem(planes + 1, rows, width),
            vmem(planes, rows, width),
            semaphores(len(inputs)),
            semaphores(2),
        ],
        tag("vmem", z_in + y_in + corner_in) + tag("hbm", inputs),
    )
    matrix = [code, cz, cy, cx, inv, south]

    def exchange(parts):
        blocks = parts.reshape(devices, -1, LANES)
        return lax.all_to_all(blocks, ("gz", "gy"), 0, 0).reshape(parts.shape)

    def share(sent, send):
        edges = [swap(sent[0], "gz", 0), swap(sent[1], "gz", 1)]
        edges += [swap(sent[2], "gy", 0), swap(sent[3], "gy", 1)]
        parts = [exchange(send)]
        return edges, parts

    def step(stage, parts, edges, state):
        last = stage == 2
        operands = state + ([diag] if last else [diag, dest])
        tall_field = shape(planes + 2, rows, width)
        sides = vmem(2, planes, width)
        if last:
            outs = tag("vmem", [shape(devices, LANES)]) + tag("kept", [tall_field] + [field] * 5)
            scratch = like(operands) + [sides] + like([field]) + [semaphores(len(operands))]
            count = 0
        else:
            fields = [field] * (2 + stage)
            outs = tag("vmem", later_edges + [wide]) + tag("hbm", fields)
            scratch = like(operands) + like([tall_field]) + [sides] + like([field] * (len(fields) + 1))
            scratch += [semaphores(len(operands)), semaphores(len(fields))]
            count = len(later_edges)
        results = call(
            partial(step_kernel, stage),
            outs,
            scratch,
            tag("vmem", parts + edges) + tag("kept", matrix) + tag("hbm", operands),
        )
        return results[:count], results[count], results[count + 1 :]

    edges, parts = share(sent, send)
    sent, send, (z0, w0) = step(0, parts, edges, [r0])
    more_edges, more_parts = share(sent, send)
    edges, parts = edges + more_edges, parts + more_parts
    sent, send, (r1, z1, w1) = step(1, parts, edges, [r0, w0, z0])
    more_edges, more_parts = share(sent, send)
    edges, parts = edges + more_edges, parts + more_parts
    _, send, kept = step(2, parts, edges, [r1, w1, w0, z1, z0])
    parts = parts + [exchange(send)]
    return tuple(
        call(
            final_kernel,
            tag("hbm", [field, field]),
            like([field, field]) + [semaphores(4)],
            tag("vmem", parts[1:]) + tag("kept", kept),
        )
    )


def solution(mesh):
    placed = (
        P("gz", "gy", None),
        P("gz", "gy", None),
        P("gz", "gy", None),
        P("gz", "gy", None),
        P(("gz", "gy"), None),
    )
    return jax.shard_map(
        solve,
        mesh=mesh,
        in_specs=placed,
        out_specs=(P("gz", "gy", None), P("gz", "gy", None)),
        check_vma=False,
    )
```

```python
import math
from functools import partial

import jax
import jax.numpy as jnp
from jax import lax
from jax.experimental import pallas as pl
from jax.experimental.pallas import tpu as pltpu
from jax.sharding import PartitionSpec as P


S_DEV = 4
B_DEV = 16
SPAN = S_DEV + B_DEV
LANES = 128
GROUPS = 4
CODES = GROUPS * B_DEV
REGIONS = S_DEV + 3 * B_DEV
SCALARS = 96
DEPTH = 3
PIECE = 16

surface_tension = 0.5
shift_term = 0.05
gas_drop = 0.75
norm_floor = 0.25
highest = lax.Precision.HIGHEST
f32 = jnp.float32
i32 = jnp.int32
i8 = jnp.int8
bf16 = jnp.bfloat16


def iota(shape, dim):
    return lax.broadcasted_iota(i32, shape, dim)


def up_rows(field):
    return pltpu.roll(field, field.shape[0] - 1, 0)


def down_rows(field):
    return pltpu.roll(field, 1, 0)


def next_x(field):
    return pltpu.roll(field, field.shape[1] - 1, 1)


def prev_x(field):
    return pltpu.roll(field, 1, 1)


def total(field):
    rows, width = field.shape
    folded = field[:, :LANES]
    for start in range(LANES, width, LANES):
        folded = folded + field[:, start : start + LANES]
    return jnp.sum(folded.reshape(rows // 8, 8, LANES), axis=0)


def digits(code):
    forms = []
    rest = code.astype(f32).astype(bf16)
    bits = []
    for power in (32, 16, 8, 4, 2, 1):
        bit = rest if power == 1 else jnp.clip(rest - (power - 1), 0, 1)
        bits.append(bit)
        rest = rest - power * bit
    for high, low in zip(bits[::2], bits[1::2]):
        no_high, no_low = 1 - high, 1 - low
        forms.append([no_high * no_low, no_high * low, high * no_low, high * low])
    return forms


def piece_sums(values, code):
    groups, outer, inner = digits(code)
    high = values.astype(bf16)
    low = (values - high.astype(f32)).astype(bf16)
    left = [group * part for part in (high, low) for group in groups]
    right = [first * second for first in outer for second in inner]
    return lax.dot_general(
        jnp.concatenate(left, axis=0),
        jnp.concatenate(right, axis=0),
        (((1,), (1,)), ((), ())),
        preferred_element_type=f32,
    )


def region_row(value_ref, code_ref):
    planes, rows, _ = value_ref.shape

    def step(plane, acc):
        code = code_ref[plane].astype(i32)
        for start in range(0, rows, PIECE):
            acc = acc + piece_sums(value_ref[plane, start : start + PIECE, :], code[start : start + PIECE])
        return acc

    acc = lax.fori_loop(
        0, planes, step, jnp.zeros((2 * GROUPS * PIECE, B_DEV * PIECE), f32), unroll=planes
    )
    shape = acc.shape
    kept = jnp.where(iota(shape, 0) % PIECE == iota(shape, 1) % PIECE, acc, 0.0)
    folded = jnp.sum(kept.reshape(2 * GROUPS, PIECE, shape[1]), axis=1)
    shape = (shape[1], LANES)
    pick = jnp.where(iota(shape, 0) // PIECE == iota(shape, 1) % B_DEV, 1.0, 0.0)
    spread = jnp.dot(folded, pick, precision=highest, preferred_element_type=f32)
    shape = spread.shape
    lane = iota(shape, 1)
    mine = (iota(shape, 0) % GROUPS == lane // B_DEV) & (lane < CODES)
    return jnp.sum(jnp.where(mine, spread, 0.0), axis=0, keepdims=True)


def scalar_row(scalars):
    lane = iota((1, LANES), 1)
    row = jnp.zeros((1, LANES), f32)
    for index, value in enumerate(scalars):
        row = jnp.where(lane == SCALARS + index, value, row)
    return row


def lane_of(row, index):
    return jnp.sum(jnp.where(iota(row.shape, 1) == SCALARS + index, row, 0.0))


def lookup(table, index):
    rows, width = index.shape
    wide = jnp.broadcast_to(table, (rows, LANES))
    return jnp.concatenate(
        [
            jnp.take_along_axis(wide, index[:, start : start + LANES], axis=1)
            for start in range(0, width, LANES)
        ],
        axis=1,
    )


class Place:
    def __init__(self):
        slab, column = lax.axis_index("gz"), lax.axis_index("gy")
        slabs, columns = lax.axis_size("gz"), lax.axis_size("gy")
        here = slab * columns + column
        self.first_z, self.last_z = slab == 0, slab == slabs - 1
        self.first_y, self.last_y = column == 0, column == columns - 1
        self.base, self.stride, self.sub_base = here * B_DEV, columns * B_DEV, here * S_DEV
        self.even_z, self.even_y = slab % 2 == 0, column % 2 == 0


def start_all(copies):
    @pl.when(lax.axis_index("gz") >= 0)
    def _():
        for copy in copies:
            copy.start()


def wait_all(copies):
    for copy in copies:
        copy.wait()


def coarse_parts(row, dest_ref):
    wide = jnp.broadcast_to(row, (8, LANES))

    def step(region, acc):
        lane = jnp.where(region < S_DEV, region, region + B_DEV - S_DEV)
        factor = jnp.take_along_axis(wide, jnp.full((8, LANES), lane, i32), axis=1)[0:1, :]
        return acc + factor * dest_ref[region]

    small = dest_ref.shape[1] <= 64
    return lax.fori_loop(0, REGIONS, step, jnp.zeros(dest_ref.shape[1:], f32), unroll=REGIONS if small else 4)


def destinations_kernel(columns, own_ref, near_ref, far_ref, dest_hbm, wide_ref, dest_ref, sems):
    devices = own_ref.shape[1]
    even_z = Place().even_z
    wide_ref[...] = jnp.zeros(wide_ref.shape, f32)
    low_start = pl.multiple_of(jnp.where(even_z, 2 * B_DEV, 0), B_DEV) + S_DEV
    high_start = pl.multiple_of(jnp.where(even_z, 0, 2 * B_DEV), B_DEV) + S_DEV
    wide_ref[0:S_DEV, :, 0:SPAN] = own_ref[0:S_DEV]
    wide_ref[S_DEV + B_DEV : S_DEV + 2 * B_DEV, :, 0:SPAN] = own_ref[S_DEV:SPAN]
    wide_ref[pl.ds(low_start, B_DEV), :, 0:SPAN] = near_ref[...]
    wide_ref[pl.ds(high_start, B_DEV), :, 0:SPAN] = far_ref[...]
    lane = iota((devices, LANES), 1)

    def place(base, shift, first, count):
        moved = pltpu.roll(base, shift, 1) if shift else base
        return jnp.where((lane >= first) & (lane < first + count), moved, 0.0)

    def from_device(field, step):
        return pltpu.roll(field, (-step) % devices, 0) if step % devices else field

    def one(region, carry):
        base = wide_ref[region]
        bubbles = B_DEV - S_DEV
        table = place(base, 0, 0, S_DEV) + place(base, B_DEV + bubbles, 2 * B_DEV, B_DEV)
        table = table + from_device(
            place(base, S_DEV, S_DEV, S_DEV) + place(base, 2 * B_DEV + bubbles, 3 * B_DEV, B_DEV), columns
        )
        table = table + from_device(
            place(base, 2 * S_DEV, 2 * S_DEV, S_DEV) + place(base, bubbles, B_DEV, B_DEV), -columns
        )
        table = table + from_device(place(base, 3 * S_DEV, 3 * S_DEV, S_DEV), 1)
        table = table + from_device(place(base, 3 * B_DEV + bubbles, 4 * B_DEV, B_DEV), 2 * columns)
        table = table + from_device(place(base, 4 * B_DEV + bubbles, 5 * B_DEV, B_DEV), -2 * columns)
        own_codes = jnp.where((lane < S_DEV) | ((lane >= B_DEV) & (lane < CODES)), table, 0.0)
        dest_ref[region, pl.ds(0, devices, stride=2), :] = table
        dest_ref[region, pl.ds(1, devices, stride=2), :] = from_device(own_codes, -1)
        return carry

    lax.fori_loop(0, REGIONS, one, 0, unroll=4)
    write = pltpu.make_async_copy(dest_ref, dest_hbm, sems.at[0])
    write.start()
    write.wait()


def write_edges(even_z, even_y, value_ref, z_refs, y_refs, convert=lambda value: value):
    planes, rows, _ = value_ref.shape
    z_refs[0][...] = convert(value_ref[jnp.where(even_z, planes - 1, 0)])
    z_refs[1][...] = convert(value_ref[jnp.where(even_z, 0, planes - 1)])
    for plane in range(planes):
        first = convert(value_ref[plane, 0:1, :])
        last = convert(value_ref[plane, rows - 1 : rows, :])
        y_refs[0][plane : plane + 1, :] = jnp.where(even_y, last, first)
        y_refs[1][plane : plane + 1, :] = jnp.where(even_y, first, last)


def slices_kernel(frac_hbm, coarse_hbm, z0_ref, z1_ref, y0_ref, y1_ref, bubble_ref, frac_ref, coarse_ref, sems):
    planes, rows, _ = frac_ref.shape
    copies = [
        pltpu.make_async_copy(frac_hbm, frac_ref, sems.at[0]),
        pltpu.make_async_copy(coarse_hbm, coarse_ref, sems.at[1]),
    ]
    start_all(copies)
    place = Place()
    even_z, even_y = place.even_z, place.even_y
    wait_all(copies)
    bubble_ref[...] = coarse_ref[S_DEV:SPAN, :]
    z0_ref[...] = frac_ref[pl.ds(jnp.where(even_z, planes - DEPTH, 0), DEPTH)]
    z1_ref[...] = frac_ref[pl.ds(jnp.where(even_z, 0, planes - DEPTH), DEPTH)]
    first, last = frac_ref[:, 0:DEPTH, :], frac_ref[:, rows - DEPTH : rows, :]
    y0_ref[...] = jnp.where(even_y, last, first)
    y1_ref[...] = jnp.where(even_y, first, last)


def setup_kernel(
    z0_in, z1_in, y0_in, y1_in, k0_in, k1_in, frac_hbm, source_hbm, label_hbm, sub_hbm, dest_hbm,
    ez0_ref, ez1_ref, ey0_ref, ey1_ref, send_ref,
    code_ref, cz_ref, cy_ref, cx_ref, inv_ref, south_ref, r_hbm, diag_hbm,
    frac_ref, source_ref, label_ref, sub_ref, dest_ref, r_ref, diag_ref, b_ref,
    deep_ref, nz_ref, flat_ref, kap_ref, fz_ref, work_ref, in_sems, out_sems,
):
    planes, rows, width = frac_ref.shape
    tall = rows + 8
    place = Place()
    first_z, last_z, first_y, last_y = place.first_z, place.last_z, place.first_y, place.last_y
    base, stride, sub_base = place.base, place.stride, place.sub_base
    even_z, even_y = place.even_z, place.even_y
    pairs = [(frac_hbm, frac_ref), (label_hbm, label_ref), (sub_hbm, sub_ref), (source_hbm, source_ref), (dest_hbm, dest_ref)]
    reads = [pltpu.make_async_copy(a, b, in_sems.at[i]) for i, (a, b) in enumerate(pairs)]
    start_all(reads)
    row = iota((tall, width), 0)
    lane = iota((tall, width), 1)
    inside_y = ((row < rows) | ((row < rows + 4) & jnp.logical_not(last_y))) | (
        (row >= rows + 4) & jnp.logical_not(first_y)
    )
    first_plane = jnp.where(first_z, 0, -planes)
    last_plane = jnp.where(last_z, planes, 2 * planes)

    def right_of(field):
        moved = next_x(field)
        tile = lane[: field.shape[0], :LANES]
        ended = jnp.where(tile == LANES - 1, 0.0, moved[:, width - LANES :])
        return jnp.concatenate([moved[:, : width - LANES], ended], axis=1)

    def left_of(field):
        moved = prev_x(field)
        tile = lane[: field.shape[0], :LANES]
        return jnp.concatenate([jnp.where(tile == 0, 0.0, moved[:, :LANES]), moved[:, LANES:]], axis=1)

    deep_ref[:, rows:tall, :] = jnp.zeros((planes + 2 * DEPTH, 8, width), f32)
    near_z = jnp.where(even_z, planes + DEPTH, 0)
    far_z = jnp.where(even_z, 0, planes + DEPTH)
    out_near, out_far = jnp.where(even_z, last_z, first_z), jnp.where(even_z, first_z, last_z)
    deep_ref[pl.ds(near_z, DEPTH), 0:rows, :] = jnp.where(out_near, 0.0, z0_in[...])
    deep_ref[pl.ds(far_z, DEPTH), 0:rows, :] = jnp.where(out_far, 0.0, z1_in[...])
    high, low = slice(rows, rows + DEPTH), slice(tall - DEPTH, tall)

    def fill_rows(first, second, out_first, out_second):
        deep_ref[DEPTH : planes + DEPTH, first, :] = jnp.where(out_first, 0.0, y0_in[...])
        deep_ref[DEPTH : planes + DEPTH, second, :] = jnp.where(out_second, 0.0, y1_in[...])
        for start, corner, out in ((near_z, k0_in, out_near), (far_z, k1_in, out_far)):
            deep_ref[pl.ds(start, DEPTH), first, :] = jnp.where(out | out_first, 0.0, corner[0])
            deep_ref[pl.ds(start, DEPTH), second, :] = jnp.where(out | out_second, 0.0, corner[1])

    @pl.when(even_y)
    def _():
        fill_rows(high, low, last_y, first_y)

    @pl.when(jnp.logical_not(even_y))
    def _():
        fill_rows(low, high, first_y, last_y)

    reads[0].wait()
    deep_ref[DEPTH : planes + DEPTH, 0:rows, :] = frac_ref[...]

    def normal_plane(index, carry):
        keep = (index - 2 >= first_plane) & (index - 2 < last_plane)
        here = deep_ref[index + 1]
        gz = deep_ref[index + 2] - deep_ref[index]
        gy = up_rows(here) - down_rows(here)
        gx = right_of(here) - left_of(here)
        scale = jnp.minimum(lax.rsqrt(gz * gz + gy * gy + gx * gx), 0.5 / norm_floor)
        scale = jnp.where(inside_y & keep, scale, 0.0)
        ny = gy * scale
        nx = gx * scale
        nz_ref[index] = gz * scale
        flat_ref[index] = (up_rows(ny) - down_rows(ny)) + (right_of(nx) - left_of(nx))
        return carry

    lax.fori_loop(0, planes + 4, normal_plane, 0, unroll=2)

    def kappa_plane(index, carry):
        keep = (index - 1 >= first_plane) & (index - 1 < last_plane)
        value = -0.5 * ((nz_ref[index + 2] - nz_ref[index]) + flat_ref[index + 1])
        kap_ref[index] = jnp.where(inside_y & keep, value, 0.0)
        return carry

    lax.fori_loop(0, planes + 2, kappa_plane, 0, unroll=2)
    mid = pl.ds(0, rows)

    def z_face(index, carry):
        f_low = deep_ref[index + 2, mid, :]
        f_high = deep_ref[index + 3, mid, :]
        coef = 2.0 * pl.reciprocal((1.0 - gas_drop * f_low) + (1.0 - gas_drop * f_high))
        cz_ref[index] = coef
        mean = 0.5 * (kap_ref[index, mid, :] + kap_ref[index + 1, mid, :])
        fz_ref[index] = coef * mean * (f_high - f_low)
        return carry

    lax.fori_loop(0, planes + 1, z_face, 0, unroll=3)
    row_mid = row[:rows]
    lane_mid = lane[:rows]
    wait_all(reads[1:])

    def assemble_plane(plane, carry):
        inv_before, g_before = carry
        f = deep_ref[plane + 3]
        k = kap_ref[plane + 1]
        d = 1.0 - gas_drop * f
        f_up = up_rows(f)
        cy = 2.0 * pl.reciprocal(d + (1.0 - gas_drop * f_up))
        fy = cy * (0.5 * (k + up_rows(k))) * (f_up - f)
        cyp, cym = cy[:rows], down_rows(cy)[:rows]
        sum_y = fy[:rows] - down_rows(fy)[:rows]
        f, k, d = f[:rows], k[:rows], d[:rows]
        f_right = right_of(f)
        cxp = 2.0 * pl.reciprocal(d + (1.0 - gas_drop * f_right))
        fx = cxp * (0.5 * (k + right_of(k))) * (f_right - f)
        outer = jnp.concatenate([2.0 / (d[:, :LANES] + 1.0), jnp.zeros((rows, width - LANES), f32)], axis=1)
        cxm = jnp.where(lane_mid == 0, outer, prev_x(cxp))
        fx_before = jnp.where(lane_mid == 0, outer * (0.5 * k) * f, prev_x(fx))
        terms = fz_ref[plane + 1] - fz_ref[plane] + sum_y + (fx - fx_before)
        rhs = source_ref[plane] - surface_tension * terms
        down = cz_ref[plane]
        diagonal = shift_term + (cz_ref[plane + 1] + down + cyp + cym + cxp + cxm)
        mult = down * inv_before
        inv = pl.reciprocal(diagonal - mult * down)
        g = rhs + mult * g_before
        r_ref[plane] = rhs
        diag_ref[plane] = diagonal
        inv_ref[plane] = inv
        work_ref[plane] = g
        cy_ref[plane] = jnp.where((row_mid == rows - 1) & last_y, 0.0, cyp)
        south_ref[pl.ds(plane, 1), :] = jnp.where(first_y, 0.0, cym[0:1, :])
        cx_ref[plane] = jnp.where(lane_mid == width - 1, 0.0, cxp)
        label = label_ref[plane]
        offset = label - base
        below = offset < 0
        above = offset >= stride
        group = jnp.where(below, 1, jnp.where(above, 3, 2))
        inner = jnp.where(below, offset + stride, jnp.where(above, offset - stride, offset))
        code = jnp.where(label >= 0, group * B_DEV + inner, sub_ref[plane] - sub_base)
        code_ref[plane] = (code & (CODES - 1)).astype(i8)
        return (inv, g)

    blank = jnp.zeros((rows, width), f32)
    lax.fori_loop(0, planes, assemble_plane, (blank, blank), unroll=2)

    def backward(step, after):
        plane = planes - 1 - step
        value = (work_ref[plane] + cz_ref[plane + 1] * after) * inv_ref[plane]
        b_ref[plane] = value
        return value

    lax.fori_loop(0, planes, backward, blank, unroll=4)
    cz_ref[0] = jnp.where(first_z, 0.0, cz_ref[0])
    cz_ref[planes] = jnp.where(last_z, 0.0, cz_ref[planes])
    writes = [
        pltpu.make_async_copy(r_ref, r_hbm, out_sems.at[0]), pltpu.make_async_copy(diag_ref, diag_hbm, out_sems.at[1])
    ]
    start_all(writes)
    write_edges(even_z, even_y, b_ref, [ez0_ref.at[0], ez1_ref.at[0]], [ey0_ref.at[0], ey1_ref.at[0]])
    for plane in range(planes):
        label_ref[plane] = code_ref[plane].astype(i32)
    write_edges(
        even_z, even_y, label_ref, [ez0_ref.at[1], ez1_ref.at[1]], [ey0_ref.at[1], ey1_ref.at[1]],
        convert=lambda value: value.astype(f32),
    )
    send_ref[...] = coarse_parts(region_row(r_ref, code_ref), dest_ref)
    wait_all(writes)


def table_rows(parts):
    folded = jnp.sum(parts.reshape(parts.shape[0] // 8, 8, LANES), axis=0)
    even = iota(folded.shape, 0) % 2 == 0
    return jnp.concatenate(
        [
            jnp.sum(jnp.where(even, folded, 0.0), axis=0, keepdims=True),
            jnp.sum(jnp.where(even, 0.0, folded), axis=0, keepdims=True),
        ],
        axis=0,
    )


def scalars_of(sums):
    alphas, betas, curves = [], [None], []
    for step, row in enumerate(sums):
        gamma = lane_of(row, 0)
        if step == 0:
            curve = lane_of(row, 1)
        else:
            beta = gamma / lane_of(sums[step - 1], 0)
            betas.append(beta)
            curve = lane_of(row, 1) + beta * (lane_of(row, 2) + beta * curves[-1])
        curves.append(curve)
        alphas.append(gamma / curve)
    return alphas, betas


def step_kernel(stage, *refs):
    refs = list(refs)

    def take(count):
        out = refs[:count]
        del refs[:count]
        return out

    parts = take(stage + 1)
    halos = [take(4) for _ in range(stage + 1)]
    code_ref, cz_ref, cy_ref, cx_ref, inv_ref, south_ref = take(6)
    last = stage == 2
    names = (("r",), ("r", "w0", "z0"), ("r", "w1", "w0", "z1", "z0"))[stage] + (("diag",) if last else ("diag", "dest"))
    sources = dict(zip(names, take(len(names))))
    out_names = (("z", "w"), ("rn", "z", "w"), ("rn", "s", "p", "z", "w"))[stage]
    if not last:
        edges_z, edges_y = take(2), take(2)
    (send_ref,) = take(1)
    if last:
        pad_ref, w_ref, *others = take(6)
        made = dict(zip(("rn", "s", "p", "x"), others))
        out_names = ()
        held = dict(zip(names, take(len(names))))
        side_ref, work_ref, in_sems = take(3)
        out_sems = None
    else:
        sinks = dict(zip(out_names, take(len(out_names))))
        held = dict(zip(names, take(len(names))))
        pad_ref, side_ref, work_ref, w_ref = take(4)
        made = {"z": pad_ref.at[pl.ds(1, pad_ref.shape[0] - 2)], "w": w_ref}
        for name in out_names[:-2]:
            (made[name],) = take(1)
        u_ref, in_sems, out_sems = take(3)

    reads = {name: pltpu.make_async_copy(sources[name], held[name], in_sems.at[i]) for i, name in enumerate(names)}
    start_all(reads.values())
    writes = {name: pltpu.make_async_copy(made[name], sinks[name], out_sems.at[i]) for i, name in enumerate(out_names)}
    planes, rows, width = code_ref.shape
    place = Place()
    even_z, even_y = place.even_z, place.even_y

    sums = [table_rows(part[...]) for part in parts]
    alphas, betas = scalars_of([row[0:1] for row in sums[1:]])
    table = sums[0]
    if stage >= 1:
        table = table - alphas[0] * sums[1]
    if stage == 2:
        table = table - alphas[1] * (sums[2] + betas[1] * sums[1])
    near, side = table[0:1], table[1:2]

    def combine(values):
        out = values[0]
        if stage >= 1:
            out = out - alphas[0] * values[1]
        if stage == 2:
            out = out - alphas[1] * (values[2] + betas[1] * values[1])
        return out

    for slot in range(2):
        upper = even_z if slot == 0 else jnp.logical_not(even_z)
        index = halos[0][slot][1].astype(i32)
        high = jnp.where(index < B_DEV, index + S_DEV, index + B_DEV)
        low = jnp.where(
            index < B_DEV, index + 2 * S_DEV, jnp.where(index < 2 * B_DEV, index + 4 * B_DEV, index - B_DEV)
        )
        block = combine([halos[0][slot][0]] + [halo[slot][...] for halo in halos[1:]])
        pad_ref[jnp.where(upper, planes + 1, 0)] = block + lookup(near, jnp.where(upper, high, low))
        upper = even_y if slot == 0 else jnp.logical_not(even_y)
        index = halos[0][2 + slot][1].astype(i32)
        block = combine([halos[0][2 + slot][0]] + [halo[2 + slot][...] for halo in halos[1:]])
        found = jnp.where(
            upper, lookup(near, (index & (B_DEV - 1)) + 3 * S_DEV), lookup(side, index)
        )
        side_ref[jnp.where(upper, 1, 0)] = block + found

    early = tuple(name for name in names if name[0] in "rw")
    for name in early:
        reads[name].wait()
    empty = jnp.zeros((rows, width), f32)

    def residual(plane, before):
        value = held["r"][plane]
        if stage == 1:
            value = value - alphas[0] * held["w0"][plane]
            made["rn"][plane] = value
        if stage == 2:
            image = held["w1"][plane] + betas[1] * held["w0"][plane]
            made["s"][plane] = image
            value = value - alphas[1] * image
            made["rn"][plane] = value
        value = value + cz_ref[plane] * before
        work_ref[plane] = value
        return value * inv_ref[plane]

    lax.fori_loop(0, planes, residual, empty, unroll=4)
    start_all([writes[name] for name in out_names[:-2]])

    def direction(step, after):
        plane = planes - 1 - step
        value = (work_ref[plane] + cz_ref[plane + 1] * after) * inv_ref[plane]
        pad_ref[plane + 1] = value + lookup(near, code_ref[plane].astype(i32))
        return value

    lax.fori_loop(0, planes, direction, empty)
    if not last:
        writes["z"].start()
    for name in names:
        if name not in early and name != "dest":
            reads[name].wait()
    row = iota((rows, width), 0)

    def image_plane(plane, carry):
        sums, before = carry
        here = pad_ref[plane + 1]
        cy, cx = cy_ref[plane], cx_ref[plane]
        north = jnp.where(row == rows - 1, side_ref[1, pl.ds(plane, 1), :], up_rows(here))
        below = south_ref[pl.ds(plane, 1), :] * side_ref[0, pl.ds(plane, 1), :]
        south = jnp.where(row == 0, below, down_rows(cy * here))
        image = held["diag"][plane] * here - (
            cz_ref[plane + 1] * pad_ref[plane + 2]
            + cz_ref[plane] * pad_ref[plane]
            + (cy * north + south)
            + (cx * next_x(here) + prev_x(cx * here))
        )
        w_ref[plane] = image
        new = made["rn"] if stage else held["r"]
        found = [total(new[plane] * here), total(here * image)]
        if stage == 1:
            found.append(total(here * held["w0"][plane] + held["z0"][plane] * image))
        if stage == 2:
            along = held["z1"][plane] + betas[1] * held["z0"][plane]
            made["p"][plane] = along
            made["x"][plane] = alphas[0] * held["z0"][plane] + alphas[1] * along
            found.append(total(here * made["s"][plane] + along * image))
        if not last:
            before = image + cz_ref[plane] * before
            work_ref[plane] = before
            before = before * inv_ref[plane]
        return tuple(old + new for old, new in zip(sums, found)), before

    blank = jnp.zeros((8, LANES), f32)
    dots, _ = lax.fori_loop(
        0, planes, image_plane, ((blank,) * (3 if stage else 2), blank if last else empty), unroll=4
    )
    if not last:
        writes["w"].start()
    row = scalar_row([jnp.sum(value) for value in dots])
    if last:
        send_ref[...] = jnp.broadcast_to(row, send_ref.shape)
    else:

        def backward(step, after):
            plane = planes - 1 - step
            value = (work_ref[plane] + cz_ref[plane + 1] * after) * inv_ref[plane]
            u_ref[plane] = value
            return value

        lax.fori_loop(0, planes, backward, empty, unroll=4)
        write_edges(even_z, even_y, u_ref, edges_z, edges_y)
        reads["dest"].wait()
        parts = coarse_parts(region_row(w_ref, code_ref), held["dest"])
        send_ref[...] = parts + jnp.where(iota(parts.shape, 0) % 2 == 0, row, 0.0)
    wait_all(writes.values())


def final_kernel(
    d0_ref, d1_ref, d2_ref, z_ref, w_ref, r_ref, s_ref, p_ref, part_ref, x_out, r_out, x_new, r_new, sems
):
    sums = [table_rows(d0_ref[...])[0:1], table_rows(d1_ref[...])[0:1], jnp.sum(d2_ref[...], axis=0, keepdims=True)]
    alphas, betas = scalars_of(sums)
    mixed = alphas[2] * betas[2]
    planes = r_ref.shape[0]
    writes = []
    for half in range(4):
        low, high = half * planes // 4, (half + 1) * planes // 4
        x_new[low:high] = part_ref[low:high] + alphas[2] * z_ref[low + 1 : high + 1] + mixed * p_ref[low:high]
        r_new[low:high] = r_ref[low:high] - alphas[2] * w_ref[low:high] - mixed * s_ref[low:high]
        piece = pl.ds(low, high - low)
        pairs = [(x_new.at[piece], x_out.at[piece]), (r_new.at[piece], r_out.at[piece])]
        copies = [pltpu.make_async_copy(a, b, sems.at[2 * half + i]) for i, (a, b) in enumerate(pairs)]
        start_all(copies)
        writes += copies
    wait_all(writes)


def call(kernel, outs, scratch, args):
    spaces = {"smem": pltpu.SMEM, "vmem": pltpu.VMEM, "kept": pltpu.VMEM, "hbm": pltpu.HBM}

    def specs(items):
        return [pl.BlockSpec(memory_space=spaces[space]) for space, _ in items]

    held = sum(4 * math.prod(ref.shape) for ref in scratch)
    places = {"hbm": pltpu.HBM, "kept": pltpu.VMEM}
    made = [places[space](out.shape, out.dtype) if space in places else out for space, out in outs]
    operands = [
        pltpu.with_memory_space_constraint(value, places[space]) if space in places else value for space, value in args
    ]
    return pl.pallas_call(
        kernel,
        out_shape=made,
        in_specs=specs(args),
        out_specs=specs(outs),
        scratch_shapes=scratch,
        compiler_params=pltpu.CompilerParams(vmem_limit_bytes=held + 12 * 1024 * 1024),
    )(*operands)


def swaps(axis, first):
    count = lax.axis_size(axis)
    pairs = []
    for i in range(first, count + first, 2):
        low, high = i % count, (i + 1) % count
        pairs += [(low, high), (high, low)]
    return pairs


def swap(block, axis, first):
    if axis == "gz" and first == 1:
        return lax.ppermute(block, ("gz", "gy"), inner_swaps())
    return lax.ppermute(block, axis, swaps(axis, first))


def inner_swaps():
    slabs, columns = lax.axis_size("gz"), lax.axis_size("gy")
    pairs = []
    for slab in range(slabs):
        for column in range(columns):
            if slab in (0, slabs - 1):
                target = slab * columns + (column ^ 1)
            else:
                target = (slab + 1 if slab % 2 else slab - 1) * columns + column
            pairs.append((slab * columns + column, target))
    return pairs


def solve(fraction, source, bubble_label, subdomain, coarse_inverse):
    planes, rows, width = fraction.shape
    slabs = lax.axis_size("gz")
    columns = lax.axis_size("gy")
    devices = slabs * columns
    slab = lax.axis_index("gz")
    even_z = slab % 2 == 0
    field = jax.ShapeDtypeStruct((planes, rows, width), f32)

    def shape(*dims, dtype=f32):
        return jax.ShapeDtypeStruct(dims, dtype)

    def vmem(*dims, dtype=f32):
        return pltpu.VMEM(dims, dtype)

    def like(items):
        return [vmem(*value.shape, dtype=value.dtype) for value in items]

    def semaphores(count):
        return pltpu.SemaphoreType.DMA((count,))

    def tag(space, items):
        return [(space, item) for item in items]

    top, bottom, *sides, bubbles = call(
        slices_kernel,
        tag("vmem", [shape(DEPTH, rows, width)] * 2 + [shape(planes, DEPTH, width)] * 2 + [shape(B_DEV, devices * SPAN)]),
        [vmem(planes, rows, width), vmem(SPAN, devices * SPAN), semaphores(2)],
        tag("hbm", [fraction, coarse_inverse]),
    )
    coarse_in = [swap(bubbles, "gz", 0), swap(bubbles, "gz", 1)]
    y_in = [swap(sides[0], "gy", 0), swap(sides[1], "gy", 1)]
    z_in = [swap(top, "gz", 0), swap(bottom, "gz", 1)]
    corner = jnp.stack(y_in)
    corner_top = jnp.where(even_z, corner[:, planes - DEPTH :], corner[:, :DEPTH])
    corner_bottom = jnp.where(even_z, corner[:, :DEPTH], corner[:, planes - DEPTH :])
    corner_in = [swap(corner_top, "gz", 0), swap(corner_bottom, "gz", 1)]

    def spread(matrix):
        return matrix.reshape(matrix.shape[0], devices, SPAN)

    dest_shape = shape(REGIONS, 2 * devices, LANES)
    spread_in = [spread(m) for m in [coarse_inverse] + coarse_in]
    (dest,) = call(
        partial(destinations_kernel, columns),
        tag("hbm", [dest_shape]),
        [vmem(REGIONS, devices, LANES)] + like([dest_shape]) + [semaphores(1)],
        tag("vmem", spread_in),
    )
    codes = shape(planes, rows, width, dtype=i8)
    faces = shape(planes + 1, rows, width)
    inputs = [fraction, source, bubble_label, subdomain, dest]
    tall = rows + 8
    wide = shape(2 * devices, LANES)
    first_edges = [shape(2, rows, width)] * 2 + [shape(2, planes, width)] * 2
    later_edges = [shape(rows, width)] * 2 + [shape(planes, width)] * 2
    outs = tag("vmem", first_edges + [wide])
    outs += tag("kept", [codes, faces, field, field, field, shape(planes, width)]) + tag("hbm", [field, field])
    *sent, send, code, cz, cy, cx, inv, south, r0, diag = call(
        setup_kernel,
        outs,
        like(inputs)
        + like([field, field, field])
        + [
            vmem(planes + 2 * DEPTH, tall, width),
            vmem(planes + 4, tall, width),
            vmem(planes + 4, tall, width),
            vmem(planes + 2, tall, width),
            vmem(planes + 1, rows, width),
            vmem(planes, rows, width),
            semaphores(len(inputs)),
            semaphores(2),
        ],
        tag("vmem", z_in + y_in + corner_in) + tag("hbm", inputs),
    )
    matrix = [code, cz, cy, cx, inv, south]

    def exchange(parts):
        blocks = parts.reshape(devices, -1, LANES)
        return lax.all_to_all(blocks, ("gz", "gy"), 0, 0).reshape(parts.shape)

    def share(sent, send):
        edges = [swap(sent[0], "gz", 0), swap(sent[1], "gz", 1)]
        edges += [swap(sent[2], "gy", 0), swap(sent[3], "gy", 1)]
        parts = [exchange(send)]
        return edges, parts

    def step(stage, parts, edges, state):
        last = stage == 2
        operands = state + ([diag] if last else [diag, dest])
        tall_field = shape(planes + 2, rows, width)
        sides = vmem(2, planes, width)
        if last:
            outs = tag("vmem", [shape(devices, LANES)]) + tag("kept", [tall_field] + [field] * 5)
            scratch = like(operands) + [sides] + like([field]) + [semaphores(len(operands))]
            count = 0
        else:
            fields = [field] * (2 + stage)
            outs = tag("vmem", later_edges + [wide]) + tag("hbm", fields)
            scratch = like(operands) + like([tall_field]) + [sides] + like([field] * (len(fields) + 1))
            scratch += [semaphores(len(operands)), semaphores(len(fields))]
            count = len(later_edges)
        results = call(
            partial(step_kernel, stage),
            outs,
            scratch,
            tag("vmem", parts + edges) + tag("kept", matrix) + tag("hbm", operands),
        )
        return results[:count], results[count], results[count + 1 :]

    edges, parts = share(sent, send)
    sent, send, (z0, w0) = step(0, parts, edges, [r0])
    more_edges, more_parts = share(sent, send)
    edges, parts = edges + more_edges, parts + more_parts
    sent, send, (r1, z1, w1) = step(1, parts, edges, [r0, w0, z0])
    more_edges, more_parts = share(sent, send)
    edges, parts = edges + more_edges, parts + more_parts
    _, send, kept = step(2, parts, edges, [r1, w1, w0, z1, z0])
    parts = parts + [exchange(send)]
    return tuple(
        call(
            final_kernel,
            tag("hbm", [field, field]),
            like([field, field]) + [semaphores(8)],
            tag("vmem", parts[1:]) + tag("kept", kept),
        )
    )


def solution(mesh):
    placed = (
        P("gz", "gy", None),
        P("gz", "gy", None),
        P("gz", "gy", None),
        P("gz", "gy", None),
        P(("gz", "gy"), None),
    )
    return jax.shard_map(
        solve,
        mesh=mesh,
        in_specs=placed,
        out_specs=(P("gz", "gy", None), P("gz", "gy", None)),
        check_vma=False,
    )
```
